128 devices in a mesh: row: 8 (over y, core), col: 16 (over x, z).
Axes of the slice: x: 4, y: 4, z: 4, core: 2. Of those that a mesh axis runs over, the one named last changes fastest.
Arguments:
- descriptors: bfloat16 [16384, 1024], P(('row', 'col'))
- gradients: bfloat16 [3, 4, 16384, 1024], P(None, None, ('row', 'col'))
- sparse_panel: bfloat16 [512, 1024], P('col')
- sparse_trail: bfloat16 [2048, 1024], P('col')
- atom_counts: int32 [128, 8], P(('row', 'col')), may hold values from 1 to 16, 64 in all within a row
- owner_rows: int32 [128, 8], P(('row', 'col')), may hold values from 0 to 7, each once within a row
- neighbor_ids: int32 [1024, 16, 4], P(('row', 'col')), may hold values from 0 to 65519
Outputs:
- panel_factor: float32 [512, 512], replicated
- cross_factor: float32 [2048, 512], P('col')
- trail_residual: float32 [2048, 65536], P('col', 'row')
The draws below stay inside these ranges and needn't reach their ends.
Inputs may be any that keep to these rules, and one draw needn't show every extreme that they name: `atom_counts`: the structures of one device's line hold 64 atoms together, and every line has a structure of 16 atoms. `owner_rows`: every device gives exactly one structure to each row group.
All inputs are finite; a program needn't handle non-finite values.
Results may differ from the reference program's by a relative error of at most 0.0043.
Values may be sent and summed in bfloat16 or wider, within the bound.
No kernel may reach another device: no remote copies, remote signals or barrier semaphores. Data moves between devices by JAX's collectives and lax.ppermute only.
A program may use at most 128 MiB of HBM per device.

```python
import math
import jax
import jax.numpy as jnp
import numpy as np
from jax import lax

DESC = 1024
PANEL = 512
AMAX = 16
NEIGH = 4
STRUCT_DEV = 8
STRUCTS = 1024
ATOM_DEV = 64
ATOMS = 16384
ROWS = 65536
TRAIL = 2048
N_ROW = 8
N_COL = 16
DEVICES = 128


def shared_center(key):
    center = jax.random.truncated_normal(jax.random.fold_in(key, 11), -4.0, 4.0, (DESC,), jnp.float32)
    return center * DESC ** (-0.25)


def rough_noise(key, array_shape):
    return jax.random.truncated_normal(key, -4.0, 4.0, array_shape, jnp.float32)


def draw_descriptors(key, part):
    center = shared_center(key)
    return (0.85 * center[None, :] + rough_noise(jax.random.fold_in(key, 21), (ATOMS, DESC))).astype(jnp.bfloat16)


def draw_gradients(key, part):
    center = shared_center(key)
    amplitude = jax.random.truncated_normal(jax.random.fold_in(key, 31), -3.0, 3.0, (3, NEIGH, ATOMS, 1), jnp.float32)
    return (0.35 * amplitude * center + 0.2 * rough_noise(jax.random.fold_in(key, 32), (3, NEIGH, ATOMS, DESC))).astype(jnp.bfloat16)


def draw_sparse_panel(key, part):
    center = shared_center(key)
    return ((0.85 * center[None, :] + rough_noise(jax.random.fold_in(key, 41), (PANEL, DESC))) * DESC ** (-0.5)).astype(jnp.bfloat16)


def draw_sparse_trail(key, part):
    center = shared_center(key)
    return ((0.85 * center[None, :] + rough_noise(jax.random.fold_in(key, 51), (TRAIL, DESC))) * DESC ** (-0.5)).astype(jnp.bfloat16)


def place_ends(drawn, key, least, largest):
    dims = drawn.shape
    place = [jax.random.randint(jax.random.fold_in(key, axis), (), 0, dims[axis]) for axis in range(len(dims))]
    drawn = drawn.at[tuple(place)].set(least)
    longest = dims.index(max(dims))
    place[longest] = (place[longest] + 1) % dims[longest]
    return drawn.at[tuple(place)].set(largest)


def split_up(number_of, total, reach, slope):
    loads = [(1 << 20) // math.isqrt(rank ** slope) + 1 for rank in range(2, number_of + 1)]
    rest, counts = total - reach - (number_of - 1), [1] * (number_of - 1)
    while rest > 0:
        free = [i for i in range(number_of - 1) if counts[i] < reach]
        whole, remaining = sum([loads[i] for i in free]), rest
        for i in free:
            extra = min(reach - counts[i], max(1, remaining * loads[i] // whole), rest)
            counts[i] = counts[i] + extra
            rest = rest - extra
    return np.array([reach] + counts)


def ragged_sizes(rng, count, total, reach, slope):
    if count == 2:
        one = jax.random.randint(rng, (), max(1, total - reach), min(reach, total - 1) + 1)
        return jnp.stack([one, total - one])
    lengths = jnp.asarray(split_up(count, total, reach, slope), jnp.int32)
    couples = (count - 1) // 2
    giver, taker = lengths[1:1 + 2 * couples:2], lengths[2:2 + 2 * couples:2]
    slack = jnp.minimum(giver - 1, reach - taker)
    passed = jax.random.randint(jax.random.fold_in(rng, 1), (couples,), 0, 1 << 20) % (slack + 1)
    lengths = lengths.at[1:1 + 2 * couples:2].set(giver - passed).at[2:2 + 2 * couples:2].set(taker + passed)
    return lengths[jax.random.permutation(jax.random.fold_in(rng, 2), count)]


def setup_inputs(seed: int = 0) -> dict:
    keys = jax.random.split(jax.random.key(seed), 8)
    descriptors = draw_descriptors(jax.random.fold_in(keys[7], 71), 0)
    gradients = draw_gradients(jax.random.fold_in(keys[7], 71), 0)
    sparse_panel = draw_sparse_panel(jax.random.fold_in(keys[7], 71), 0)
    sparse_trail = draw_sparse_trail(jax.random.fold_in(keys[7], 71), 0)
    atom_counts = jax.vmap(lambda own: ragged_sizes(own, STRUCT_DEV, ATOM_DEV, AMAX, 1))(jax.random.split(keys[4], DEVICES)).reshape((DEVICES, STRUCT_DEV)).astype(jnp.int32)
    owner_rows = jax.vmap(lambda own: jax.random.permutation(own, N_ROW))(jax.random.split(keys[5], DEVICES)).reshape((DEVICES, STRUCT_DEV)).astype(jnp.int32)
    neighbor_ids = place_ends(jax.random.randint(keys[6], (STRUCTS, AMAX, NEIGH), 0, 65520), jax.random.fold_in(keys[6], 1), 0, 65519).astype(jnp.int32)
    return dict(descriptors=descriptors, gradients=gradients, sparse_panel=sparse_panel, sparse_trail=sparse_trail, atom_counts=atom_counts, owner_rows=owner_rows, neighbor_ids=neighbor_ids)


ridge_value = 0.1

def slot_rows(environments, desc_here, slope_here, count_here, neighbor_here, owner_here):
    struct_count = count_here.shape[0]
    atom_slots = neighbor_here.shape[1]
    neighbor_count = neighbor_here.shape[2]
    env_count = environments.shape[0]
    correlation = lax.dot_general(environments.astype(jnp.float32), desc_here.astype(jnp.float32), (((1,), (1,)), ((), ())), preferred_element_type=jnp.float32)
    slope_dots = lax.dot_general(environments.astype(jnp.float32), slope_here.astype(jnp.float32), (((1,), (1,)), ((), ())), preferred_element_type=jnp.float32)
    slope_dots = slope_dots.reshape(env_count, 3, neighbor_count, struct_count, atom_slots)
    slot_index = jnp.arange(atom_slots, dtype=jnp.int32)
    live_mask = (slot_index[None, :] < count_here[:, None]).astype(jnp.float32)
    squares = (correlation * correlation).reshape(env_count, struct_count, atom_slots)
    energy = jnp.sum(squares * live_mask[None], axis=2) / count_here.astype(jnp.float32)[None, :]
    partner = neighbor_here % count_here[:, None, None]
    struct_index = jnp.arange(struct_count, dtype=jnp.int32)
    flat_index = (struct_index[:, None, None] * atom_slots + partner).reshape(-1).astype(jnp.int32)
    picked = jnp.take(correlation, flat_index, axis=1).reshape(env_count, struct_count, atom_slots, neighbor_count)
    picked = jnp.transpose(picked, (0, 3, 1, 2))
    forces = -2.0 * jnp.sum(picked[:, None] * slope_dots, axis=2) * live_mask[None, None]
    forces = jnp.transpose(forces, (0, 2, 3, 1)).reshape(env_count, struct_count, 3 * atom_slots)
    padding = jnp.zeros((env_count, struct_count, atom_slots - 1), jnp.float32)
    slot_values = jnp.concatenate([energy[:, :, None], forces, padding], axis=2).astype(jnp.bfloat16)
    chosen = (owner_here[None, :] == struct_index[:, None]).astype(jnp.int32)
    owner_order = jnp.sum(struct_index[None, :] * chosen, axis=1).astype(jnp.int32)
    return jnp.take(slot_values, owner_order, axis=1)

def factor_panel(gram_sum, cross_sum, total_rows):
    gram_matrix = gram_sum / total_rows + ridge_value * jnp.eye(gram_sum.shape[0], dtype=jnp.float32)
    lower_factor = jnp.linalg.cholesky(gram_matrix)
    coupling = lax.linalg.triangular_solve(lower_factor, cross_sum / total_rows, left_side=True, lower=True)
    weights = lax.linalg.triangular_solve(lower_factor, coupling, left_side=True, lower=True, transpose_a=True)
    return (lower_factor.T, coupling, weights)

def split_weights(weights):
    weight_high = weights.astype(jnp.bfloat16)
    held_high = lax.optimization_barrier(weight_high)
    weight_low = (weights - held_high.astype(jnp.float32)).astype(jnp.bfloat16)
    return (weight_high, weight_low)

def reference(descriptors, gradients, sparse_panel, sparse_trail, atom_counts, owner_rows, neighbor_ids):
    environments = jnp.concatenate([sparse_panel, sparse_trail], axis=0)
    env_count = environments.shape[0]
    atoms_dev = N_ROW * AMAX

    def one_device(device_index):
        desc_here = lax.dynamic_slice_in_dim(descriptors, device_index * atoms_dev, atoms_dev, 0)
        slope_here = lax.dynamic_slice_in_dim(gradients, device_index * atoms_dev, atoms_dev, 2).reshape(-1, DESC)
        count_here = lax.dynamic_index_in_dim(atom_counts, device_index, 0, keepdims=False)
        owner_here = lax.dynamic_index_in_dim(owner_rows, device_index, 0, keepdims=False)
        neighbor_here = lax.dynamic_slice_in_dim(neighbor_ids, device_index * N_ROW, N_ROW, 0)
        return slot_rows(environments, desc_here, slope_here, count_here, neighbor_here, owner_here)
    per_device = lax.map(one_device, jnp.arange(DEVICES, dtype=jnp.int32))
    slot_count = per_device.shape[3]
    design = jnp.transpose(per_device.reshape(N_ROW, N_COL, env_count, N_ROW, slot_count), (2, 3, 1, 0, 4)).reshape(env_count, ROWS)
    design_panel = design[:PANEL]
    design_trail = design[PANEL:]
    gram_sum = lax.dot_general(design_panel.astype(jnp.float32), design_panel.astype(jnp.float32), (((1,), (1,)), ((), ())), preferred_element_type=jnp.float32)
    cross_sum = lax.dot_general(design_panel.astype(jnp.float32), design_trail.astype(jnp.float32), (((1,), (1,)), ((), ())), preferred_element_type=jnp.float32)
    panel_factor, coupling, weights = factor_panel(gram_sum, cross_sum, ROWS)
    weight_high, weight_low = split_weights(weights)
    projected = lax.dot_general(weight_high.astype(jnp.float32), design_panel.astype(jnp.float32), (((0,), (0,)), ((), ())), preferred_element_type=jnp.float32)
    projected = projected + lax.dot_general(weight_low.astype(jnp.float32), design_panel.astype(jnp.float32), (((0,), (0,)), ((), ())), preferred_element_type=jnp.float32)
    trail_residual = design_trail.astype(jnp.float32) - projected
    return (panel_factor, coupling.T, trail_residual)
```

```python
import functools

import jax
import jax.numpy as jnp
from jax import lax
from jax.experimental import pallas as pl
from jax.experimental.pallas import tpu as pltpu
from jax.sharding import PartitionSpec as P

ridge_value = 0.1
HIGHEST = lax.Precision.HIGHEST
F32 = jnp.float32
BF16 = jnp.bfloat16
NT = (((1,), (1,)), ((), ()))
NN = (((1,), (0,)), ((), ()))
TN = (((0,), (0,)), ((), ()))

CORE_SWAP = [(i, i ^ 1) for i in range(8)]


def y_shift(s):
    return [(2 * y + c, 2 * ((y + s) % 4) + c) for y in range(4) for c in range(2)]


def z_shift(s):
    return [(x * 4 + z, x * 4 + (z + s) % 4) for x in range(4) for z in range(4)]


def x_shift(s):
    return [(x * 4 + z, ((x + s) % 4) * 4 + z) for x in range(4) for z in range(4)]


def dot(a, b, dims, precision=None):
    return lax.dot_general(a, b, dims, precision=precision, preferred_element_type=F32)


def in_order(pieces, index):
    return jnp.concatenate(
        [lax.select_n((index - j) % 4, *pieces) for j in range(4)], axis=0
    )


def gather4(v, axis, shift, index):
    pieces = [v] + [lax.ppermute(v, axis, shift(s)) for s in (1, 2, 3)]
    return in_order(pieces, index)


def ring4(v, axis, shift, index):
    h = v.shape[0] // 2
    a = lax.ppermute(v, axis, shift(1))
    b = lax.ppermute(v, axis, shift(3))
    c = lax.ppermute(a[:h], axis, shift(1))
    d = lax.ppermute(b[h:], axis, shift(3))
    return in_order([v, a, jnp.concatenate([c, d], axis=0), b], index)


def scatter4(v, axis, shift, index):
    n = v.shape[0] // 4
    total = lax.dynamic_slice_in_dim(v, index * n, n, 0)
    got = [
        lax.ppermute(
            lax.dynamic_slice_in_dim(v, ((index + s) % 4) * n, n, 0), axis, shift(s)
        )
        for s in (1, 2, 3)
    ]
    return total + got[0] + got[1] + got[2]


def swap_add(v, core):
    n = v.shape[0] // 2
    mine = lax.dynamic_slice_in_dim(v, core * n, n, 0)
    other = lax.dynamic_slice_in_dim(v, (1 - core) * n, n, 0)
    return mine + lax.ppermute(other, "row", CORE_SWAP)


def swap_gather(v, core):
    other = lax.ppermute(v, "row", CORE_SWAP)
    first = core == 0
    return jnp.where(first, v, other), jnp.where(first, other, v)


def spread4(v, axis, shift):
    got = [lax.ppermute(v, axis, shift(s)) for s in (1, 2, 3)]
    return v + got[0] + got[1] + got[2]


def tables(count, owner, neighbors):
    structs = jnp.arange(8, dtype=jnp.int32)
    offset = jnp.sum(jnp.where(structs[None, :] < structs[:, None], count[None, :], 0), axis=1)
    atoms = jnp.arange(64, dtype=jnp.int32)
    inside = (atoms[:, None] >= offset[None, :]) & (
        atoms[:, None] < (offset + count)[None, :]
    )
    slot = jnp.sum(jnp.where(inside, 16 * structs + atoms[:, None] - offset, 0), axis=1)
    slots = jnp.arange(128, dtype=jnp.int32)
    live = slot[:, None] == slots[None, :]
    partner = (16 * structs[:, None, None] + neighbors % count[:, None, None]).reshape(128, 4)
    picked = jnp.sum(jnp.where(live[:, :, None], partner[None], 0), axis=1)
    rows = jnp.concatenate([slot, picked.T.reshape(256)])
    pick_atoms = (rows[:, None] == slots[None, :]).astype(BF16)
    mean = (inside.astype(F32) / count.astype(F32)[None, :]).T
    of_group = owner[None, :] == structs[:, None]
    struct_g = jnp.sum(jnp.where(of_group, structs[None, :], 0), axis=1)
    count_g = jnp.sum(jnp.where(of_group, count[None, :], 0), axis=1)
    offset_g = jnp.sum(jnp.where(of_group, offset[None, :], 0), axis=1)
    place = jnp.arange(64, dtype=jnp.int32)[None, :]
    atom, part = (place - 1) // 3, (place - 1) % 3
    is_force = (place >= 1) & (atom < count_g[:, None])
    column = jnp.where(is_force, part * 64 + offset_g[:, None] + atom, -1)
    column = jnp.where(place == 0, 192 + struct_g[:, None], column).reshape(512)
    order = (column[:, None] == jnp.arange(256, dtype=jnp.int32)[None, :]).astype(BF16)
    return pick_atoms, mean, order


def compact_rows(env, atoms, grads, mean):
    near = dot(atoms, env, NT)
    slope = dot(grads, env, NT)
    inner = near[:64]
    parts = []
    for k in range(3):
        total = near[64:128] * slope[k * 256 : k * 256 + 64]
        for j in range(1, 4):
            total = total + near[64 + j * 64 : 128 + j * 64] * slope[
                k * 256 + j * 64 : k * 256 + j * 64 + 64
            ]
        parts.append((-2.0 * total).astype(BF16))
    energy = dot(mean, inner * inner, NN, HIGHEST)
    pad = jnp.zeros((56, env.shape[0]), F32)
    parts.append(jnp.concatenate([energy, pad], axis=0).astype(BF16))
    return jnp.concatenate(parts, axis=0)


def panel_kernel(env_ref, atoms_ref, grads_ref, mean_ref, order_ref, out_ref, gram_ref):
    rows = compact_rows(env_ref[...], atoms_ref[...], grads_ref[...], mean_ref[...])
    out_ref[...] = dot(order_ref[...], rows, NN).astype(BF16).reshape(out_ref.shape)
    gram_ref[...] = dot(rows, rows, TN)


def trail_kernel(env_ref, atoms_ref, grads_ref, mean_ref, order_ref, out_ref):
    rows = compact_rows(env_ref[...], atoms_ref[...], grads_ref[...], mean_ref[...])
    full = dot(order_ref[...], rows, NN).astype(BF16)
    for c in range(out_ref.shape[1]):
        out_ref[:, c] = full[:, c * 128 : c * 128 + 128].reshape(8, 64, 128)


def params():
    return pltpu.CompilerParams(vmem_limit_bytes=40 << 20)


def panel_rows(env, atoms, grads, mean, order):
    m = env.shape[0]
    return pl.pallas_call(
        panel_kernel,
        out_shape=(
            jax.ShapeDtypeStruct((8, 64, m), BF16),
            jax.ShapeDtypeStruct((m, m), F32),
        ),
        compiler_params=params(),
        cost_estimate=pl.CostEstimate(
            flops=2 * m * 1024 * 1088, bytes_accessed=5 << 20, transcendentals=0
        ),
    )(env, atoms, grads, mean, order)


def trail_rows(env, atoms, grads, mean, order):
    m = env.shape[0]
    tile = 512
    whole = lambda shape: pl.BlockSpec(shape, lambda i: (0, 0))
    return pl.pallas_call(
        trail_kernel,
        out_shape=jax.ShapeDtypeStruct((8, m // 128, 64, 128), BF16),
        grid=(m // tile,),
        in_specs=[
            pl.BlockSpec((tile, 1024), lambda i: (i, 0)),
            whole(atoms.shape),
            whole(grads.shape),
            whole(mean.shape),
            whole(order.shape),
        ],
        out_specs=pl.BlockSpec((8, tile // 128, 64, 128), lambda i: (0, i, 0, 0)),
        compiler_params=params(),
        cost_estimate=pl.CostEstimate(
            flops=2 * m * 1024 * 1088, bytes_accessed=9 << 20, transcendentals=0
        ),
    )(env, atoms, grads, mean, order)


def eliminate(a):
    lanes = lax.broadcasted_iota(jnp.int32, (8, 128), 1)
    subs = lax.broadcasted_iota(jnp.int32, (8, 128), 0)
    left = [a[8 * g : 8 * g + 8] for g in range(16)]
    right = [(lanes == subs + 8 * g).astype(F32) for g in range(16)]
    done = []
    for p in range(16):
        count = 16 - p
        cols = [
            [
                jnp.broadcast_to(left[g][:, 8 * p + q : 8 * p + q + 1], (8, 128))
                for g in range(count)
            ]
            for q in range(8)
        ]
        pivots = jnp.ones((8, 128), F32)
        for q in range(8):
            pivot = cols[q][0][q : q + 1]
            inverse = 1.0 / pivot
            pivots = jnp.where(subs == q, pivot, pivots)
            ratio = [c * inverse for c in cols[q]]
            ratio[0] = jnp.where(subs > q, ratio[0], 0.0)
            for t in range(q + 1, 8):
                here = cols[t][0][q : q + 1]
                for g in range(count):
                    cols[t][g] = cols[t][g] - ratio[g] * here
            row_left = left[0][q : q + 1]
            row_right = right[0][q : q + 1]
            for g in range(count):
                left[g] = left[g] - ratio[g] * row_left
                right[g] = right[g] - ratio[g] * row_right
        done.append(right[0] * lax.rsqrt(pivots))
        left, right = left[1:], right[1:]
    return jnp.concatenate(done, axis=0)


def factor_kernel(rows_total, gram_ref, factor_ref, inverse_ref, work):
    n = gram_ref.shape[0]
    r = lax.broadcasted_iota(jnp.int32, (n, n), 0)
    c = lax.broadcasted_iota(jnp.int32, (n, n), 1)
    work[:, :n] = gram_ref[...] / rows_total + jnp.where(r == c, ridge_value, 0.0)
    work[:, n:] = jnp.where(r == c, 1.0, 0.0)

    def step(b, carry):
        at = pl.multiple_of(b * 128, 128)
        low = eliminate(work[pl.ds(at, 128), pl.ds(at, 128)])
        row = dot(low, work[pl.ds(at, 128), :], NN, HIGHEST)
        lane = lax.broadcasted_iota(jnp.int32, (128, n), 1)
        later = jnp.where(lane >= at + 128, row[:, :n], 0.0)
        work[...] = work[...] - dot(later, row, TN, HIGHEST)
        work[pl.ds(at, 128), :] = row
        return carry

    lax.fori_loop(0, n // 128, step, 0)
    factor_ref[...] = jnp.where(c >= r, work[:, :n], 0.0)
    inverse_ref[...] = jnp.where(c <= r, work[:, n:], 0.0)


def factor_panel(gram, rows_total):
    n = gram.shape[0]
    return pl.pallas_call(
        functools.partial(factor_kernel, float(rows_total)),
        out_shape=(jax.ShapeDtypeStruct((n, n), F32), jax.ShapeDtypeStruct((n, n), F32)),
        scratch_shapes=[pltpu.VMEM((n, 2 * n), F32)],
        compiler_params=params(),
        cost_estimate=pl.CostEstimate(
            flops=20 * n * n * n, bytes_accessed=4 << 20, transcendentals=n
        ),
    )(gram)


def cross_kernel(panel_ref, trail_ref, out_ref):
    @pl.when(pl.program_id(0) == 0)
    def _():
        out_ref[...] = jnp.zeros_like(out_ref)

    trail = trail_ref[...].reshape(512, 128)
    out_ref[...] += dot(trail, panel_ref[0], TN)


def cross_part(segment, trail):
    n = segment.shape[2]
    return pl.pallas_call(
        cross_kernel,
        out_shape=jax.ShapeDtypeStruct((128, n), F32),
        grid=(segment.shape[0],),
        in_specs=[
            pl.BlockSpec((1, 512, n), lambda i: (i, 0, 0)),
            pl.BlockSpec((8, 1, 64, 128), lambda i: (0, i, 0, 0)),
        ],
        out_specs=pl.BlockSpec((128, n), lambda i: (0, 0)),
        compiler_params=params(),
        cost_estimate=pl.CostEstimate(
            flops=2 * 128 * n * 8192, bytes_accessed=11 << 20, transcendentals=0
        ),
    )(segment, trail)


def residual_kernel(
    rows_total, cross_ref, inverse_ref, panel_ref, trail_ref, coupling_ref, out_ref, weights
):
    @pl.when(pl.program_id(0) == 0)
    def _():
        coupling = dot(cross_ref[...] / rows_total, inverse_ref[...], NT, HIGHEST)
        coupling_ref[...] = coupling
        solved = dot(coupling, inverse_ref[...], NN, HIGHEST)
        high = solved.astype(BF16)
        weights[:128] = high
        weights[128:] = (solved - high.astype(F32)).astype(BF16)

    r = lax.broadcasted_iota(jnp.int32, (128, 128), 0)
    c = lax.broadcasted_iota(jnp.int32, (128, 128), 1)
    same = (r == c).astype(BF16)
    both = dot(weights[...], panel_ref[0], NT)
    own = dot(same, trail_ref[...].reshape(512, 128), NT)
    out_ref[...] = own - both[:128] - both[128:]


def residual(cross, inverse, segment, trail, rows_total):
    n = inverse.shape[0]
    chunks = segment.shape[0]
    whole = lambda shape: pl.BlockSpec(shape, lambda i: (0, 0))
    return pl.pallas_call(
        functools.partial(residual_kernel, float(rows_total)),
        out_shape=(
            jax.ShapeDtypeStruct((128, n), F32),
            jax.ShapeDtypeStruct((128, 512 * chunks), F32),
        ),
        grid=(chunks,),
        in_specs=[
            whole((128, n)),
            whole((n, n)),
            pl.BlockSpec((1, 512, n), lambda i: (i, 0, 0)),
            pl.BlockSpec((8, 1, 64, 128), lambda i: (0, i, 0, 0)),
        ],
        out_specs=(whole((128, n)), pl.BlockSpec((128, 512), lambda i: (0, i))),
        scratch_shapes=[pltpu.VMEM((256, n), BF16)],
        compiler_params=params(),
        cost_estimate=pl.CostEstimate(
            flops=4 * 128 * n * 8192, bytes_accessed=16 << 20, transcendentals=0
        ),
    )(cross, inverse, segment, trail)


def sum_all(v, core, y):
    v = scatter4(swap_add(v, core), "row", y_shift, y)
    v = spread4(spread4(v, "col", z_shift), "col", x_shift)
    v = gather4(v, "row", y_shift, y)
    return jnp.concatenate(swap_gather(v, core), axis=0)


def sum_row(v, core, y):
    v = scatter4(swap_add(v, core), "row", y_shift, y)
    v = gather4(v, "row", y_shift, y)
    return jnp.concatenate(swap_gather(v, core), axis=0)


def per_device(
    descriptors, gradients, sparse_panel, sparse_trail, atom_counts, owner_rows, neighbor_ids
):
    row = lax.axis_index("row")
    col = lax.axis_index("col")
    core, y = row % 2, row // 2
    x, z = col // 4, col % 4
    rows_total = 65536

    own = lax.dynamic_slice_in_dim(sparse_panel, core * 16, 16, 0)
    own = gather4(gather4(own, "col", z_shift, z), "col", x_shift, x)
    low, high = swap_gather(own, core)
    env_panel = jnp.stack(
        [low.reshape(16, 16, 1024), high.reshape(16, 16, 1024)], axis=1
    ).reshape(512, 1024)

    pick_atoms, mean, order = tables(atom_counts[0], owner_rows[0], neighbor_ids)
    atoms = dot(pick_atoms, descriptors, NN).astype(BF16)
    grads = lax.dot_general(
        gradients.reshape(12, 128, 1024),
        pick_atoms[:64],
        (((1,), (1,)), ((), ())),
        preferred_element_type=F32,
    )
    grads = jnp.transpose(grads, (0, 2, 1)).astype(BF16).reshape(768, 1024)

    panel, gram = panel_rows(env_panel, atoms, grads, mean, order)
    panel = lax.all_to_all(panel, "row", 0, 0, tiled=True).reshape(512, 512)
    segment = lax.all_gather(panel, "col", axis=0, tiled=False)

    own = lax.dynamic_slice_in_dim(sparse_trail, row * 16, 16, 0)
    own = gather4(gather4(own, "col", z_shift, z), "col", x_shift, x)
    own = ring4(own, "row", y_shift, y)
    low, high = swap_gather(own, core)
    env_trail = jnp.stack(
        [low.reshape(4, 16, 16, 1024), high.reshape(4, 16, 16, 1024)], axis=1
    )
    env_trail = jnp.transpose(env_trail, (2, 0, 1, 3, 4)).reshape(2048, 1024)
    trail = trail_rows(env_trail, atoms, grads, mean, order).reshape(128, 64, 128)
    trail = lax.all_to_all(trail, ("row", "col"), 0, 0, tiled=True).reshape(8, 16, 64, 128)

    gram = sum_all(gram, core, y)
    factor, inverse = factor_panel(gram, rows_total)

    cross = sum_row(cross_part(segment, trail), core, y)
    coupling, result = residual(cross, inverse, segment, trail, rows_total)
    return factor, coupling, result


def solution(mesh):
    return jax.shard_map(
        per_device,
        mesh=mesh,
        in_specs=(
            P(("row", "col"), None),
            P(None, None, ("row", "col"), None),
            P("col", None),
            P("col", None),
            P(("row", "col"), None),
            P(("row", "col"), None),
            P(("row", "col"), None, None),
        ),
        out_specs=(P(), P("col", None), P("col", "row")),
        check_vma=False,
    )
```

```python
import functools

import jax
import jax.numpy as jnp
from jax import lax
from jax.experimental import pallas as pl
from jax.experimental.pallas import tpu as pltpu
from jax.sharding import PartitionSpec as P

ridge_value = 0.1
HIGHEST = lax.Precision.HIGHEST
F32 = jnp.float32
BF16 = jnp.bfloat16
NT = (((1,), (1,)), ((), ()))
NN = (((1,), (0,)), ((), ()))
TN = (((0,), (0,)), ((), ()))

CORE_SWAP = [(i, i ^ 1) for i in range(8)]


def y_shift(s):
    return [(2 * y + c, 2 * ((y + s) % 4) + c) for y in range(4) for c in range(2)]


def z_shift(s):
    return [(x * 4 + z, x * 4 + (z + s) % 4) for x in range(4) for z in range(4)]


def x_shift(s):
    return [(x * 4 + z, ((x + s) % 4) * 4 + z) for x in range(4) for z in range(4)]


def dot(a, b, dims, precision=None):
    return lax.dot_general(a, b, dims, precision=precision, preferred_element_type=F32)


def in_order(pieces, index):
    return jnp.concatenate(
        [lax.select_n((index - j) % 4, *pieces) for j in range(4)], axis=0
    )


def gather4(v, axis, shift, index):
    pieces = [v] + [lax.ppermute(v, axis, shift(s)) for s in (1, 2, 3)]
    return in_order(pieces, index)


def ring4(v, axis, shift, index):
    h = v.shape[0] // 2
    a = lax.ppermute(v, axis, shift(1))
    b = lax.ppermute(v, axis, shift(3))
    c = lax.ppermute(a[:h], axis, shift(1))
    d = lax.ppermute(b[h:], axis, shift(3))
    return in_order([v, a, jnp.concatenate([c, d], axis=0), b], index)


def scatter4(v, axis, shift, index):
    n = v.shape[0] // 4
    total = lax.dynamic_slice_in_dim(v, index * n, n, 0)
    got = [
        lax.ppermute(
            lax.dynamic_slice_in_dim(v, ((index + s) % 4) * n, n, 0), axis, shift(s)
        )
        for s in (1, 2, 3)
    ]
    return total + got[0] + got[1] + got[2]


def swap_add(v, core):
    n = v.shape[0] // 2
    mine = lax.dynamic_slice_in_dim(v, core * n, n, 0)
    other = lax.dynamic_slice_in_dim(v, (1 - core) * n, n, 0)
    return mine + lax.ppermute(other, "row", CORE_SWAP)


def swap_gather(v, core):
    other = lax.ppermute(v, "row", CORE_SWAP)
    first = core == 0
    return jnp.where(first, v, other), jnp.where(first, other, v)


def spread4(v, axis, shift):
    got = [lax.ppermute(v, axis, shift(s)) for s in (1, 2, 3)]
    return v + got[0] + got[1] + got[2]


def prep_kernel(
    count_ref, owner_ref, neighbor_ref, desc_ref, grad_ref, atoms_ref, grads_ref, mean_ref, order_ref
):
    counts = [count_ref[0, s] for s in range(8)]
    owners = [owner_ref[0, s] for s in range(8)]
    offsets = [jnp.int32(0)]
    for s in range(7):
        offsets.append(offsets[s] + counts[s])

    lane = lax.broadcasted_iota(jnp.int32, (8, 128), 1)
    struct, atom = lane >> 4, lane & 15
    count_l, offset_l = jnp.ones((8, 128), jnp.int32), jnp.zeros((8, 128), jnp.int32)
    for s in range(8):
        count_l = jnp.where(struct == s, counts[s], count_l)
        offset_l = jnp.where(struct == s, offsets[s], offset_l)
    place = jnp.where(atom < count_l, offset_l + atom, -1)
    rows = lax.broadcasted_iota(jnp.int32, (64, 128), 0)
    lanes = lax.broadcasted_iota(jnp.int32, (64, 128), 1)
    live = place[:1] == rows
    live_f = live.astype(F32)

    value = neighbor_ref[...].astype(F32)
    size = count_l.astype(F32)[:4]
    rest = value - size * jnp.floor(value / size)
    rest = jnp.where(rest < 0.0, rest + size, rest)
    rest = jnp.where(rest >= size, rest - size, rest)
    partner = rest + (16 * struct).astype(F32)[:4]

    picks = [live_f.astype(BF16)]
    for j in range(4):
        slot = jnp.sum(live_f * partner[j : j + 1], axis=1, keepdims=True)
        picks.append((slot == lanes.astype(F32)).astype(F32).astype(BF16))
    desc = desc_ref[...]
    for j in range(5):
        atoms_ref[64 * j : 64 * j + 64] = dot(picks[j], desc, NN).astype(BF16)
    for i in range(12):
        grads_ref[64 * i : 64 * i + 64] = dot(picks[0], grad_ref[i], NN).astype(BF16)

    sub8 = lax.broadcasted_iota(jnp.int32, (8, 64), 0)
    atom8 = lax.broadcasted_iota(jnp.int32, (8, 64), 1)
    low, size8 = jnp.zeros((8, 64), jnp.int32), jnp.ones((8, 64), jnp.int32)
    for s in range(8):
        low = jnp.where(sub8 == s, offsets[s], low)
        size8 = jnp.where(sub8 == s, counts[s], size8)
    inside = (atom8 >= low) & (atom8 < low + size8)
    mean_ref[...] = jnp.where(inside, 1.0 / size8.astype(F32), 0.0)

    r = lax.broadcasted_iota(jnp.int32, (64, 256), 0)
    wanted = lax.broadcasted_iota(jnp.int32, (64, 256), 1)
    third = ((r - 1) * 43) >> 7
    part = (r - 1) - 3 * third
    for g in range(8):
        struct_g, count_g, offset_g = jnp.int32(0), jnp.int32(0), jnp.int32(0)
        for s in range(8):
            mine = owners[s] == g
            struct_g = jnp.where(mine, s, struct_g)
            count_g = jnp.where(mine, counts[s], count_g)
            offset_g = jnp.where(mine, offsets[s], offset_g)
        column = jnp.where(third < count_g, part * 64 + offset_g + third, -1)
        column = jnp.where(r == 0, 192 + struct_g, column)
        order_ref[64 * g : 64 * g + 64] = (column == wanted).astype(F32).astype(BF16)


def prepare(count, owner, neighbors, descriptors, gradients):
    smem = pl.BlockSpec(memory_space=pltpu.SMEM)
    vmem = pl.BlockSpec(memory_space=pltpu.VMEM)
    return pl.pallas_call(
        prep_kernel,
        out_shape=(
            jax.ShapeDtypeStruct((320, 1024), BF16),
            jax.ShapeDtypeStruct((768, 1024), BF16),
            jax.ShapeDtypeStruct((8, 64), F32),
            jax.ShapeDtypeStruct((512, 256), BF16),
        ),
        in_specs=[smem, smem, vmem, vmem, vmem],
        out_specs=(vmem, vmem, vmem, vmem),
        compiler_params=params(),
        cost_estimate=pl.CostEstimate(
            flops=2 * 64 * 128 * 1024 * 17, bytes_accessed=6 << 20, transcendentals=0
        ),
    )(count, owner, neighbors, descriptors, gradients)


def compact_rows(env, atoms, grads, mean):
    near = dot(atoms, env, NT)
    slope = dot(grads, env, NT)
    inner = near[:64]
    parts = []
    for k in range(3):
        total = near[64:128] * slope[k * 256 : k * 256 + 64]
        for j in range(1, 4):
            total = total + near[64 + j * 64 : 128 + j * 64] * slope[
                k * 256 + j * 64 : k * 256 + j * 64 + 64
            ]
        parts.append((-2.0 * total).astype(BF16))
    energy = dot(mean, inner * inner, NN, HIGHEST)
    pad = jnp.zeros((56, env.shape[0]), F32)
    parts.append(jnp.concatenate([energy, pad], axis=0).astype(BF16))
    return jnp.concatenate(parts, axis=0)


def panel_kernel(env_ref, atoms_ref, grads_ref, mean_ref, order_ref, out_ref, gram_ref):
    rows = compact_rows(env_ref[...], atoms_ref[...], grads_ref[...], mean_ref[...])
    out_ref[...] = dot(order_ref[...], rows, NN).astype(BF16).reshape(out_ref.shape)
    gram_ref[...] = dot(rows, rows, TN)


def trail_kernel(
    core_ref, own_ref, other_ref, atoms_ref, grads_ref, mean_ref, order_ref, out_ref
):
    first = core_ref[0] == 0
    own, other = own_ref[...], other_ref[...]
    low, high = jnp.where(first, own, other), jnp.where(first, other, own)
    env = jnp.concatenate([low, high], axis=1).reshape(-1, 1024)
    rows = compact_rows(env, atoms_ref[...], grads_ref[...], mean_ref[...])
    full = dot(order_ref[...], rows, NN).astype(BF16)
    for c in range(out_ref.shape[1]):
        out_ref[:, c] = full[:, c * 128 : c * 128 + 128].reshape(8, 64, 128)


def params():
    return pltpu.CompilerParams(vmem_limit_bytes=40 << 20)


def panel_rows(env, atoms, grads, mean, order):
    m = env.shape[0]
    return pl.pallas_call(
        panel_kernel,
        out_shape=(
            jax.ShapeDtypeStruct((8, 64, m), BF16),
            jax.ShapeDtypeStruct((m, m), F32),
        ),
        compiler_params=params(),
        cost_estimate=pl.CostEstimate(
            flops=2 * m * 1024 * 1088, bytes_accessed=5 << 20, transcendentals=0
        ),
    )(env, atoms, grads, mean, order)


def trail_rows(core, own, other, atoms, grads, mean, order):
    blocks = own.shape[0]
    step = 4
    half = pl.BlockSpec((step, 64, 1024), lambda i, core: (i, 0, 0))
    whole = lambda shape: pl.BlockSpec(shape, lambda i, core: (0, 0))
    return pl.pallas_call(
        trail_kernel,
        out_shape=jax.ShapeDtypeStruct((8, blocks, 64, 128), BF16),
        grid_spec=pltpu.PrefetchScalarGridSpec(
            num_scalar_prefetch=1,
            grid=(blocks // step,),
            in_specs=[
                half,
                half,
                whole(atoms.shape),
                whole(grads.shape),
                whole(mean.shape),
                whole(order.shape),
            ],
            out_specs=pl.BlockSpec((8, step, 64, 128), lambda i, core: (0, i, 0, 0)),
        ),
        compiler_params=params(),
        cost_estimate=pl.CostEstimate(
            flops=2 * 2048 * 1024 * 1088, bytes_accessed=9 << 20, transcendentals=0
        ),
    )(core.reshape(1).astype(jnp.int32), own, other, atoms, grads, mean, order)


def eliminate(a):
    lanes = lax.broadcasted_iota(jnp.int32, (8, 128), 1)
    subs = lax.broadcasted_iota(jnp.int32, (8, 128), 0)
    left = [a[8 * g : 8 * g + 8] for g in range(16)]
    right = [(lanes == subs + 8 * g).astype(F32) for g in range(16)]
    done = []
    for p in range(16):
        count = 16 - p
        cols = [
            [
                jnp.broadcast_to(left[g][:, 8 * p + q : 8 * p + q + 1], (8, 128))
                for g in range(count)
            ]
            for q in range(8)
        ]
        pivots = jnp.ones((8, 128), F32)
        for q in range(8):
            pivot = cols[q][0][q : q + 1]
            inverse = 1.0 / pivot
            pivots = jnp.where(subs == q, pivot, pivots)
            ratio = [c * inverse for c in cols[q]]
            ratio[0] = jnp.where(subs > q, ratio[0], 0.0)
            for t in range(q + 1, 8):
                here = cols[t][0][q : q + 1]
                for g in range(count):
                    cols[t][g] = cols[t][g] - ratio[g] * here
            row_left = left[0][q : q + 1]
            row_right = right[0][q : q + 1]
            for g in range(count):
                left[g] = left[g] - ratio[g] * row_left
                right[g] = right[g] - ratio[g] * row_right
        done.append(right[0] * lax.rsqrt(pivots))
        left, right = left[1:], right[1:]
    return jnp.concatenate(done, axis=0)


def factor_kernel(rows_total, gram_ref, factor_ref, inverse_ref, work):
    n = gram_ref.shape[0]
    r = lax.broadcasted_iota(jnp.int32, (n, n), 0)
    c = lax.broadcasted_iota(jnp.int32, (n, n), 1)
    work[:, :n] = gram_ref[...] / rows_total + jnp.where(r == c, ridge_value, 0.0)
    work[:, n:] = jnp.where(r == c, 1.0, 0.0)

    def step(b, carry):
        at = pl.multiple_of(b * 128, 128)
        low = eliminate(work[pl.ds(at, 128), pl.ds(at, 128)])
        row = dot(low, work[pl.ds(at, 128), :], NN, HIGHEST)
        lane = lax.broadcasted_iota(jnp.int32, (128, n), 1)
        later = jnp.where(lane >= at + 128, row[:, :n], 0.0)
        work[...] = work[...] - dot(later, row, TN, HIGHEST)
        work[pl.ds(at, 128), :] = row
        return carry

    lax.fori_loop(0, n // 128, step, 0)
    factor_ref[...] = jnp.where(c >= r, work[:, :n], 0.0)
    inverse_ref[...] = jnp.where(c <= r, work[:, n:], 0.0)


def factor_panel(gram, rows_total):
    n = gram.shape[0]
    return pl.pallas_call(
        functools.partial(factor_kernel, float(rows_total)),
        out_shape=(jax.ShapeDtypeStruct((n, n), F32), jax.ShapeDtypeStruct((n, n), F32)),
        scratch_shapes=[pltpu.VMEM((n, 2 * n), F32)],
        compiler_params=params(),
        cost_estimate=pl.CostEstimate(
            flops=20 * n * n * n, bytes_accessed=4 << 20, transcendentals=n
        ),
    )(gram)


def cross_kernel(panel_ref, trail_ref, out_ref):
    @pl.when(pl.program_id(0) == 0)
    def _():
        out_ref[...] = jnp.zeros_like(out_ref)

    n = panel_ref.shape[2]
    trail = jnp.concatenate(
        [trail_ref[:, i].reshape(512, 128) for i in range(panel_ref.shape[0])], axis=0
    )
    out_ref[...] += dot(trail, panel_ref[...].reshape(-1, n), TN)


def cross_part(segment, trail):
    n = segment.shape[2]
    return pl.pallas_call(
        cross_kernel,
        out_shape=jax.ShapeDtypeStruct((128, n), F32),
        grid=(segment.shape[0] // 4,),
        in_specs=[
            pl.BlockSpec((4, 512, n), lambda i: (i, 0, 0)),
            pl.BlockSpec((8, 4, 64, 128), lambda i: (0, i, 0, 0)),
        ],
        out_specs=pl.BlockSpec((128, n), lambda i: (0, 0)),
        compiler_params=params(),
        cost_estimate=pl.CostEstimate(
            flops=2 * 128 * n * 8192, bytes_accessed=11 << 20, transcendentals=0
        ),
    )(segment, trail)


def residual_kernel(
    rows_total, cross_ref, inverse_ref, panel_ref, trail_ref, coupling_ref, out_ref, weights
):
    @pl.when(pl.program_id(0) == 0)
    def _():
        coupling = dot(cross_ref[...] / rows_total, inverse_ref[...], NT, HIGHEST)
        coupling_ref[...] = coupling
        solved = dot(coupling, inverse_ref[...], NN, HIGHEST)
        high = solved.astype(BF16)
        weights[:128] = high
        weights[128:] = (solved - high.astype(F32)).astype(BF16)

    r = lax.broadcasted_iota(jnp.int32, (128, 128), 0)
    c = lax.broadcasted_iota(jnp.int32, (128, 128), 1)
    same = (r == c).astype(BF16)
    for i in range(panel_ref.shape[0]):
        both = dot(weights[...], panel_ref[i], NT)
        own = dot(same, trail_ref[:, i].reshape(512, 128), NT)
        out_ref[:, i * 512 : i * 512 + 512] = own - both[:128] - both[128:]


def residual(cross, inverse, segment, trail, rows_total):
    n = inverse.shape[0]
    chunks = segment.shape[0]
    whole = lambda shape: pl.BlockSpec(shape, lambda i: (0, 0))
    return pl.pallas_call(
        functools.partial(residual_kernel, float(rows_total)),
        out_shape=(
            jax.ShapeDtypeStruct((128, n), F32),
            jax.ShapeDtypeStruct((128, 512 * chunks), F32),
        ),
        grid=(chunks // 4,),
        in_specs=[
            whole((128, n)),
            whole((n, n)),
            pl.BlockSpec((4, 512, n), lambda i: (i, 0, 0)),
            pl.BlockSpec((8, 4, 64, 128), lambda i: (0, i, 0, 0)),
        ],
        out_specs=(whole((128, n)), pl.BlockSpec((128, 2048), lambda i: (0, i))),
        scratch_shapes=[pltpu.VMEM((256, n), BF16)],
        compiler_params=params(),
        cost_estimate=pl.CostEstimate(
            flops=4 * 128 * n * 8192, bytes_accessed=16 << 20, transcendentals=0
        ),
    )(cross, inverse, segment, trail)


def sum_all(v, core, y):
    v = scatter4(swap_add(v, core), "row", y_shift, y)
    v = spread4(spread4(v, "col", z_shift), "col", x_shift)
    v = gather4(v, "row", y_shift, y)
    return jnp.concatenate(swap_gather(v, core), axis=0)


def sum_row(v, core):
    v = spread4(swap_add(v, core), "row", y_shift)
    return jnp.concatenate(swap_gather(v, core), axis=0)


def per_device(
    descriptors, gradients, sparse_panel, sparse_trail, atom_counts, owner_rows, neighbor_ids
):
    row = lax.axis_index("row")
    col = lax.axis_index("col")
    core, y = row % 2, row // 2
    x, z = col // 4, col % 4
    rows_total = 65536

    trail_half = lax.dynamic_slice_in_dim(sparse_trail, core * 64, 64, 0)
    trail_half = lax.all_gather(trail_half, "col", axis=0, tiled=False)
    own = lax.dynamic_slice_in_dim(sparse_panel, core * 16, 16, 0)
    own = gather4(gather4(own, "col", z_shift, z), "col", x_shift, x)
    low, high = swap_gather(own, core)
    env_panel = jnp.stack(
        [low.reshape(16, 16, 1024), high.reshape(16, 16, 1024)], axis=1
    ).reshape(512, 1024)

    atoms, grads, mean, order = prepare(
        atom_counts,
        owner_rows,
        neighbor_ids.reshape(128, 4).T,
        descriptors,
        gradients.reshape(12, 128, 1024),
    )

    panel, gram = panel_rows(env_panel, atoms, grads, mean, order)
    panel = lax.all_to_all(panel, "row", 0, 0, tiled=True).reshape(512, 512)
    panel, gram = lax.optimization_barrier((panel, gram))
    segment = lax.all_gather(panel, "col", axis=0, tiled=False)
    gram = sum_all(gram, core, y)

    trail_half, gram = lax.optimization_barrier((trail_half, gram))
    other_half = lax.ppermute(trail_half, "row", CORE_SWAP)
    trail = trail_rows(core, trail_half, other_half, atoms, grads, mean, order)
    trail, gram = lax.optimization_barrier((trail, gram))
    trail = lax.all_to_all(
        trail.reshape(128, 64, 128), ("row", "col"), 0, 0, tiled=True
    ).reshape(8, 16, 64, 128)
    factor, inverse = factor_panel(gram, rows_total)

    segment, inverse = lax.optimization_barrier((segment, inverse))
    cross = sum_row(cross_part(segment, trail), core)
    coupling, result = residual(cross, inverse, segment, trail, rows_total)
    return factor, coupling, result


def solution(mesh):
    return jax.shard_map(
        per_device,
        mesh=mesh,
        in_specs=(
            P(("row", "col"), None),
            P(None, None, ("row", "col"), None),
            P("col", None),
            P("col", None),
            P(("row", "col"), None),
            P(("row", "col"), None),
            P(("row", "col"), None, None),
        ),
        out_specs=(P(), P("col", None), P("col", "row")),
        check_vma=False,
    )
```

```python
import functools

import jax
import jax.numpy as jnp
from jax import lax
from jax.experimental import pallas as pl
from jax.experimental.pallas import tpu as pltpu
from jax.sharding import PartitionSpec as P

ridge_value = 0.1
HIGHEST = lax.Precision.HIGHEST
F32 = jnp.float32
BF16 = jnp.bfloat16
NT = (((1,), (1,)), ((), ()))
NN = (((1,), (0,)), ((), ()))
TN = (((0,), (0,)), ((), ()))

CORE_SWAP = [(i, i ^ 1) for i in range(8)]


def y_shift(s):
    return [(2 * y + c, 2 * ((y + s) % 4) + c) for y in range(4) for c in range(2)]


def z_shift(s):
    return [(x * 4 + z, x * 4 + (z + s) % 4) for x in range(4) for z in range(4)]


def x_shift(s):
    return [(x * 4 + z, ((x + s) % 4) * 4 + z) for x in range(4) for z in range(4)]


UPPER = [(i, j) for i in range(4) for j in range(i, 4)]


def dot(a, b, dims, precision=None):
    return lax.dot_general(a, b, dims, precision=precision, preferred_element_type=F32)


def in_order(pieces, index):
    return jnp.concatenate(
        [lax.select_n((index - j) % 4, *pieces) for j in range(4)], axis=0
    )


def shifted(v, axis, shift):
    return [v] + [lax.ppermute(v, axis, shift(s)) for s in (1, 2, 3)]


def gather4(v, axis, shift, index):
    pieces = [v] + [lax.ppermute(v, axis, shift(s)) for s in (1, 2, 3)]
    return in_order(pieces, index)


def scatter4(v, axis, shift, index):
    n = v.shape[0] // 4
    total = lax.dynamic_slice_in_dim(v, index * n, n, 0)
    got = [
        lax.ppermute(
            lax.dynamic_slice_in_dim(v, ((index + s) % 4) * n, n, 0), axis, shift(s)
        )
        for s in (1, 2, 3)
    ]
    return total + got[0] + got[1] + got[2]


def swap_add(v, core):
    n = v.shape[0] // 2
    mine = lax.dynamic_slice_in_dim(v, core * n, n, 0)
    other = lax.dynamic_slice_in_dim(v, (1 - core) * n, n, 0)
    return mine + lax.ppermute(other, "row", CORE_SWAP)


def swap_gather(v, core):
    other = lax.ppermute(v, "row", CORE_SWAP)
    first = core == 0
    return jnp.where(first, v, other), jnp.where(first, other, v)


def spread4(v, axis, shift):
    got = [lax.ppermute(v, axis, shift(s)) for s in (1, 2, 3)]
    return v + got[0] + got[1] + got[2]


def prep_kernel(
    count_ref, owner_ref, neighbor_ref, desc_ref, grad_ref, atoms_ref, grads_ref, mean_ref, order_ref
):
    counts = [count_ref[0, s] for s in range(8)]
    owners = [owner_ref[0, s] for s in range(8)]
    offsets = [jnp.int32(0)]
    for s in range(7):
        offsets.append(offsets[s] + counts[s])

    lane = lax.broadcasted_iota(jnp.int32, (8, 128), 1)
    struct, atom = lane >> 4, lane & 15
    count_l, offset_l = jnp.ones((8, 128), jnp.int32), jnp.zeros((8, 128), jnp.int32)
    for s in range(8):
        count_l = jnp.where(struct == s, counts[s], count_l)
        offset_l = jnp.where(struct == s, offsets[s], offset_l)
    place = jnp.where(atom < count_l, offset_l + atom, -1)
    rows = lax.broadcasted_iota(jnp.int32, (64, 128), 0)
    lanes = lax.broadcasted_iota(jnp.int32, (64, 128), 1)
    live = place[:1] == rows
    live_f = live.astype(F32)

    value = neighbor_ref[...].astype(F32)
    size = count_l.astype(F32)[:4]
    rest = value - size * jnp.floor(value / size)
    rest = jnp.where(rest < 0.0, rest + size, rest)
    rest = jnp.where(rest >= size, rest - size, rest)
    partner = rest + (16 * struct).astype(F32)[:4]

    picks = [live_f.astype(BF16)]
    for j in range(4):
        slot = jnp.sum(live_f * partner[j : j + 1], axis=1, keepdims=True)
        picks.append((slot == lanes.astype(F32)).astype(F32).astype(BF16))
    desc = desc_ref[...]
    for j in range(5):
        atoms_ref[64 * j : 64 * j + 64] = dot(picks[j], desc, NN).astype(BF16)
    for i in range(12):
        grads_ref[64 * i : 64 * i + 64] = dot(picks[0], grad_ref[i], NN).astype(BF16)

    sub8 = lax.broadcasted_iota(jnp.int32, (8, 64), 0)
    atom8 = lax.broadcasted_iota(jnp.int32, (8, 64), 1)
    low, size8 = jnp.zeros((8, 64), jnp.int32), jnp.ones((8, 64), jnp.int32)
    for s in range(8):
        low = jnp.where(sub8 == s, offsets[s], low)
        size8 = jnp.where(sub8 == s, counts[s], size8)
    inside = (atom8 >= low) & (atom8 < low + size8)
    mean_ref[...] = jnp.where(inside, 1.0 / size8.astype(F32), 0.0)

    r = lax.broadcasted_iota(jnp.int32, (64, 256), 0)
    wanted = lax.broadcasted_iota(jnp.int32, (64, 256), 1)
    third = ((r - 1) * 43) >> 7
    part = (r - 1) - 3 * third
    for g in range(8):
        struct_g, count_g, offset_g = jnp.int32(0), jnp.int32(0), jnp.int32(0)
        for s in range(8):
            mine = owners[s] == g
            struct_g = jnp.where(mine, s, struct_g)
            count_g = jnp.where(mine, counts[s], count_g)
            offset_g = jnp.where(mine, offsets[s], offset_g)
        column = jnp.where(third < count_g, part * 64 + offset_g + third, -1)
        column = jnp.where(r == 0, 192 + struct_g, column)
        order_ref[64 * g : 64 * g + 64] = (column == wanted).astype(F32).astype(BF16)


def prepare(count, owner, neighbors, descriptors, gradients):
    smem = pl.BlockSpec(memory_space=pltpu.SMEM)
    vmem = pl.BlockSpec(memory_space=pltpu.VMEM)
    return pl.pallas_call(
        prep_kernel,
        out_shape=(
            jax.ShapeDtypeStruct((320, 1024), BF16),
            jax.ShapeDtypeStruct((768, 1024), BF16),
            jax.ShapeDtypeStruct((8, 64), F32),
            jax.ShapeDtypeStruct((512, 256), BF16),
        ),
        in_specs=[smem, smem, vmem, vmem, vmem],
        out_specs=(vmem, vmem, vmem, vmem),
        compiler_params=params(),
        cost_estimate=pl.CostEstimate(
            flops=2 * 64 * 128 * 1024 * 17, bytes_accessed=6 << 20, transcendentals=0
        ),
    )(count, owner, neighbors, descriptors, gradients)


def compact_rows(env, atoms, grads, mean):
    near = dot(atoms, env, NT)
    slope = dot(grads, env, NT)
    inner = near[:64]
    parts = []
    for k in range(3):
        total = near[64:128] * slope[k * 256 : k * 256 + 64]
        for j in range(1, 4):
            total = total + near[64 + j * 64 : 128 + j * 64] * slope[
                k * 256 + j * 64 : k * 256 + j * 64 + 64
            ]
        parts.append((-2.0 * total).astype(BF16))
    energy = dot(mean, inner * inner, NN, HIGHEST)
    pad = jnp.zeros((56, env.shape[0]), F32)
    parts.append(jnp.concatenate([energy, pad], axis=0).astype(BF16))
    return jnp.concatenate(parts, axis=0)


def put_env(env, where, own, other, block, at):
    core = where[3]
    env[pl.ds(pl.multiple_of(at + core * 16, 16), 16)] = own[block]
    env[pl.ds(pl.multiple_of(at + (1 - core) * 16, 16), 16)] = other[block]


def panel_kernel(
    where, own, other, atoms_ref, grads_ref, mean_ref, order_ref, near_ref, far_ref, gram_ref, env
):
    x, z, y, core = where[0], where[1], where[2], where[3]
    for i in range(4):
        for j in range(4):
            place = ((x - i) & 3) * 4 + ((z - j) & 3)
            put_env(env, where, own, other, (i, j), place * 32)
    rows = compact_rows(env[...], atoms_ref[...], grads_ref[...], mean_ref[...])
    full = dot(order_ref[...], rows, NN).astype(BF16)
    first = core == 0
    for i in range(4):
        low, high = full[128 * i : 128 * i + 64], full[128 * i + 64 : 128 * i + 128]
        s = (i - y) & 3
        near_ref[s] = jnp.where(first, low, high)
        far_ref[s] = jnp.where(first, high, low)
    gram = dot(rows, rows, TN)
    for n, (i, j) in enumerate(UPPER):
        gram_ref[128 * n : 128 * n + 128] = gram[
            128 * i : 128 * i + 128, 128 * j : 128 * j + 128
        ]


def trail_kernel(
    where,
    own0,
    own1,
    own2,
    own3,
    other0,
    other1,
    other2,
    other3,
    atoms_ref,
    grads_ref,
    mean_ref,
    order_ref,
    out_ref,
    env,
):
    z, y = where[1], where[2]
    pairs = [(own0, other0), (own1, other1), (own2, other2), (own3, other3)]
    for j in range(4):
        place = ((z - j) & 3) * 128
        for s in range(4):
            own, other = pairs[s]
            put_env(env, where, own, other, (0, j), place + ((y - s) & 3) * 32)
    rows = compact_rows(env[...], atoms_ref[...], grads_ref[...], mean_ref[...])
    full = dot(order_ref[...], rows, NN).astype(BF16)
    for c in range(out_ref.shape[1]):
        out_ref[:, c] = full[:, c * 128 : c * 128 + 128].reshape(8, 64, 128)


def assemble_kernel(where, near, far, got1, got2, got3, out):
    y, core = where[2], where[3]
    out[2 * y + core] = near[0]
    out[2 * y + 1 - core] = far[0]
    for s, got in ((1, got1), (2, got2), (3, got3)):
        at = 2 * ((y - s) & 3)
        out[at + core] = got[0]
        out[at + 1 - core] = got[1]


def params():
    return pltpu.CompilerParams(vmem_limit_bytes=40 << 20)


def in_smem():
    return pl.BlockSpec(memory_space=pltpu.SMEM)


def in_vmem():
    return pl.BlockSpec(memory_space=pltpu.VMEM)


def panel_rows(where, own, other, atoms, grads, mean, order):
    return pl.pallas_call(
        panel_kernel,
        out_shape=(
            jax.ShapeDtypeStruct((4, 64, 512), BF16),
            jax.ShapeDtypeStruct((4, 64, 512), BF16),
            jax.ShapeDtypeStruct((1280, 128), F32),
        ),
        in_specs=[in_smem()] + [in_vmem()] * 6,
        out_specs=(in_vmem(),) * 3,
        scratch_shapes=[pltpu.VMEM((512, 1024), BF16)],
        compiler_params=params(),
        cost_estimate=pl.CostEstimate(
            flops=2 * 512 * 1024 * 1088, bytes_accessed=5 << 20, transcendentals=0
        ),
    )(where, own, other, atoms, grads, mean, order)


def assemble(where, near, far, got):
    return pl.pallas_call(
        assemble_kernel,
        out_shape=jax.ShapeDtypeStruct((8, 64, 512), BF16),
        in_specs=[in_smem()] + [in_vmem()] * 5,
        out_specs=in_vmem(),
        compiler_params=params(),
        cost_estimate=pl.CostEstimate(flops=0, bytes_accessed=1 << 20, transcendentals=0),
    )(where, near, far, *got)


def trail_rows(where, own, other, atoms, grads, mean, order):
    piece = pl.BlockSpec((1, 4, 16, 1024), lambda i, w: (i, 0, 0, 0))
    whole = lambda shape: pl.BlockSpec(shape, lambda i, w: (0, 0))
    return pl.pallas_call(
        trail_kernel,
        out_shape=jax.ShapeDtypeStruct((8, 16, 64, 128), BF16),
        grid_spec=pltpu.PrefetchScalarGridSpec(
            num_scalar_prefetch=1,
            grid=(4,),
            in_specs=[piece] * 8
            + [
                whole(atoms.shape),
                whole(grads.shape),
                whole(mean.shape),
                whole(order.shape),
            ],
            out_specs=pl.BlockSpec((8, 4, 64, 128), lambda i, w: (0, (w[0] - i) & 3, 0, 0)),
            scratch_shapes=[pltpu.VMEM((512, 1024), BF16)],
        ),
        compiler_params=params(),
        cost_estimate=pl.CostEstimate(
            flops=2 * 2048 * 1024 * 1088, bytes_accessed=9 << 20, transcendentals=0
        ),
    )(where, *own, *other, atoms, grads, mean, order)


def eliminate(a):
    lanes = lax.broadcasted_iota(jnp.int32, (8, 128), 1)
    subs = lax.broadcasted_iota(jnp.int32, (8, 128), 0)
    left = [a[8 * g : 8 * g + 8] for g in range(16)]
    right = [(lanes == subs + 8 * g).astype(F32) for g in range(16)]
    done = []
    for p in range(16):
        count = 16 - p
        cols = [
            [
                jnp.broadcast_to(left[g][:, 8 * p + q : 8 * p + q + 1], (8, 128))
                for g in range(count)
            ]
            for q in range(8)
        ]
        pivots = jnp.ones((8, 128), F32)
        for q in range(8):
            pivot = cols[q][0][q : q + 1]
            inverse = 1.0 / pivot
            pivots = jnp.where(subs == q, pivot, pivots)
            ratio = [c * inverse for c in cols[q]]
            ratio[0] = jnp.where(subs > q, ratio[0], 0.0)
            for t in range(q + 1, 8):
                here = cols[t][0][q : q + 1]
                for g in range(count):
                    cols[t][g] = cols[t][g] - ratio[g] * here
            row_left = left[0][q : q + 1]
            row_right = right[0][q : q + 1]
            for g in range(count):
                left[g] = left[g] - ratio[g] * row_left
                right[g] = right[g] - ratio[g] * row_right
        done.append(right[0] * lax.rsqrt(pivots))
        left, right = left[1:], right[1:]
    return jnp.concatenate(done, axis=0)


def factor_kernel(rows_total, gram_ref, factor_ref, inverse_ref, work):
    n = factor_ref.shape[0]
    r = lax.broadcasted_iota(jnp.int32, (n, n), 0)
    c = lax.broadcasted_iota(jnp.int32, (n, n), 1)
    same = r[:128, :128] == c[:128, :128]
    work[:, :n] = jnp.zeros((n, n), F32)
    for m, (i, j) in enumerate(UPPER):
        block = gram_ref[128 * m : 128 * m + 128] / rows_total
        if i == j:
            block = block + jnp.where(same, ridge_value, 0.0)
        work[128 * i : 128 * i + 128, 128 * j : 128 * j + 128] = block
    work[:, n:] = jnp.where(r == c, 1.0, 0.0)

    def step(b, carry):
        at = pl.multiple_of(b * 128, 128)
        low = eliminate(work[pl.ds(at, 128), pl.ds(at, 128)])
        row = dot(low, work[pl.ds(at, 128), :], NN, HIGHEST)
        lane = lax.broadcasted_iota(jnp.int32, (128, n), 1)
        later = jnp.where(lane >= at + 128, row[:, :n], 0.0)
        work[...] = work[...] - dot(later, row, TN, HIGHEST)
        work[pl.ds(at, 128), :] = row
        return carry

    lax.fori_loop(0, n // 128, step, 0)
    factor_ref[...] = jnp.where(c >= r, work[:, :n], 0.0)
    inverse_ref[...] = jnp.where(c <= r, work[:, n:], 0.0)


def factor_panel(gram, rows_total):
    n = 512
    return pl.pallas_call(
        functools.partial(factor_kernel, float(rows_total)),
        out_shape=(jax.ShapeDtypeStruct((n, n), F32), jax.ShapeDtypeStruct((n, n), F32)),
        scratch_shapes=[pltpu.VMEM((n, 2 * n), F32)],
        compiler_params=params(),
        cost_estimate=pl.CostEstimate(
            flops=20 * n * n * n, bytes_accessed=4 << 20, transcendentals=n
        ),
    )(gram)


def cross_kernel(panel_ref, trail_ref, out_ref):
    @pl.when(pl.program_id(0) == 0)
    def _():
        out_ref[...] = jnp.zeros_like(out_ref)

    n = panel_ref.shape[2]
    trail = jnp.concatenate(
        [trail_ref[:, i].reshape(512, 128) for i in range(panel_ref.shape[0])], axis=0
    )
    out_ref[...] += dot(trail, panel_ref[...].reshape(-1, n), TN)


def cross_part(segment, trail):
    n = segment.shape[2]
    return pl.pallas_call(
        cross_kernel,
        out_shape=jax.ShapeDtypeStruct((128, n), F32),
        grid=(segment.shape[0] // 4,),
        in_specs=[
            pl.BlockSpec((4, 512, n), lambda i: (i, 0, 0)),
            pl.BlockSpec((8, 4, 64, 128), lambda i: (0, i, 0, 0)),
        ],
        out_specs=pl.BlockSpec((128, n), lambda i: (0, 0)),
        compiler_params=params(),
        cost_estimate=pl.CostEstimate(
            flops=2 * 128 * n * 8192, bytes_accessed=11 << 20, transcendentals=0
        ),
    )(segment, trail)


def residual_kernel(
    rows_total, cross_ref, inverse_ref, panel_ref, trail_ref, coupling_ref, out_ref, weights
):
    @pl.when(pl.program_id(0) == 0)
    def _():
        coupling = dot(cross_ref[...] / rows_total, inverse_ref[...], NT, HIGHEST)
        coupling_ref[...] = coupling
        solved = dot(coupling, inverse_ref[...], NN, HIGHEST)
        high = solved.astype(BF16)
        weights[:128] = high
        weights[128:] = (solved - high.astype(F32)).astype(BF16)

    r = lax.broadcasted_iota(jnp.int32, (128, 128), 0)
    c = lax.broadcasted_iota(jnp.int32, (128, 128), 1)
    same = (r == c).astype(BF16)
    for i in range(panel_ref.shape[0]):
        both = dot(weights[...], panel_ref[i], NT)
        own = dot(same, trail_ref[:, i].reshape(512, 128), NT)
        out_ref[:, i * 512 : i * 512 + 512] = own - both[:128] - both[128:]


def residual(cross, inverse, segment, trail, rows_total):
    n = inverse.shape[0]
    chunks = segment.shape[0]
    whole = lambda shape: pl.BlockSpec(shape, lambda i: (0, 0))
    return pl.pallas_call(
        functools.partial(residual_kernel, float(rows_total)),
        out_shape=(
            jax.ShapeDtypeStruct((128, n), F32),
            jax.ShapeDtypeStruct((128, 512 * chunks), F32),
        ),
        grid=(chunks // 4,),
        in_specs=[
            whole((128, n)),
            whole((n, n)),
            pl.BlockSpec((4, 512, n), lambda i: (i, 0, 0)),
            pl.BlockSpec((8, 4, 64, 128), lambda i: (0, i, 0, 0)),
        ],
        out_specs=(whole((128, n)), pl.BlockSpec((128, 2048), lambda i: (0, i))),
        scratch_shapes=[pltpu.VMEM((256, n), BF16)],
        compiler_params=params(),
        cost_estimate=pl.CostEstimate(
            flops=4 * 128 * n * 8192, bytes_accessed=16 << 20, transcendentals=0
        ),
    )(cross, inverse, segment, trail)


def sum_all(v, core, y):
    v = scatter4(swap_add(v, core), "row", y_shift, y)
    v = spread4(spread4(v, "col", z_shift), "col", x_shift)
    v = gather4(v, "row", y_shift, y)
    return jnp.concatenate(swap_gather(v, core), axis=0)


def sum_row(v, core):
    v = spread4(swap_add(v, core), "row", y_shift)
    return jnp.concatenate(swap_gather(v, core), axis=0)


def per_device(
    descriptors, gradients, sparse_panel, sparse_trail, atom_counts, owner_rows, neighbor_ids
):
    row = lax.axis_index("row")
    col = lax.axis_index("col")
    core, y = row % 2, row // 2
    x, z = col // 4, col % 4
    rows_total = 65536

    where = jnp.stack([x, z, y, core]).astype(jnp.int32)

    piece = jnp.concatenate(
        [
            lax.dynamic_slice_in_dim(sparse_panel, core * 16, 16, 0),
            lax.dynamic_slice_in_dim(sparse_trail, row * 16, 16, 0),
        ],
        axis=0,
    )
    piece = jnp.stack(shifted(piece, "col", z_shift))
    pieces = shifted(piece, "col", x_shift)
    own = jnp.stack([p[:, :16] for p in pieces])
    other = lax.ppermute(own, "row", CORE_SWAP)
    own_trail = jnp.stack([p[:, 16:] for p in pieces])

    atoms, grads, mean, order = prepare(
        atom_counts,
        owner_rows,
        neighbor_ids.reshape(128, 4).T,
        descriptors,
        gradients.reshape(12, 128, 1024),
    )

    near, far, gram = panel_rows(where, own, other, atoms, grads, mean, order)
    far = lax.ppermute(far, "row", CORE_SWAP)
    got = [
        lax.ppermute(jnp.stack([near[s], far[s]]), "row", y_shift(s)) for s in (1, 2, 3)
    ]
    panel = assemble(where, near, far, got).reshape(512, 512)
    segment = lax.all_gather(panel, "col", axis=0, tiled=False)
    gram = sum_all(gram, core, y)

    trail_own = shifted(own_trail, "row", y_shift)
    trail_other = [lax.ppermute(p, "row", CORE_SWAP) for p in trail_own]
    trail = trail_rows(where, trail_own, trail_other, atoms, grads, mean, order)
    trail, gram = lax.optimization_barrier((trail, gram))
    trail = lax.all_to_all(
        trail.reshape(128, 64, 128), ("row", "col"), 0, 0, tiled=True
    ).reshape(8, 16, 64, 128)
    factor, inverse = factor_panel(gram, rows_total)

    segment, inverse = lax.optimization_barrier((segment, inverse))
    cross = sum_row(cross_part(segment, trail), core)
    coupling, result = residual(cross, inverse, segment, trail, rows_total)
    return factor, coupling, result


def solution(mesh):
    return jax.shard_map(
        per_device,
        mesh=mesh,
        in_specs=(
            P(("row", "col"), None),
            P(None, None, ("row", "col"), None),
            P("col", None),
            P("col", None),
            P(("row", "col"), None),
            P(("row", "col"), None),
            P(("row", "col"), None, None),
        ),
        out_specs=(P(), P("col", None), P("col", "row")),
        check_vma=False,
    )
```

```python
import functools

import jax
import jax.numpy as jnp
from jax import lax
from jax.experimental import pallas as pl
from jax.experimental.pallas import tpu as pltpu
from jax.sharding import PartitionSpec as P

ridge_value = 0.1
HIGHEST = lax.Precision.HIGHEST
F32 = jnp.float32
BF16 = jnp.bfloat16
NT = (((1,), (1,)), ((), ()))
NN = (((1,), (0,)), ((), ()))
TN = (((0,), (0,)), ((), ()))

CORE_SWAP = [(i, i ^ 1) for i in range(8)]


def y_shift(s):
    return [(2 * y + c, 2 * ((y + s) % 4) + c) for y in range(4) for c in range(2)]


def z_shift(s):
    return [(x * 4 + z, x * 4 + (z + s) % 4) for x in range(4) for z in range(4)]


def x_shift(s):
    return [(x * 4 + z, ((x + s) % 4) * 4 + z) for x in range(4) for z in range(4)]


UPPER = [(i, j) for i in range(4) for j in range(i, 4)]


def dot(a, b, dims, precision=None):
    return lax.dot_general(a, b, dims, precision=precision, preferred_element_type=F32)


def in_order(pieces, index):
    return jnp.concatenate(
        [lax.select_n((index - j) % 4, *pieces) for j in range(4)], axis=0
    )


def shifted(v, axis, shift):
    return [v] + [lax.ppermute(v, axis, shift(s)) for s in (1, 2, 3)]


def gather4(v, axis, shift, index):
    pieces = [v] + [lax.ppermute(v, axis, shift(s)) for s in (1, 2, 3)]
    return in_order(pieces, index)


def scatter4(v, axis, shift, index):
    n = v.shape[0] // 4
    total = lax.dynamic_slice_in_dim(v, index * n, n, 0)
    got = [
        lax.ppermute(
            lax.dynamic_slice_in_dim(v, ((index + s) % 4) * n, n, 0), axis, shift(s)
        )
        for s in (1, 2, 3)
    ]
    return total + got[0] + got[1] + got[2]


def swap_add(v, core):
    n = v.shape[0] // 2
    mine = lax.dynamic_slice_in_dim(v, core * n, n, 0)
    other = lax.dynamic_slice_in_dim(v, (1 - core) * n, n, 0)
    return mine + lax.ppermute(other, "row", CORE_SWAP)


def swap_gather(v, core):
    other = lax.ppermute(v, "row", CORE_SWAP)
    first = core == 0
    return jnp.where(first, v, other), jnp.where(first, other, v)


def spread4(v, axis, shift):
    got = [lax.ppermute(v, axis, shift(s)) for s in (1, 2, 3)]
    return v + got[0] + got[1] + got[2]


def prep_kernel(
    count_ref, owner_ref, neighbor_ref, desc_ref, grad_ref, atoms_ref, grads_ref, mean_ref, order_ref
):
    counts = [count_ref[0, s] for s in range(8)]
    owners = [owner_ref[0, s] for s in range(8)]
    offsets = [jnp.int32(0)]
    for s in range(7):
        offsets.append(offsets[s] + counts[s])

    lane = lax.broadcasted_iota(jnp.int32, (8, 128), 1)
    struct, atom = lane >> 4, lane & 15
    count_l, offset_l = jnp.ones((8, 128), jnp.int32), jnp.zeros((8, 128), jnp.int32)
    for s in range(8):
        count_l = jnp.where(struct == s, counts[s], count_l)
        offset_l = jnp.where(struct == s, offsets[s], offset_l)
    place = jnp.where(atom < count_l, offset_l + atom, -1)
    rows = lax.broadcasted_iota(jnp.int32, (64, 128), 0)
    lanes = lax.broadcasted_iota(jnp.int32, (64, 128), 1)
    live = place[:1] == rows
    live_f = live.astype(F32)

    value = neighbor_ref[...].astype(F32)
    size = count_l.astype(F32)[:4]
    rest = value - size * jnp.floor(value / size)
    rest = jnp.where(rest < 0.0, rest + size, rest)
    rest = jnp.where(rest >= size, rest - size, rest)
    partner = rest + (16 * struct).astype(F32)[:4]

    picks = [live_f.astype(BF16)]
    for j in range(4):
        slot = jnp.sum(live_f * partner[j : j + 1], axis=1, keepdims=True)
        picks.append((slot == lanes.astype(F32)).astype(F32).astype(BF16))
    desc = desc_ref[...]
    for j in range(5):
        atoms_ref[64 * j : 64 * j + 64] = dot(picks[j], desc, NN).astype(BF16)
    for i in range(12):
        grads_ref[64 * i : 64 * i + 64] = dot(picks[0], grad_ref[i], NN).astype(BF16)

    sub8 = lax.broadcasted_iota(jnp.int32, (8, 64), 0)
    atom8 = lax.broadcasted_iota(jnp.int32, (8, 64), 1)
    low, size8 = jnp.zeros((8, 64), jnp.int32), jnp.ones((8, 64), jnp.int32)
    for s in range(8):
        low = jnp.where(sub8 == s, offsets[s], low)
        size8 = jnp.where(sub8 == s, counts[s], size8)
    inside = (atom8 >= low) & (atom8 < low + size8)
    mean_ref[...] = jnp.where(inside, 1.0 / size8.astype(F32), 0.0)

    r = lax.broadcasted_iota(jnp.int32, (64, 256), 0)
    wanted = lax.broadcasted_iota(jnp.int32, (64, 256), 1)
    third = ((r - 1) * 43) >> 7
    part = (r - 1) - 3 * third
    for g in range(8):
        struct_g, count_g, offset_g = jnp.int32(0), jnp.int32(0), jnp.int32(0)
        for s in range(8):
            mine = owners[s] == g
            struct_g = jnp.where(mine, s, struct_g)
            count_g = jnp.where(mine, counts[s], count_g)
            offset_g = jnp.where(mine, offsets[s], offset_g)
        column = jnp.where(third < count_g, part * 64 + offset_g + third, -1)
        column = jnp.where(r == 0, 192 + struct_g, column)
        order_ref[64 * g : 64 * g + 64] = (column == wanted).astype(F32).astype(BF16)


def prepare(count, owner, neighbors, descriptors, gradients):
    smem = pl.BlockSpec(memory_space=pltpu.SMEM)
    vmem = pl.BlockSpec(memory_space=pltpu.VMEM)
    return pl.pallas_call(
        prep_kernel,
        out_shape=(
            jax.ShapeDtypeStruct((320, 1024), BF16),
            jax.ShapeDtypeStruct((768, 1024), BF16),
            jax.ShapeDtypeStruct((8, 64), F32),
            jax.ShapeDtypeStruct((512, 256), BF16),
        ),
        in_specs=[smem, smem, vmem, vmem, vmem],
        out_specs=(vmem, vmem, vmem, vmem),
        compiler_params=params(),
        cost_estimate=pl.CostEstimate(
            flops=2 * 64 * 128 * 1024 * 17, bytes_accessed=6 << 20, transcendentals=0
        ),
    )(count, owner, neighbors, descriptors, gradients)


def compact_rows(env, atoms, grads, mean):
    near = dot(atoms, env, NT)
    slope = dot(grads, env, NT)
    inner = near[:64]
    parts = []
    for k in range(3):
        total = near[64:128] * slope[k * 256 : k * 256 + 64]
        for j in range(1, 4):
            total = total + near[64 + j * 64 : 128 + j * 64] * slope[
                k * 256 + j * 64 : k * 256 + j * 64 + 64
            ]
        parts.append((-2.0 * total).astype(BF16))
    energy = dot(mean, inner * inner, NN, HIGHEST)
    pad = jnp.zeros((56, env.shape[0]), F32)
    parts.append(jnp.concatenate([energy, pad], axis=0).astype(BF16))
    return jnp.concatenate(parts, axis=0)


def put_env(env, where, own, other, block, at):
    core = where[3]
    env[pl.ds(pl.multiple_of(at + core * 16, 16), 16)] = own[block]
    env[pl.ds(pl.multiple_of(at + (1 - core) * 16, 16), 16)] = other[block]


def panel_kernel(
    where, own, other, atoms_ref, grads_ref, mean_ref, order_ref, near_ref, far_ref, gram_ref, env
):
    x, z, y, core = where[0], where[1], where[2], where[3]
    for i in range(4):
        for j in range(4):
            place = ((x - i) & 3) * 4 + ((z - j) & 3)
            put_env(env, where, own, other, (i, j), place * 32)
    rows = compact_rows(env[...], atoms_ref[...], grads_ref[...], mean_ref[...])
    full = dot(order_ref[...], rows, NN).astype(BF16)
    first = core == 0
    for i in range(4):
        low, high = full[128 * i : 128 * i + 64], full[128 * i + 64 : 128 * i + 128]
        s = (i - y) & 3
        near_ref[s] = jnp.where(first, low, high)
        far_ref[s] = jnp.where(first, high, low)
    gram = dot(rows, rows, TN)
    for n, (i, j) in enumerate(UPPER):
        gram_ref[128 * n : 128 * n + 128] = gram[
            128 * i : 128 * i + 128, 128 * j : 128 * j + 128
        ]


def trail_kernel(
    where, own, other, atoms_ref, grads_ref, mean_ref, order_ref, out_ref, env
):
    z, y = where[1], where[2]
    for j in range(4):
        place = ((z - j) & 3) * 128
        for s in range(4):
            put_env(env, where, own, other, (s, 0, j), place + ((y - s) & 3) * 32)
    rows = compact_rows(env[...], atoms_ref[...], grads_ref[...], mean_ref[...])
    full = dot(order_ref[...], rows, NN).astype(BF16)
    for c in range(out_ref.shape[1]):
        out_ref[:, c] = full[:, c * 128 : c * 128 + 128].reshape(8, 64, 128)


def assemble_kernel(where, near, far, got1, got2, got3, out):
    y, core = where[2], where[3]
    out[2 * y + core] = near[0]
    out[2 * y + 1 - core] = far[0]
    for s, got in ((1, got1), (2, got2), (3, got3)):
        at = 2 * ((y - s) & 3)
        out[at + core] = got[0]
        out[at + 1 - core] = got[1]


def params(mib=40):
    return pltpu.CompilerParams(vmem_limit_bytes=mib << 20)


def in_smem():
    return pl.BlockSpec(memory_space=pltpu.SMEM)


def in_vmem():
    return pl.BlockSpec(memory_space=pltpu.VMEM)


def panel_rows(where, own, other, atoms, grads, mean, order):
    return pl.pallas_call(
        panel_kernel,
        out_shape=(
            jax.ShapeDtypeStruct((4, 64, 512), BF16),
            jax.ShapeDtypeStruct((4, 64, 512), BF16),
            jax.ShapeDtypeStruct((1280, 128), F32),
        ),
        in_specs=[in_smem()] + [in_vmem()] * 6,
        out_specs=(in_vmem(),) * 3,
        scratch_shapes=[pltpu.VMEM((512, 1024), BF16)],
        compiler_params=params(),
        cost_estimate=pl.CostEstimate(
            flops=2 * 512 * 1024 * 1088, bytes_accessed=5 << 20, transcendentals=0
        ),
    )(where, own, other, atoms, grads, mean, order)


def assemble(where, near, far, got):
    return pl.pallas_call(
        assemble_kernel,
        out_shape=jax.ShapeDtypeStruct((8, 64, 512), BF16),
        in_specs=[in_smem()] + [in_vmem()] * 5,
        out_specs=in_vmem(),
        compiler_params=params(),
        cost_estimate=pl.CostEstimate(flops=0, bytes_accessed=1 << 20, transcendentals=0),
    )(where, near, far, *got)


def trail_rows(where, own, other, atoms, grads, mean, order):
    piece = pl.BlockSpec((4, 1, 4, 16, 1024), lambda i, w: (0, i, 0, 0, 0))
    whole = lambda shape: pl.BlockSpec(shape, lambda i, w: (0, 0))
    return pl.pallas_call(
        trail_kernel,
        out_shape=jax.ShapeDtypeStruct((8, 16, 64, 128), BF16),
        grid_spec=pltpu.PrefetchScalarGridSpec(
            num_scalar_prefetch=1,
            grid=(4,),
            in_specs=[piece] * 2
            + [
                whole(atoms.shape),
                whole(grads.shape),
                whole(mean.shape),
                whole(order.shape),
            ],
            out_specs=pl.BlockSpec((8, 4, 64, 128), lambda i, w: (0, (w[0] - i) & 3, 0, 0)),
            scratch_shapes=[pltpu.VMEM((512, 1024), BF16)],
        ),
        compiler_params=params(),
        cost_estimate=pl.CostEstimate(
            flops=2 * 2048 * 1024 * 1088, bytes_accessed=9 << 20, transcendentals=0
        ),
    )(where, own, other, atoms, grads, mean, order)


def eliminate(a):
    lanes = lax.broadcasted_iota(jnp.int32, (8, 128), 1)
    subs = lax.broadcasted_iota(jnp.int32, (8, 128), 0)
    left = [a[8 * g : 8 * g + 8] for g in range(16)]
    right = [(lanes == subs + 8 * g).astype(F32) for g in range(16)]
    done = []
    for p in range(16):
        count = 16 - p
        cols = [
            [
                jnp.broadcast_to(left[g][:, 8 * p + q : 8 * p + q + 1], (8, 128))
                for g in range(count)
            ]
            for q in range(8)
        ]
        pivots = jnp.ones((8, 128), F32)
        for q in range(8):
            pivot = cols[q][0][q : q + 1]
            inverse = 1.0 / pivot
            pivots = jnp.where(subs == q, pivot, pivots)
            ratio = [c * inverse for c in cols[q]]
            ratio[0] = jnp.where(subs > q, ratio[0], 0.0)
            for t in range(q + 1, 8):
                here = cols[t][0][q : q + 1]
                for g in range(count):
                    cols[t][g] = cols[t][g] - ratio[g] * here
            row_left = left[0][q : q + 1]
            row_right = right[0][q : q + 1]
            for g in range(count):
                left[g] = left[g] - ratio[g] * row_left
                right[g] = right[g] - ratio[g] * row_right
        done.append(right[0] * lax.rsqrt(pivots))
        left, right = left[1:], right[1:]
    return jnp.concatenate(done, axis=0)


def factor_kernel(rows_total, gram_ref, factor_ref, inverse_ref, work):
    n = factor_ref.shape[0]
    r = lax.broadcasted_iota(jnp.int32, (n, n), 0)
    c = lax.broadcasted_iota(jnp.int32, (n, n), 1)
    same = r[:128, :128] == c[:128, :128]
    work[:, :n] = jnp.zeros((n, n), F32)
    for m, (i, j) in enumerate(UPPER):
        block = gram_ref[128 * m : 128 * m + 128] / rows_total
        if i == j:
            block = block + jnp.where(same, ridge_value, 0.0)
        work[128 * i : 128 * i + 128, 128 * j : 128 * j + 128] = block
    work[:, n:] = jnp.where(r == c, 1.0, 0.0)

    def step(b, carry):
        at = pl.multiple_of(b * 128, 128)
        low = eliminate(work[pl.ds(at, 128), pl.ds(at, 128)])
        row = dot(low, work[pl.ds(at, 128), :], NN, HIGHEST)
        lane = lax.broadcasted_iota(jnp.int32, (128, n), 1)
        later = jnp.where(lane >= at + 128, row[:, :n], 0.0)
        work[...] = work[...] - dot(later, row, TN, HIGHEST)
        work[pl.ds(at, 128), :] = row
        return carry

    lax.fori_loop(0, n // 128, step, 0)
    factor_ref[...] = jnp.where(c >= r, work[:, :n], 0.0)
    inverse_ref[...] = jnp.where(c <= r, work[:, n:], 0.0)


def factor_panel(gram, rows_total):
    n = 512
    return pl.pallas_call(
        functools.partial(factor_kernel, float(rows_total)),
        out_shape=(jax.ShapeDtypeStruct((n, n), F32), jax.ShapeDtypeStruct((n, n), F32)),
        scratch_shapes=[pltpu.VMEM((n, 2 * n), F32)],
        compiler_params=params(),
        cost_estimate=pl.CostEstimate(
            flops=20 * n * n * n, bytes_accessed=4 << 20, transcendentals=n
        ),
    )(gram)


def cross_kernel(panel_ref, trail_ref, out_ref):
    @pl.when(pl.program_id(0) == 0)
    def _():
        out_ref[...] = jnp.zeros_like(out_ref)

    n = panel_ref.shape[2]
    trail = jnp.concatenate(
        [trail_ref[:, i].reshape(512, 128) for i in range(panel_ref.shape[0])], axis=0
    )
    out_ref[...] += dot(trail, panel_ref[...].reshape(-1, n), TN)


def cross_part(segment, trail):
    n = segment.shape[2]
    return pl.pallas_call(
        cross_kernel,
        out_shape=jax.ShapeDtypeStruct((128, n), F32),
        grid=(segment.shape[0] // 4,),
        in_specs=[
            pl.BlockSpec((4, 512, n), lambda i: (i, 0, 0)),
            pl.BlockSpec((8, 4, 64, 128), lambda i: (0, i, 0, 0)),
        ],
        out_specs=pl.BlockSpec((128, n), lambda i: (0, 0)),
        compiler_params=params(58),
        cost_estimate=pl.CostEstimate(
            flops=2 * 128 * n * 8192, bytes_accessed=11 << 20, transcendentals=0
        ),
    )(segment, trail)


def residual_kernel(
    rows_total, cross_ref, inverse_ref, panel_ref, trail_ref, coupling_ref, out_ref, weights
):
    @pl.when(pl.program_id(0) == 0)
    def _():
        coupling = dot(cross_ref[...] / rows_total, inverse_ref[...], NT, HIGHEST)
        coupling_ref[...] = coupling
        solved = dot(coupling, inverse_ref[...], NN, HIGHEST)
        high = solved.astype(BF16)
        weights[:128] = high
        weights[128:] = (solved - high.astype(F32)).astype(BF16)

    r = lax.broadcasted_iota(jnp.int32, (128, 128), 0)
    c = lax.broadcasted_iota(jnp.int32, (128, 128), 1)
    same = (r == c).astype(BF16)
    for i in range(panel_ref.shape[0]):
        both = dot(weights[...], panel_ref[i], NT)
        own = dot(same, trail_ref[:, i].reshape(512, 128), NT)
        out_ref[:, i * 512 : i * 512 + 512] = own - both[:128] - both[128:]


def residual(cross, inverse, segment, trail, rows_total):
    n = inverse.shape[0]
    chunks = segment.shape[0]
    whole = lambda shape: pl.BlockSpec(shape, lambda i: (0, 0))
    return pl.pallas_call(
        functools.partial(residual_kernel, float(rows_total)),
        out_shape=(
            jax.ShapeDtypeStruct((128, n), F32),
            jax.ShapeDtypeStruct((128, 512 * chunks), F32),
        ),
        grid=(chunks // 4,),
        in_specs=[
            whole((128, n)),
            whole((n, n)),
            pl.BlockSpec((4, 512, n), lambda i: (i, 0, 0)),
            pl.BlockSpec((8, 4, 64, 128), lambda i: (0, i, 0, 0)),
        ],
        out_specs=(whole((128, n)), pl.BlockSpec((128, 2048), lambda i: (0, i))),
        scratch_shapes=[pltpu.VMEM((256, n), BF16)],
        compiler_params=params(58),
        cost_estimate=pl.CostEstimate(
            flops=4 * 128 * n * 8192, bytes_accessed=16 << 20, transcendentals=0
        ),
    )(cross, inverse, segment, trail)


def sum_row(v, core):
    v = spread4(swap_add(v, core), "row", y_shift)
    return jnp.concatenate(swap_gather(v, core), axis=0)


def per_device(
    descriptors, gradients, sparse_panel, sparse_trail, atom_counts, owner_rows, neighbor_ids
):
    row = lax.axis_index("row")
    col = lax.axis_index("col")
    core, y = row % 2, row // 2
    x, z = col // 4, col % 4
    rows_total = 65536

    where = jnp.stack([x, z, y, core]).astype(jnp.int32)

    piece = jnp.concatenate(
        [
            lax.dynamic_slice_in_dim(sparse_panel, core * 16, 16, 0),
            lax.dynamic_slice_in_dim(sparse_trail, row * 16, 16, 0),
        ],
        axis=0,
    )
    pieces = shifted(piece, "col", z_shift)
    piece = jnp.stack([p[:16] for p in pieces])
    piece_trail = jnp.stack([p[16:] for p in pieces])
    own = jnp.stack(shifted(piece, "col", x_shift))
    own, piece_trail = lax.optimization_barrier((own, piece_trail))
    other = lax.ppermute(own, "row", CORE_SWAP)
    own_trail = jnp.stack(shifted(piece_trail, "col", x_shift))

    atoms, grads, mean, order = prepare(
        atom_counts,
        owner_rows,
        neighbor_ids.reshape(128, 4).T,
        descriptors,
        gradients.reshape(12, 128, 1024),
    )

    near, far, gram = panel_rows(where, own, other, atoms, grads, mean, order)
    far, own_trail = lax.optimization_barrier((far, own_trail))
    far = lax.ppermute(far, "row", CORE_SWAP)
    got = [
        lax.ppermute(jnp.stack([near[s], far[s]]), "row", y_shift(s)) for s in (1, 2, 3)
    ]
    panel = assemble(where, near, far, got).reshape(512, 512)
    segment = lax.all_gather(panel, "col", axis=0, tiled=False)
    gram = scatter4(swap_add(gram, core), "row", y_shift, y)
    trail_own = jnp.stack(shifted(own_trail, "row", y_shift))
    trail_own, gram = lax.optimization_barrier((trail_own, gram))
    trail_other = lax.ppermute(trail_own, "row", CORE_SWAP)
    gram = spread4(gram, "col", z_shift)
    trail_other, gram = lax.optimization_barrier((trail_other, gram))
    gram = spread4(gram, "col", x_shift)
    trail = trail_rows(where, trail_own, trail_other, atoms, grads, mean, order)
    trail, gram = lax.optimization_barrier((trail, gram))
    gram = gather4(gram, "row", y_shift, y)
    gram = jnp.concatenate(swap_gather(gram, core), axis=0)
    trail = lax.all_to_all(
        trail.reshape(128, 64, 128), ("row", "col"), 0, 0, tiled=True
    ).reshape(8, 16, 64, 128)
    factor, inverse = factor_panel(gram, rows_total)

    segment, inverse = lax.optimization_barrier((segment, inverse))
    cross = sum_row(cross_part(segment, trail), core)
    coupling, result = residual(cross, inverse, segment, trail, rows_total)
    return factor, coupling, result


def solution(mesh):
    return jax.shard_map(
        per_device,
        mesh=mesh,
        in_specs=(
            P(("row", "col"), None),
            P(None, None, ("row", "col"), None),
            P("col", None),
            P("col", None),
            P(("row", "col"), None),
            P(("row", "col"), None),
            P(("row", "col"), None, None),
        ),
        out_specs=(P(), P("col", None), P("col", "row")),
        check_vma=False,
    )
```

```python
import functools

import jax
import jax.numpy as jnp
from jax import lax
from jax.experimental import pallas as pl
from jax.experimental.pallas import tpu as pltpu
from jax.sharding import PartitionSpec as P

ridge_value = 0.1
HIGHEST = lax.Precision.HIGHEST
F32 = jnp.float32
BF16 = jnp.bfloat16
NT = (((1,), (1,)), ((), ()))
NN = (((1,), (0,)), ((), ()))
TN = (((0,), (0,)), ((), ()))

CORE_SWAP = [(i, i ^ 1) for i in range(8)]


def y_shift(s):
    return [(2 * y + c, 2 * ((y + s) % 4) + c) for y in range(4) for c in range(2)]


def z_shift(s):
    return [(x * 4 + z, x * 4 + (z + s) % 4) for x in range(4) for z in range(4)]


def x_shift(s):
    return [(x * 4 + z, ((x + s) % 4) * 4 + z) for x in range(4) for z in range(4)]


UPPER = [(i, j) for i in range(4) for j in range(i, 4)]


def dot(a, b, dims, precision=None):
    return lax.dot_general(a, b, dims, precision=precision, preferred_element_type=F32)


def in_order(pieces, index):
    return jnp.concatenate(
        [lax.select_n((index - j) % 4, *pieces) for j in range(4)], axis=0
    )


def shifted(v, axis, shift):
    return [v] + [lax.ppermute(v, axis, shift(s)) for s in (1, 2, 3)]


def gather4(v, axis, shift, index):
    pieces = [v] + [lax.ppermute(v, axis, shift(s)) for s in (1, 2, 3)]
    return in_order(pieces, index)


def scatter4(v, axis, shift, index):
    n = v.shape[0] // 4
    total = lax.dynamic_slice_in_dim(v, index * n, n, 0)
    got = [
        lax.ppermute(
            lax.dynamic_slice_in_dim(v, ((index + s) % 4) * n, n, 0), axis, shift(s)
        )
        for s in (1, 2, 3)
    ]
    return total + got[0] + got[1] + got[2]


def swap_add(v, core):
    n = v.shape[0] // 2
    mine = lax.dynamic_slice_in_dim(v, core * n, n, 0)
    other = lax.dynamic_slice_in_dim(v, (1 - core) * n, n, 0)
    return mine + lax.ppermute(other, "row", CORE_SWAP)


def swap_gather(v, core):
    other = lax.ppermute(v, "row", CORE_SWAP)
    first = core == 0
    return jnp.where(first, v, other), jnp.where(first, other, v)


def spread4(v, axis, shift):
    got = [lax.ppermute(v, axis, shift(s)) for s in (1, 2, 3)]
    return v + got[0] + got[1] + got[2]


def prep_kernel(
    count_ref, owner_ref, neighbor_ref, desc_ref, grad_ref, atoms_ref, grads_ref, mean_ref, order_ref
):
    counts = [count_ref[0, s] for s in range(8)]
    owners = [owner_ref[0, s] for s in range(8)]
    offsets = [jnp.int32(0)]
    for s in range(7):
        offsets.append(offsets[s] + counts[s])

    lane = lax.broadcasted_iota(jnp.int32, (8, 128), 1)
    struct, atom = lane >> 4, lane & 15
    count_l, offset_l = jnp.ones((8, 128), jnp.int32), jnp.zeros((8, 128), jnp.int32)
    for s in range(8):
        count_l = jnp.where(struct == s, counts[s], count_l)
        offset_l = jnp.where(struct == s, offsets[s], offset_l)
    place = jnp.where(atom < count_l, offset_l + atom, -1)
    rows = lax.broadcasted_iota(jnp.int32, (64, 128), 0)
    lanes = lax.broadcasted_iota(jnp.int32, (64, 128), 1)
    live = place[:1] == rows
    live_f = live.astype(F32)

    value = neighbor_ref[...].astype(F32)
    size = count_l.astype(F32)[:4]
    rest = value - size * jnp.floor(value / size)
    rest = jnp.where(rest < 0.0, rest + size, rest)
    rest = jnp.where(rest >= size, rest - size, rest)
    partner = rest + (16 * struct).astype(F32)[:4]

    picks = [live_f.astype(BF16)]
    for j in range(4):
        slot = jnp.sum(live_f * partner[j : j + 1], axis=1, keepdims=True)
        picks.append((slot == lanes.astype(F32)).astype(F32).astype(BF16))
    desc = desc_ref[...]
    for j in range(5):
        atoms_ref[64 * j : 64 * j + 64] = dot(picks[j], desc, NN).astype(BF16)
    for i in range(12):
        grads_ref[64 * i : 64 * i + 64] = dot(picks[0], grad_ref[i], NN).astype(BF16)

    sub8 = lax.broadcasted_iota(jnp.int32, (8, 64), 0)
    atom8 = lax.broadcasted_iota(jnp.int32, (8, 64), 1)
    low, size8 = jnp.zeros((8, 64), jnp.int32), jnp.ones((8, 64), jnp.int32)
    for s in range(8):
        low = jnp.where(sub8 == s, offsets[s], low)
        size8 = jnp.where(sub8 == s, counts[s], size8)
    inside = (atom8 >= low) & (atom8 < low + size8)
    mean_ref[...] = jnp.where(inside, 1.0 / size8.astype(F32), 0.0)

    r = lax.broadcasted_iota(jnp.int32, (64, 256), 0)
    wanted = lax.broadcasted_iota(jnp.int32, (64, 256), 1)
    third = ((r - 1) * 43) >> 7
    part = (r - 1) - 3 * third
    for g in range(8):
        struct_g, count_g, offset_g = jnp.int32(0), jnp.int32(0), jnp.int32(0)
        for s in range(8):
            mine = owners[s] == g
            struct_g = jnp.where(mine, s, struct_g)
            count_g = jnp.where(mine, counts[s], count_g)
            offset_g = jnp.where(mine, offsets[s], offset_g)
        column = jnp.where(third < count_g, part * 64 + offset_g + third, -1)
        column = jnp.where(r == 0, 192 + struct_g, column)
        order_ref[64 * g : 64 * g + 64] = (column == wanted).astype(F32).astype(BF16)


def prepare(count, owner, neighbors, descriptors, gradients):
    smem = pl.BlockSpec(memory_space=pltpu.SMEM)
    vmem = pl.BlockSpec(memory_space=pltpu.VMEM)
    return pl.pallas_call(
        prep_kernel,
        out_shape=(
            jax.ShapeDtypeStruct((320, 1024), BF16),
            jax.ShapeDtypeStruct((768, 1024), BF16),
            jax.ShapeDtypeStruct((8, 64), F32),
            jax.ShapeDtypeStruct((512, 256), BF16),
        ),
        in_specs=[smem, smem, vmem, vmem, vmem],
        out_specs=(vmem, vmem, vmem, vmem),
        compiler_params=params(),
        cost_estimate=pl.CostEstimate(
            flops=2 * 64 * 128 * 1024 * 17, bytes_accessed=6 << 20, transcendentals=0
        ),
    )(count, owner, neighbors, descriptors, gradients)


def compact_rows(env, atoms, grads, mean):
    near = dot(atoms, env, NT)
    slope = dot(grads, env, NT)
    inner = near[:64]
    parts = []
    for k in range(3):
        total = near[64:128] * slope[k * 256 : k * 256 + 64]
        for j in range(1, 4):
            total = total + near[64 + j * 64 : 128 + j * 64] * slope[
                k * 256 + j * 64 : k * 256 + j * 64 + 64
            ]
        parts.append((-2.0 * total).astype(BF16))
    energy = dot(mean, inner * inner, NN, HIGHEST)
    pad = jnp.zeros((56, env.shape[0]), F32)
    parts.append(jnp.concatenate([energy, pad], axis=0).astype(BF16))
    return jnp.concatenate(parts, axis=0)


def put_env(env, where, own, other, block, at):
    core = where[3]
    env[pl.ds(pl.multiple_of(at + core * 16, 16), 16)] = own[block]
    env[pl.ds(pl.multiple_of(at + (1 - core) * 16, 16), 16)] = other[block]


def panel_kernel(
    where, own, other, atoms_ref, grads_ref, mean_ref, order_ref, near_ref, far_ref, gram_ref, env
):
    x, z, y, core = where[0], where[1], where[2], where[3]
    for i in range(4):
        for j in range(4):
            place = ((x - i) & 3) * 4 + ((z - j) & 3)
            put_env(env, where, own, other, (i, j), place * 32)
    rows = compact_rows(env[...], atoms_ref[...], grads_ref[...], mean_ref[...])
    full = dot(order_ref[...], rows, NN).astype(BF16)
    first = core == 0
    for i in range(4):
        low, high = full[128 * i : 128 * i + 64], full[128 * i + 64 : 128 * i + 128]
        s = (i - y) & 3
        near_ref[s] = jnp.where(first, low, high)
        far_ref[s] = jnp.where(first, high, low)
    gram = dot(rows, rows, TN)
    for n, (i, j) in enumerate(UPPER):
        gram_ref[128 * n : 128 * n + 128] = gram[
            128 * i : 128 * i + 128, 128 * j : 128 * j + 128
        ]


def trail_kernel(
    where, own_ref, other_ref, atoms_ref, grads_ref, mean_ref, order_ref, out_ref
):
    first = where[3] == 0
    own, other = own_ref[...], other_ref[...]
    low, high = jnp.where(first, own, other), jnp.where(first, other, own)
    env = jnp.concatenate([low, high], axis=1).reshape(-1, 1024)
    rows = compact_rows(env, atoms_ref[...], grads_ref[...], mean_ref[...])
    full = dot(order_ref[...], rows, NN).astype(BF16)
    for c in range(out_ref.shape[1]):
        out_ref[:, c] = full[:, c * 128 : c * 128 + 128].reshape(8, 64, 128)


def assemble_kernel(where, near, far, got1, got2, got3, out):
    y, core = where[2], where[3]
    out[2 * y + core] = near[0]
    out[2 * y + 1 - core] = far[0]
    for s, got in ((1, got1), (2, got2), (3, got3)):
        at = 2 * ((y - s) & 3)
        out[at + core] = got[0]
        out[at + 1 - core] = got[1]


def params(mib=40):
    return pltpu.CompilerParams(vmem_limit_bytes=mib << 20)


def in_smem():
    return pl.BlockSpec(memory_space=pltpu.SMEM)


def in_vmem():
    return pl.BlockSpec(memory_space=pltpu.VMEM)


def panel_rows(where, own, other, atoms, grads, mean, order):
    return pl.pallas_call(
        panel_kernel,
        out_shape=(
            jax.ShapeDtypeStruct((4, 64, 512), BF16),
            jax.ShapeDtypeStruct((4, 64, 512), BF16),
            jax.ShapeDtypeStruct((1280, 128), F32),
        ),
        in_specs=[in_smem()] + [in_vmem()] * 6,
        out_specs=(in_vmem(),) * 3,
        scratch_shapes=[pltpu.VMEM((512, 1024), BF16)],
        compiler_params=params(),
        cost_estimate=pl.CostEstimate(
            flops=2 * 512 * 1024 * 1088, bytes_accessed=5 << 20, transcendentals=0
        ),
    )(where, own, other, atoms, grads, mean, order)


def assemble(where, near, far, got):
    return pl.pallas_call(
        assemble_kernel,
        out_shape=jax.ShapeDtypeStruct((8, 64, 512), BF16),
        in_specs=[in_smem()] + [in_vmem()] * 5,
        out_specs=in_vmem(),
        compiler_params=params(),
        cost_estimate=pl.CostEstimate(flops=0, bytes_accessed=1 << 20, transcendentals=0),
    )(where, near, far, *got)


def trail_rows(where, own, other, atoms, grads, mean, order):
    blocks = own.shape[0]
    step = 4
    half = pl.BlockSpec((step, 64, 1024), lambda i, w: (i, 0, 0))
    whole = lambda shape: pl.BlockSpec(shape, lambda i, w: (0, 0))
    return pl.pallas_call(
        trail_kernel,
        out_shape=jax.ShapeDtypeStruct((8, blocks, 64, 128), BF16),
        grid_spec=pltpu.PrefetchScalarGridSpec(
            num_scalar_prefetch=1,
            grid=(blocks // step,),
            in_specs=[
                half,
                half,
                whole(atoms.shape),
                whole(grads.shape),
                whole(mean.shape),
                whole(order.shape),
            ],
            out_specs=pl.BlockSpec((8, step, 64, 128), lambda i, w: (0, i, 0, 0)),
        ),
        compiler_params=params(),
        cost_estimate=pl.CostEstimate(
            flops=2 * 2048 * 1024 * 1088, bytes_accessed=9 << 20, transcendentals=0
        ),
    )(where, own, other, atoms, grads, mean, order)


def eliminate(a):
    lanes = lax.broadcasted_iota(jnp.int32, (8, 128), 1)
    subs = lax.broadcasted_iota(jnp.int32, (8, 128), 0)
    left = [a[8 * g : 8 * g + 8] for g in range(16)]
    right = [(lanes == subs + 8 * g).astype(F32) for g in range(16)]
    done = []
    for p in range(16):
        count = 16 - p
        cols = [
            [
                jnp.broadcast_to(left[g][:, 8 * p + q : 8 * p + q + 1], (8, 128))
                for g in range(count)
            ]
            for q in range(8)
        ]
        pivots = jnp.ones((8, 128), F32)
        for q in range(8):
            pivot = cols[q][0][q : q + 1]
            inverse = 1.0 / pivot
            pivots = jnp.where(subs == q, pivot, pivots)
            ratio = [c * inverse for c in cols[q]]
            ratio[0] = jnp.where(subs > q, ratio[0], 0.0)
            for t in range(q + 1, 8):
                here = cols[t][0][q : q + 1]
                for g in range(count):
                    cols[t][g] = cols[t][g] - ratio[g] * here
            row_left = left[0][q : q + 1]
            row_right = right[0][q : q + 1]
            for g in range(count):
                left[g] = left[g] - ratio[g] * row_left
                right[g] = right[g] - ratio[g] * row_right
        done.append(right[0] * lax.rsqrt(pivots))
        left, right = left[1:], right[1:]
    return jnp.concatenate(done, axis=0)


def factor_kernel(rows_total, gram_ref, factor_ref, inverse_ref, work):
    n = factor_ref.shape[0]
    r = lax.broadcasted_iota(jnp.int32, (n, n), 0)
    c = lax.broadcasted_iota(jnp.int32, (n, n), 1)
    same = r[:128, :128] == c[:128, :128]
    work[:, :n] = jnp.zeros((n, n), F32)
    for m, (i, j) in enumerate(UPPER):
        block = gram_ref[128 * m : 128 * m + 128] / rows_total
        if i == j:
            block = block + jnp.where(same, ridge_value, 0.0)
        work[128 * i : 128 * i + 128, 128 * j : 128 * j + 128] = block
    work[:, n:] = jnp.where(r == c, 1.0, 0.0)

    def step(b, carry):
        at = pl.multiple_of(b * 128, 128)
        low = eliminate(work[pl.ds(at, 128), pl.ds(at, 128)])
        row = dot(low, work[pl.ds(at, 128), :], NN, HIGHEST)
        lane = lax.broadcasted_iota(jnp.int32, (128, n), 1)
        later = jnp.where(lane >= at + 128, row[:, :n], 0.0)
        work[...] = work[...] - dot(later, row, TN, HIGHEST)
        work[pl.ds(at, 128), :] = row
        return carry

    lax.fori_loop(0, n // 128, step, 0)
    factor_ref[...] = jnp.where(c >= r, work[:, :n], 0.0)
    inverse_ref[...] = jnp.where(c <= r, work[:, n:], 0.0)


def factor_panel(gram, rows_total):
    n = 512
    return pl.pallas_call(
        functools.partial(factor_kernel, float(rows_total)),
        out_shape=(jax.ShapeDtypeStruct((n, n), F32), jax.ShapeDtypeStruct((n, n), F32)),
        scratch_shapes=[pltpu.VMEM((n, 2 * n), F32)],
        compiler_params=params(),
        cost_estimate=pl.CostEstimate(
            flops=20 * n * n * n, bytes_accessed=4 << 20, transcendentals=n
        ),
    )(gram)


def cross_kernel(panel_ref, trail_ref, out_ref):
    @pl.when(pl.program_id(0) == 0)
    def _():
        out_ref[...] = jnp.zeros_like(out_ref)

    n = panel_ref.shape[2]
    trail = jnp.concatenate(
        [trail_ref[:, i].reshape(512, 128) for i in range(panel_ref.shape[0])], axis=0
    )
    out_ref[...] += dot(trail, panel_ref[...].reshape(-1, n), TN)


def cross_part(segment, trail):
    n = segment.shape[2]
    return pl.pallas_call(
        cross_kernel,
        out_shape=jax.ShapeDtypeStruct((128, n), F32),
        grid=(segment.shape[0] // 4,),
        in_specs=[
            pl.BlockSpec((4, 512, n), lambda i: (i, 0, 0)),
            pl.BlockSpec((8, 4, 64, 128), lambda i: (0, i, 0, 0)),
        ],
        out_specs=pl.BlockSpec((128, n), lambda i: (0, 0)),
        compiler_params=params(),
        cost_estimate=pl.CostEstimate(
            flops=2 * 128 * n * 8192, bytes_accessed=11 << 20, transcendentals=0
        ),
    )(segment, trail)


def residual_kernel(
    rows_total, cross_ref, inverse_ref, panel_ref, trail_ref, coupling_ref, out_ref, weights
):
    @pl.when(pl.program_id(0) == 0)
    def _():
        coupling = dot(cross_ref[...] / rows_total, inverse_ref[...], NT, HIGHEST)
        coupling_ref[...] = coupling
        solved = dot(coupling, inverse_ref[...], NN, HIGHEST)
        high = solved.astype(BF16)
        weights[:128] = high
        weights[128:] = (solved - high.astype(F32)).astype(BF16)

    r = lax.broadcasted_iota(jnp.int32, (128, 128), 0)
    c = lax.broadcasted_iota(jnp.int32, (128, 128), 1)
    same = (r == c).astype(BF16)
    for i in range(panel_ref.shape[0]):
        both = dot(weights[...], panel_ref[i], NT)
        own = dot(same, trail_ref[:, i].reshape(512, 128), NT)
        out_ref[:, i * 512 : i * 512 + 512] = own - both[:128] - both[128:]


def residual(cross, inverse, segment, trail, rows_total):
    n = inverse.shape[0]
    chunks = segment.shape[0]
    whole = lambda shape: pl.BlockSpec(shape, lambda i: (0, 0))
    return pl.pallas_call(
        functools.partial(residual_kernel, float(rows_total)),
        out_shape=(
            jax.ShapeDtypeStruct((128, n), F32),
            jax.ShapeDtypeStruct((128, 512 * chunks), F32),
        ),
        grid=(chunks // 4,),
        in_specs=[
            whole((128, n)),
            whole((n, n)),
            pl.BlockSpec((4, 512, n), lambda i: (i, 0, 0)),
            pl.BlockSpec((8, 4, 64, 128), lambda i: (0, i, 0, 0)),
        ],
        out_specs=(whole((128, n)), pl.BlockSpec((128, 2048), lambda i: (0, i))),
        scratch_shapes=[pltpu.VMEM((256, n), BF16)],
        compiler_params=params(),
        cost_estimate=pl.CostEstimate(
            flops=4 * 128 * n * 8192, bytes_accessed=16 << 20, transcendentals=0
        ),
    )(cross, inverse, segment, trail)


def sum_row(v, core):
    v = spread4(swap_add(v, core), "row", y_shift)
    return jnp.concatenate(swap_gather(v, core), axis=0)


def per_device(
    descriptors, gradients, sparse_panel, sparse_trail, atom_counts, owner_rows, neighbor_ids
):
    row = lax.axis_index("row")
    col = lax.axis_index("col")
    core, y = row % 2, row // 2
    x, z = col // 4, col % 4
    rows_total = 65536

    where = jnp.stack([x, z, y, core]).astype(jnp.int32)

    trail_own = lax.dynamic_slice_in_dim(sparse_trail, core * 64, 64, 0)
    trail_own = lax.all_gather(trail_own, "col", axis=0, tiled=False)
    piece = lax.dynamic_slice_in_dim(sparse_panel, core * 16, 16, 0)
    piece = jnp.stack(shifted(piece, "col", z_shift))
    own = jnp.stack(shifted(piece, "col", x_shift))
    other = lax.ppermute(own, "row", CORE_SWAP)

    atoms, grads, mean, order = prepare(
        atom_counts,
        owner_rows,
        neighbor_ids.reshape(128, 4).T,
        descriptors,
        gradients.reshape(12, 128, 1024),
    )

    near, far, gram = panel_rows(where, own, other, atoms, grads, mean, order)
    far = lax.ppermute(far, "row", CORE_SWAP)
    gram = swap_add(gram, core)
    far, gram = lax.optimization_barrier((far, gram))
    got = [
        lax.ppermute(jnp.stack([near[s], far[s]]), "row", y_shift(s)) for s in (1, 2, 3)
    ]
    panel = assemble(where, near, far, got).reshape(512, 512)
    panel, gram = lax.optimization_barrier((panel, gram))
    segment = lax.all_gather(panel, "col", axis=0, tiled=False)
    gram = scatter4(gram, "row", y_shift, y)
    trail_own, gram = lax.optimization_barrier((trail_own, gram))
    trail_other = lax.ppermute(trail_own, "row", CORE_SWAP)
    gram = spread4(gram, "col", z_shift)
    trail_other, gram = lax.optimization_barrier((trail_other, gram))
    gram = spread4(gram, "col", x_shift)
    trail = trail_rows(where, trail_own, trail_other, atoms, grads, mean, order)
    trail, gram = lax.optimization_barrier((trail, gram))
    gram = gather4(gram, "row", y_shift, y)
    gram = jnp.concatenate(swap_gather(gram, core), axis=0)
    trail, gram = lax.optimization_barrier((trail, gram))
    trail = lax.all_to_all(
        trail.reshape(128, 64, 128), ("row", "col"), 0, 0, tiled=True
    ).reshape(8, 16, 64, 128)
    factor, inverse = factor_panel(gram, rows_total)

    segment, inverse = lax.optimization_barrier((segment, inverse))
    cross = sum_row(cross_part(segment, trail), core)
    coupling, result = residual(cross, inverse, segment, trail, rows_total)
    return factor, coupling, result


def solution(mesh):
    return jax.shard_map(
        per_device,
        mesh=mesh,
        in_specs=(
            P(("row", "col"), None),
            P(None, None, ("row", "col"), None),
            P("col", None),
            P("col", None),
            P(("row", "col"), None),
            P(("row", "col"), None),
            P(("row", "col"), None, None),
        ),
        out_specs=(P(), P("col", None), P("col", "row")),
        check_vma=False,
    )
```

```python
import functools

import jax
import jax.numpy as jnp
from jax import lax
from jax.experimental import pallas as pl
from jax.experimental.pallas import tpu as pltpu
from jax.sharding import PartitionSpec as P

ridge_value = 0.1
HIGHEST = lax.Precision.HIGHEST
F32 = jnp.float32
BF16 = jnp.bfloat16
NT = (((1,), (1,)), ((), ()))
NN = (((1,), (0,)), ((), ()))
TN = (((0,), (0,)), ((), ()))

CORE_SWAP = [(i, i ^ 1) for i in range(8)]


def y_shift(s):
    return [(2 * y + c, 2 * ((y + s) % 4) + c) for y in range(4) for c in range(2)]


def z_shift(s):
    return [(x * 4 + z, x * 4 + (z + s) % 4) for x in range(4) for z in range(4)]


def x_shift(s):
    return [(x * 4 + z, ((x + s) % 4) * 4 + z) for x in range(4) for z in range(4)]


UPPER = [(i, j) for i in range(4) for j in range(i, 4)]


def y_pair(f):
    return [(2 * y + c, 2 * (y ^ f) + c) for y in range(4) for c in range(2)]


def z_pair(f):
    return [(x * 4 + z, x * 4 + (z ^ f)) for x in range(4) for z in range(4)]


def x_pair(f):
    return [(x * 4 + z, (x ^ f) * 4 + z) for x in range(4) for z in range(4)]


def dot(a, b, dims, precision=None):
    return lax.dot_general(a, b, dims, precision=precision, preferred_element_type=F32)


def in_order(pieces, index):
    return jnp.concatenate(
        [lax.select_n((index - j) % 4, *pieces) for j in range(4)], axis=0
    )


def shifted(v, axis, shift):
    return [v] + [lax.ppermute(v, axis, shift(s)) for s in (1, 2, 3)]


def gather4(v, axis, shift, index):
    pieces = [v] + [lax.ppermute(v, axis, shift(s)) for s in (1, 2, 3)]
    return in_order(pieces, index)


def scatter4(v, axis, shift, index):
    n = v.shape[0] // 4
    total = lax.dynamic_slice_in_dim(v, index * n, n, 0)
    got = [
        lax.ppermute(
            lax.dynamic_slice_in_dim(v, ((index + s) % 4) * n, n, 0), axis, shift(s)
        )
        for s in (1, 2, 3)
    ]
    return total + got[0] + got[1] + got[2]


def swap_add(v, core):
    n = v.shape[0] // 2
    mine = lax.dynamic_slice_in_dim(v, core * n, n, 0)
    other = lax.dynamic_slice_in_dim(v, (1 - core) * n, n, 0)
    return mine + lax.ppermute(other, "row", CORE_SWAP)


def swap_gather(v, core):
    other = lax.ppermute(v, "row", CORE_SWAP)
    first = core == 0
    return jnp.where(first, v, other), jnp.where(first, other, v)


def sum4(v, axis, pairs):
    for flip in (1, 3):
        v = v + lax.ppermute(v, axis, pairs(flip))
    return v


def prep_kernel(
    count_ref, owner_ref, neighbor_ref, desc_ref, grad_ref, atoms_ref, grads_ref, mean_ref, order_ref
):
    counts = [count_ref[0, s] for s in range(8)]
    owners = [owner_ref[0, s] for s in range(8)]
    offsets = [jnp.int32(0)]
    for s in range(7):
        offsets.append(offsets[s] + counts[s])

    lane = lax.broadcasted_iota(jnp.int32, (8, 128), 1)
    struct, atom = lane >> 4, lane & 15
    count_l, offset_l = jnp.ones((8, 128), jnp.int32), jnp.zeros((8, 128), jnp.int32)
    for s in range(8):
        count_l = jnp.where(struct == s, counts[s], count_l)
        offset_l = jnp.where(struct == s, offsets[s], offset_l)
    place = jnp.where(atom < count_l, offset_l + atom, -1)
    rows = lax.broadcasted_iota(jnp.int32, (64, 128), 0)
    lanes = lax.broadcasted_iota(jnp.int32, (64, 128), 1)
    live = place[:1] == rows
    live_f = live.astype(F32)

    value = neighbor_ref[...].astype(F32)
    size = count_l.astype(F32)[:4]
    rest = value - size * jnp.floor(value / size)
    rest = jnp.where(rest < 0.0, rest + size, rest)
    rest = jnp.where(rest >= size, rest - size, rest)
    partner = rest + (16 * struct).astype(F32)[:4]

    picks = [live_f.astype(BF16)]
    for j in range(4):
        slot = jnp.sum(live_f * partner[j : j + 1], axis=1, keepdims=True)
        picks.append((slot == lanes.astype(F32)).astype(F32).astype(BF16))
    desc = desc_ref[...]
    for j in range(5):
        atoms_ref[64 * j : 64 * j + 64] = dot(picks[j], desc, NN).astype(BF16)
    for i in range(12):
        grads_ref[64 * i : 64 * i + 64] = dot(picks[0], grad_ref[i], NN).astype(BF16)

    sub8 = lax.broadcasted_iota(jnp.int32, (8, 64), 0)
    atom8 = lax.broadcasted_iota(jnp.int32, (8, 64), 1)
    low, size8 = jnp.zeros((8, 64), jnp.int32), jnp.ones((8, 64), jnp.int32)
    for s in range(8):
        low = jnp.where(sub8 == s, offsets[s], low)
        size8 = jnp.where(sub8 == s, counts[s], size8)
    inside = (atom8 >= low) & (atom8 < low + size8)
    mean_ref[...] = jnp.where(inside, 1.0 / size8.astype(F32), 0.0)

    r = lax.broadcasted_iota(jnp.int32, (64, 256), 0)
    wanted = lax.broadcasted_iota(jnp.int32, (64, 256), 1)
    third = ((r - 1) * 43) >> 7
    part = (r - 1) - 3 * third
    for g in range(8):
        struct_g, count_g, offset_g = jnp.int32(0), jnp.int32(0), jnp.int32(0)
        for s in range(8):
            mine = owners[s] == g
            struct_g = jnp.where(mine, s, struct_g)
            count_g = jnp.where(mine, counts[s], count_g)
            offset_g = jnp.where(mine, offsets[s], offset_g)
        column = jnp.where(third < count_g, part * 64 + offset_g + third, -1)
        column = jnp.where(r == 0, 192 + struct_g, column)
        order_ref[64 * g : 64 * g + 64] = (column == wanted).astype(F32).astype(BF16)


def prepare(count, owner, neighbors, descriptors, gradients):
    smem = pl.BlockSpec(memory_space=pltpu.SMEM)
    vmem = pl.BlockSpec(memory_space=pltpu.VMEM)
    return pl.pallas_call(
        prep_kernel,
        out_shape=(
            jax.ShapeDtypeStruct((320, 1024), BF16),
            jax.ShapeDtypeStruct((768, 1024), BF16),
            jax.ShapeDtypeStruct((8, 64), F32),
            jax.ShapeDtypeStruct((512, 256), BF16),
        ),
        in_specs=[smem, smem, vmem, vmem, vmem],
        out_specs=(vmem, vmem, vmem, vmem),
        compiler_params=params(),
        cost_estimate=pl.CostEstimate(
            flops=2 * 64 * 128 * 1024 * 17, bytes_accessed=6 << 20, transcendentals=0
        ),
    )(count, owner, neighbors, descriptors, gradients)


def compact_rows(env, atoms, grads, mean):
    near = dot(atoms, env, NT)
    slope = dot(grads, env, NT)
    inner = near[:64]
    parts = []
    for k in range(3):
        total = near[64:128] * slope[k * 256 : k * 256 + 64]
        for j in range(1, 4):
            total = total + near[64 + j * 64 : 128 + j * 64] * slope[
                k * 256 + j * 64 : k * 256 + j * 64 + 64
            ]
        parts.append((-2.0 * total).astype(BF16))
    energy = dot(mean, inner * inner, NN, HIGHEST)
    pad = jnp.zeros((56, env.shape[0]), F32)
    parts.append(jnp.concatenate([energy, pad], axis=0).astype(BF16))
    return jnp.concatenate(parts, axis=0)


def put_env(env, where, own, other, block, at):
    core = where[3]
    env[pl.ds(pl.multiple_of(at + core * 16, 16), 16)] = own[block]
    env[pl.ds(pl.multiple_of(at + (1 - core) * 16, 16), 16)] = other[block]


def panel_kernel(
    where, own, other, atoms_ref, grads_ref, mean_ref, order_ref, near_ref, far_ref, gram_ref, env
):
    x, z, y, core = where[0], where[1], where[2], where[3]
    for i in range(4):
        for j in range(4):
            place = ((x - i) & 3) * 4 + ((z - j) & 3)
            put_env(env, where, own, other, (i, j), place * 32)
    rows = compact_rows(env[...], atoms_ref[...], grads_ref[...], mean_ref[...])
    full = dot(order_ref[...], rows, NN).astype(BF16)
    first = core == 0
    for i in range(4):
        low, high = full[128 * i : 128 * i + 64], full[128 * i + 64 : 128 * i + 128]
        s = (i - y) & 3
        near_ref[s] = jnp.where(first, low, high)
        far_ref[s] = jnp.where(first, high, low)
    gram = dot(rows, rows, TN)
    for n, (i, j) in enumerate(UPPER):
        gram_ref[128 * n : 128 * n + 128] = gram[
            128 * i : 128 * i + 128, 128 * j : 128 * j + 128
        ]


def trail_kernel(
    where, own_ref, other_ref, atoms_ref, grads_ref, mean_ref, order_ref, out_ref
):
    first = where[3] == 0
    own, other = own_ref[...], other_ref[...]
    low, high = jnp.where(first, own, other), jnp.where(first, other, own)
    env = jnp.concatenate([low, high], axis=1).reshape(-1, 1024)
    rows = compact_rows(env, atoms_ref[...], grads_ref[...], mean_ref[...])
    full = dot(order_ref[...], rows, NN).astype(BF16)
    for c in range(out_ref.shape[1]):
        out_ref[:, c] = full[:, c * 128 : c * 128 + 128].reshape(8, 64, 128)


def assemble_kernel(where, near, far, got1, got2, got3, out):
    y, core = where[2], where[3]
    out[2 * y + core] = near[0]
    out[2 * y + 1 - core] = far[0]
    for s, got in ((1, got1), (2, got2), (3, got3)):
        at = 2 * ((y - s) & 3)
        out[at + core] = got[0]
        out[at + 1 - core] = got[1]


def params(mib=40):
    return pltpu.CompilerParams(vmem_limit_bytes=mib << 20)


def in_smem():
    return pl.BlockSpec(memory_space=pltpu.SMEM)


def in_vmem():
    return pl.BlockSpec(memory_space=pltpu.VMEM)


def panel_rows(where, own, other, atoms, grads, mean, order):
    return pl.pallas_call(
        panel_kernel,
        out_shape=(
            jax.ShapeDtypeStruct((4, 64, 512), BF16),
            jax.ShapeDtypeStruct((4, 64, 512), BF16),
            jax.ShapeDtypeStruct((1280, 128), F32),
        ),
        in_specs=[in_smem()] + [in_vmem()] * 6,
        out_specs=(in_vmem(),) * 3,
        scratch_shapes=[pltpu.VMEM((512, 1024), BF16)],
        compiler_params=params(),
        cost_estimate=pl.CostEstimate(
            flops=2 * 512 * 1024 * 1088, bytes_accessed=5 << 20, transcendentals=0
        ),
    )(where, own, other, atoms, grads, mean, order)


def assemble(where, near, far, got):
    return pl.pallas_call(
        assemble_kernel,
        out_shape=jax.ShapeDtypeStruct((8, 64, 512), BF16),
        in_specs=[in_smem()] + [in_vmem()] * 5,
        out_specs=in_vmem(),
        compiler_params=params(),
        cost_estimate=pl.CostEstimate(flops=0, bytes_accessed=1 << 20, transcendentals=0),
    )(where, near, far, *got)


def trail_rows(where, own, other, atoms, grads, mean, order):
    blocks = own.shape[0]
    step = 4
    half = pl.BlockSpec((step, 64, 1024), lambda i, w: (i, 0, 0))
    whole = lambda shape: pl.BlockSpec(shape, lambda i, w: (0, 0))
    return pl.pallas_call(
        trail_kernel,
        out_shape=jax.ShapeDtypeStruct((8, blocks, 64, 128), BF16),
        grid_spec=pltpu.PrefetchScalarGridSpec(
            num_scalar_prefetch=1,
            grid=(blocks // step,),
            in_specs=[
                half,
                half,
                whole(atoms.shape),
                whole(grads.shape),
                whole(mean.shape),
                whole(order.shape),
            ],
            out_specs=pl.BlockSpec((8, step, 64, 128), lambda i, w: (0, i, 0, 0)),
        ),
        compiler_params=params(),
        cost_estimate=pl.CostEstimate(
            flops=2 * 2048 * 1024 * 1088, bytes_accessed=9 << 20, transcendentals=0
        ),
    )(where, own, other, atoms, grads, mean, order)


def eliminate(a):
    lanes = lax.broadcasted_iota(jnp.int32, (8, 128), 1)
    subs = lax.broadcasted_iota(jnp.int32, (8, 128), 0)
    left = [a[8 * g : 8 * g + 8] for g in range(16)]
    right = [(lanes == subs + 8 * g).astype(F32) for g in range(16)]
    done = []
    for p in range(16):
        count = 16 - p
        cols = [
            [
                jnp.broadcast_to(left[g][:, 8 * p + q : 8 * p + q + 1], (8, 128))
                for g in range(count)
            ]
            for q in range(8)
        ]
        pivots = jnp.ones((8, 128), F32)
        for q in range(8):
            pivot = cols[q][0][q : q + 1]
            inverse = 1.0 / pivot
            pivots = jnp.where(subs == q, pivot, pivots)
            ratio = [c * inverse for c in cols[q]]
            ratio[0] = jnp.where(subs > q, ratio[0], 0.0)
            for t in range(q + 1, 8):
                here = cols[t][0][q : q + 1]
                for g in range(count):
                    cols[t][g] = cols[t][g] - ratio[g] * here
            row_left = left[0][q : q + 1]
            row_right = right[0][q : q + 1]
            for g in range(count):
                left[g] = left[g] - ratio[g] * row_left
                right[g] = right[g] - ratio[g] * row_right
        done.append(right[0] * lax.rsqrt(pivots))
        left, right = left[1:], right[1:]
    return jnp.concatenate(done, axis=0)


def factor_kernel(rows_total, gram_ref, factor_ref, inverse_ref, work):
    n = factor_ref.shape[0]
    r = lax.broadcasted_iota(jnp.int32, (n, n), 0)
    c = lax.broadcasted_iota(jnp.int32, (n, n), 1)
    same = r[:128, :128] == c[:128, :128]
    work[:, :n] = jnp.zeros((n, n), F32)
    for m, (i, j) in enumerate(UPPER):
        block = gram_ref[128 * m : 128 * m + 128] / rows_total
        if i == j:
            block = block + jnp.where(same, ridge_value, 0.0)
        work[128 * i : 128 * i + 128, 128 * j : 128 * j + 128] = block
    work[:, n:] = jnp.where(r == c, 1.0, 0.0)

    def step(b, carry):
        at = pl.multiple_of(b * 128, 128)
        low = eliminate(work[pl.ds(at, 128), pl.ds(at, 128)])
        row = dot(low, work[pl.ds(at, 128), :], NN, HIGHEST)
        lane = lax.broadcasted_iota(jnp.int32, (128, n), 1)
        later = jnp.where(lane >= at + 128, row[:, :n], 0.0)
        work[...] = work[...] - dot(later, row, TN, HIGHEST)
        work[pl.ds(at, 128), :] = row
        return carry

    lax.fori_loop(0, n // 128, step, 0)
    factor_ref[...] = jnp.where(c >= r, work[:, :n], 0.0)
    inverse_ref[...] = jnp.where(c <= r, work[:, n:], 0.0)


def factor_panel(gram, rows_total):
    n = 512
    return pl.pallas_call(
        functools.partial(factor_kernel, float(rows_total)),
        out_shape=(jax.ShapeDtypeStruct((n, n), F32), jax.ShapeDtypeStruct((n, n), F32)),
        scratch_shapes=[pltpu.VMEM((n, 2 * n), F32)],
        compiler_params=params(),
        cost_estimate=pl.CostEstimate(
            flops=20 * n * n * n, bytes_accessed=4 << 20, transcendentals=n
        ),
    )(gram)


def cross_kernel(panel_ref, trail_ref, out_ref):
    @pl.when(pl.program_id(0) == 0)
    def _():
        out_ref[...] = jnp.zeros_like(out_ref)

    n = panel_ref.shape[2]
    trail = jnp.concatenate(
        [trail_ref[:, i].reshape(512, 128) for i in range(panel_ref.shape[0])], axis=0
    )
    out_ref[...] += dot(trail, panel_ref[...].reshape(-1, n), TN)


def cross_part(segment, trail):
    n = segment.shape[2]
    return pl.pallas_call(
        cross_kernel,
        out_shape=jax.ShapeDtypeStruct((128, n), F32),
        grid=(segment.shape[0] // 4,),
        in_specs=[
            pl.BlockSpec((4, 512, n), lambda i: (i, 0, 0)),
            pl.BlockSpec((8, 4, 64, 128), lambda i: (0, i, 0, 0)),
        ],
        out_specs=pl.BlockSpec((128, n), lambda i: (0, 0)),
        compiler_params=params(),
        cost_estimate=pl.CostEstimate(
            flops=2 * 128 * n * 8192, bytes_accessed=11 << 20, transcendentals=0
        ),
    )(segment, trail)


def residual_kernel(
    rows_total, cross_ref, inverse_ref, panel_ref, trail_ref, coupling_ref, out_ref, weights
):
    @pl.when(pl.program_id(0) == 0)
    def _():
        coupling = dot(cross_ref[...] / rows_total, inverse_ref[...], NT, HIGHEST)
        coupling_ref[...] = coupling
        solved = dot(coupling, inverse_ref[...], NN, HIGHEST)
        high = solved.astype(BF16)
        weights[:128] = high
        weights[128:] = (solved - high.astype(F32)).astype(BF16)

    r = lax.broadcasted_iota(jnp.int32, (128, 128), 0)
    c = lax.broadcasted_iota(jnp.int32, (128, 128), 1)
    same = (r == c).astype(BF16)
    for i in range(panel_ref.shape[0]):
        both = dot(weights[...], panel_ref[i], NT)
        own = dot(same, trail_ref[:, i].reshape(512, 128), NT)
        out_ref[:, i * 512 : i * 512 + 512] = own - both[:128] - both[128:]


def residual(cross, inverse, segment, trail, rows_total):
    n = inverse.shape[0]
    chunks = segment.shape[0]
    whole = lambda shape: pl.BlockSpec(shape, lambda i: (0, 0))
    return pl.pallas_call(
        functools.partial(residual_kernel, float(rows_total)),
        out_shape=(
            jax.ShapeDtypeStruct((128, n), F32),
            jax.ShapeDtypeStruct((128, 512 * chunks), F32),
        ),
        grid=(chunks // 4,),
        in_specs=[
            whole((128, n)),
            whole((n, n)),
            pl.BlockSpec((4, 512, n), lambda i: (i, 0, 0)),
            pl.BlockSpec((8, 4, 64, 128), lambda i: (0, i, 0, 0)),
        ],
        out_specs=(whole((128, n)), pl.BlockSpec((128, 2048), lambda i: (0, i))),
        scratch_shapes=[pltpu.VMEM((256, n), BF16)],
        compiler_params=params(),
        cost_estimate=pl.CostEstimate(
            flops=4 * 128 * n * 8192, bytes_accessed=16 << 20, transcendentals=0
        ),
    )(cross, inverse, segment, trail)


def sum_row(v, core):
    v = sum4(swap_add(v, core), "row", y_pair)
    return jnp.concatenate(swap_gather(v, core), axis=0)


def per_device(
    descriptors, gradients, sparse_panel, sparse_trail, atom_counts, owner_rows, neighbor_ids
):
    row = lax.axis_index("row")
    col = lax.axis_index("col")
    core, y = row % 2, row // 2
    x, z = col // 4, col % 4
    rows_total = 65536

    where = jnp.stack([x, z, y, core]).astype(jnp.int32)

    trail_own = lax.dynamic_slice_in_dim(sparse_trail, core * 64, 64, 0)
    trail_own = lax.all_gather(trail_own, "col", axis=0, tiled=False)
    piece = lax.dynamic_slice_in_dim(sparse_panel, core * 16, 16, 0)
    piece = jnp.stack(shifted(piece, "col", z_shift))
    own = jnp.stack(shifted(piece, "col", x_shift))
    other = lax.ppermute(own, "row", CORE_SWAP)

    atoms, grads, mean, order = prepare(
        atom_counts,
        owner_rows,
        neighbor_ids.reshape(128, 4).T,
        descriptors,
        gradients.reshape(12, 128, 1024),
    )

    near, far, gram = panel_rows(where, own, other, atoms, grads, mean, order)
    far = lax.ppermute(far, "row", CORE_SWAP)
    gram = swap_add(gram, core)
    far, gram = lax.optimization_barrier((far, gram))
    got = [
        lax.ppermute(jnp.stack([near[s], far[s]]), "row", y_shift(s)) for s in (1, 2, 3)
    ]
    gram = scatter4(gram, "row", y_shift, y)
    got, gram = lax.optimization_barrier((got, gram))
    panel = assemble(where, near, far, got).reshape(512, 512)
    segment = lax.all_gather(panel, "col", axis=0, tiled=False)
    trail_other = lax.ppermute(trail_own, "row", CORE_SWAP)
    gram = sum4(gram, "col", z_pair)
    trail_other, gram = lax.optimization_barrier((trail_other, gram))
    gram = sum4(gram, "col", x_pair)
    trail = trail_rows(where, trail_own, trail_other, atoms, grads, mean, order)
    trail, gram = lax.optimization_barrier((trail, gram))
    gram = gather4(gram, "row", y_shift, y)
    trail, gram = lax.optimization_barrier((trail, gram))
    gram = jnp.concatenate(swap_gather(gram, core), axis=0)
    trail = lax.all_to_all(
        trail.reshape(128, 64, 128), ("row", "col"), 0, 0, tiled=True
    ).reshape(8, 16, 64, 128)
    factor, inverse = factor_panel(gram, rows_total)

    segment, inverse = lax.optimization_barrier((segment, inverse))
    cross = sum_row(cross_part(segment, trail), core)
    coupling, result = residual(cross, inverse, segment, trail, rows_total)
    return factor, coupling, result


def solution(mesh):
    return jax.shard_map(
        per_device,
        mesh=mesh,
        in_specs=(
            P(("row", "col"), None),
            P(None, None, ("row", "col"), None),
            P("col", None),
            P("col", None),
            P(("row", "col"), None),
            P(("row", "col"), None),
            P(("row", "col"), None, None),
        ),
        out_specs=(P(), P("col", None), P("col", "row")),
        check_vma=False,
    )
```

```python
import functools

import jax
import jax.numpy as jnp
from jax import lax
from jax.experimental import pallas as pl
from jax.experimental.pallas import tpu as pltpu
from jax.sharding import PartitionSpec as P

ridge_value = 0.1
HIGHEST = lax.Precision.HIGHEST
F32 = jnp.float32
BF16 = jnp.bfloat16
NT = (((1,), (1,)), ((), ()))
NN = (((1,), (0,)), ((), ()))
TN = (((0,), (0,)), ((), ()))

CORE_SWAP = [(i, i ^ 1) for i in range(8)]


def y_shift(s):
    return [(2 * y + c, 2 * ((y + s) % 4) + c) for y in range(4) for c in range(2)]


def z_shift(s):
    return [(x * 4 + z, x * 4 + (z + s) % 4) for x in range(4) for z in range(4)]


def x_shift(s):
    return [(x * 4 + z, ((x + s) % 4) * 4 + z) for x in range(4) for z in range(4)]


SENT = 56
HELD = 400
UPPER = [(i, j) for i in range(4) for j in range(i, 4)]


def y_pair(f):
    return [(2 * y + c, 2 * (y ^ f) + c) for y in range(4) for c in range(2)]


def z_pair(f):
    return [(x * 4 + z, x * 4 + (z ^ f)) for x in range(4) for z in range(4)]


def x_pair(f):
    return [(x * 4 + z, (x ^ f) * 4 + z) for x in range(4) for z in range(4)]


def dot(a, b, dims, precision=None):
    return lax.dot_general(a, b, dims, precision=precision, preferred_element_type=F32)


def in_order(pieces, index):
    return jnp.concatenate(
        [lax.select_n((index - j) % 4, *pieces) for j in range(4)], axis=0
    )


def shifted(v, axis, shift):
    return [v] + [lax.ppermute(v, axis, shift(s)) for s in (1, 2, 3)]


def gather4(v, axis, shift, index):
    pieces = [v] + [lax.ppermute(v, axis, shift(s)) for s in (1, 2, 3)]
    return in_order(pieces, index)


def scatter4(v, axis, shift, index):
    n = v.shape[0] // 4
    total = lax.dynamic_slice_in_dim(v, index * n, n, 0)
    got = [
        lax.ppermute(
            lax.dynamic_slice_in_dim(v, ((index + s) % 4) * n, n, 0), axis, shift(s)
        )
        for s in (1, 2, 3)
    ]
    return total + got[0] + got[1] + got[2]


def swap_add(v, core):
    n = v.shape[0] // 2
    mine = lax.dynamic_slice_in_dim(v, core * n, n, 0)
    other = lax.dynamic_slice_in_dim(v, (1 - core) * n, n, 0)
    return mine + lax.ppermute(other, "row", CORE_SWAP)


def swap_gather(v, core):
    other = lax.ppermute(v, "row", CORE_SWAP)
    first = core == 0
    return jnp.where(first, v, other), jnp.where(first, other, v)


def sum4(v, axis, pairs):
    for flip in (1, 3):
        v = v + lax.ppermute(v, axis, pairs(flip))
    return v


def prep_kernel(
    where, count_ref, owner_ref, neighbor_ref, desc_ref, grad_ref, atoms_ref, grads_ref, mean_ref, order_ref
):
    counts = [count_ref[0, s] for s in range(8)]
    owners = [owner_ref[0, s] for s in range(8)]
    offsets = [jnp.int32(0)]
    for s in range(7):
        offsets.append(offsets[s] + counts[s])

    lane = lax.broadcasted_iota(jnp.int32, (8, 128), 1)
    struct, atom = lane >> 4, lane & 15
    count_l, offset_l = jnp.ones((8, 128), jnp.int32), jnp.zeros((8, 128), jnp.int32)
    for s in range(8):
        count_l = jnp.where(struct == s, counts[s], count_l)
        offset_l = jnp.where(struct == s, offsets[s], offset_l)
    place = jnp.where(atom < count_l, offset_l + atom, -1)
    rows = lax.broadcasted_iota(jnp.int32, (64, 128), 0)
    lanes = lax.broadcasted_iota(jnp.int32, (64, 128), 1)
    live = place[:1] == rows
    live_f = live.astype(F32)

    value = neighbor_ref[...].astype(F32)
    size = count_l.astype(F32)[:4]
    rest = value - size * jnp.floor(value / size)
    rest = jnp.where(rest < 0.0, rest + size, rest)
    rest = jnp.where(rest >= size, rest - size, rest)
    partner = rest + (16 * struct).astype(F32)[:4]

    picks = [live_f.astype(BF16)]
    for j in range(4):
        slot = jnp.sum(live_f * partner[j : j + 1], axis=1, keepdims=True)
        picks.append((slot == lanes.astype(F32)).astype(F32).astype(BF16))
    desc = desc_ref[...]
    for j in range(5):
        atoms_ref[64 * j : 64 * j + 64] = dot(picks[j], desc, NN).astype(BF16)
    for i in range(12):
        grads_ref[64 * i : 64 * i + 64] = dot(picks[0], grad_ref[i], NN).astype(BF16)

    sub8 = lax.broadcasted_iota(jnp.int32, (8, 64), 0)
    atom8 = lax.broadcasted_iota(jnp.int32, (8, 64), 1)
    low, size8 = jnp.zeros((8, 64), jnp.int32), jnp.ones((8, 64), jnp.int32)
    for s in range(8):
        low = jnp.where(sub8 == s, offsets[s], low)
        size8 = jnp.where(sub8 == s, counts[s], size8)
    inside = (atom8 >= low) & (atom8 < low + size8)
    mean_ref[...] = jnp.where(inside, 1.0 / size8.astype(F32), 0.0)

    source = 2 * where[2] + where[3]
    r = lax.broadcasted_iota(jnp.int32, (SENT, 256), 0)
    wanted = lax.broadcasted_iota(jnp.int32, (SENT, 256), 1)
    third = (r * 43) >> 7
    part = r - 3 * third
    for g in range(8):
        struct_g, count_g, offset_g = jnp.int32(0), jnp.int32(0), jnp.int32(0)
        for s in range(8):
            mine = owners[s] == g
            struct_g = jnp.where(mine, s, struct_g)
            count_g = jnp.where(mine, counts[s], count_g)
            offset_g = jnp.where(mine, offsets[s], offset_g)
        column = jnp.where((third < count_g) & (r < 48), part * 64 + offset_g + third, -1)
        column = jnp.where(r == 48 + source, 192 + struct_g, column)
        order_ref[SENT * g : SENT * g + SENT] = (column == wanted).astype(F32)


def prepare(where, count, owner, neighbors, descriptors, gradients):
    smem = pl.BlockSpec(memory_space=pltpu.SMEM)
    vmem = pl.BlockSpec(memory_space=pltpu.VMEM)
    return pl.pallas_call(
        prep_kernel,
        out_shape=(
            jax.ShapeDtypeStruct((320, 1024), BF16),
            jax.ShapeDtypeStruct((768, 1024), BF16),
            jax.ShapeDtypeStruct((8, 64), F32),
            jax.ShapeDtypeStruct((8 * SENT, 256), F32),
        ),
        in_specs=[smem, smem, smem, vmem, vmem, vmem],
        out_specs=(vmem, vmem, vmem, vmem),
        compiler_params=params(),
        cost_estimate=pl.CostEstimate(
            flops=2 * 64 * 128 * 1024 * 17, bytes_accessed=6 << 20, transcendentals=0
        ),
    )(where, count, owner, neighbors, descriptors, gradients)


def compact_rows(env, atoms, grads, mean):
    near = dot(atoms, env, NT)
    slope = dot(grads, env, NT)
    inner = near[:64]
    parts = []
    for k in range(3):
        total = near[64:128] * slope[k * 256 : k * 256 + 64]
        for j in range(1, 4):
            total = total + near[64 + j * 64 : 128 + j * 64] * slope[
                k * 256 + j * 64 : k * 256 + j * 64 + 64
            ]
        parts.append((-2.0 * total).astype(BF16))
    energy = dot(mean, inner * inner, NN, HIGHEST)
    pad = jnp.zeros((56, env.shape[0]), F32)
    parts.append(jnp.concatenate([energy, pad], axis=0).astype(BF16))
    return jnp.concatenate(parts, axis=0)


def put_env(env, where, own, other, block, at):
    core = where[3]
    env[pl.ds(pl.multiple_of(at + core * 16, 16), 16)] = own[block]
    env[pl.ds(pl.multiple_of(at + (1 - core) * 16, 16), 16)] = other[block]


def panel_kernel(
    where, own, other, atoms_ref, grads_ref, mean_ref, order_ref, near_ref, far_ref, gram_ref, env
):
    x, z, y, core = where[0], where[1], where[2], where[3]
    for i in range(4):
        for j in range(4):
            place = ((x - i) & 3) * 4 + ((z - j) & 3)
            put_env(env, where, own, other, (i, j), place * 32)
    rows = compact_rows(env[...], atoms_ref[...], grads_ref[...], mean_ref[...])
    full = dot(order_ref[...].astype(BF16), rows, NN)
    first = core == 0
    for i in range(4):
        at = 2 * SENT * i
        low, high = full[at : at + SENT], full[at + SENT : at + 2 * SENT]
        s = (i - y) & 3
        near_ref[s] = jnp.where(first, low, high).astype(BF16)
        far_ref[s] = jnp.where(first, high, low).astype(BF16)
    gram = dot(rows, rows, TN)
    for n, (i, j) in enumerate(UPPER):
        gram_ref[128 * n : 128 * n + 128] = gram[
            128 * i : 128 * i + 128, 128 * j : 128 * j + 128
        ]


def trail_kernel(
    where, own_ref, other_ref, atoms_ref, grads_ref, mean_ref, order_ref, out_ref
):
    first = where[3] == 0
    own, other = own_ref[...], other_ref[...]
    low, high = jnp.where(first, own, other), jnp.where(first, other, own)
    env = jnp.concatenate([low, high], axis=1).reshape(-1, 1024)
    rows = compact_rows(env, atoms_ref[...], grads_ref[...], mean_ref[...])
    full = dot(order_ref[...].astype(BF16), rows, NN)
    for c in range(out_ref.shape[1]):
        part = full[:, c * 128 : c * 128 + 128].reshape(8, SENT, 128)
        out_ref[:, c] = part.astype(BF16)


def assemble_kernel(where, near, far, got1, got2, got3, out):
    y, core = where[2], where[3]
    blocks = [(near, 0, 0, core), (far, 0, 0, 1 - core)]
    for s, got in ((1, got1), (2, got2), (3, got3)):
        blocks += [(got, 0, s, core), (got, 1, s, 1 - core)]
    energy = jnp.zeros((8, out.shape[1]), F32)
    for ref, i, s, c in blocks:
        at = (2 * ((y - s) & 3) + c) * 48
        out[pl.ds(pl.multiple_of(at, 16), 48)] = ref[i, :48]
        energy = energy + ref[i, 48:].astype(F32)
    out[384:] = jnp.concatenate([energy, jnp.zeros_like(energy)], axis=0).astype(BF16)


def trail_chunk(ref, i):
    rows = [ref[r, i, :48].astype(F32) for r in range(8)]
    energy = ref[0, i, 48:].astype(F32)
    for r in range(1, 8):
        energy = energy + ref[r, i, 48:].astype(F32)
    return jnp.concatenate(rows + [energy, jnp.zeros_like(energy)], axis=0).astype(BF16)


def params(mib=40):
    return pltpu.CompilerParams(vmem_limit_bytes=mib << 20)


def in_smem():
    return pl.BlockSpec(memory_space=pltpu.SMEM)


def in_vmem():
    return pl.BlockSpec(memory_space=pltpu.VMEM)


def panel_rows(where, own, other, atoms, grads, mean, order):
    return pl.pallas_call(
        panel_kernel,
        out_shape=(
            jax.ShapeDtypeStruct((4, SENT, 512), BF16),
            jax.ShapeDtypeStruct((4, SENT, 512), BF16),
            jax.ShapeDtypeStruct((1280, 128), F32),
        ),
        in_specs=[in_smem()] + [in_vmem()] * 6,
        out_specs=(in_vmem(),) * 3,
        scratch_shapes=[pltpu.VMEM((512, 1024), BF16)],
        compiler_params=params(),
        cost_estimate=pl.CostEstimate(
            flops=2 * 512 * 1024 * 1088, bytes_accessed=5 << 20, transcendentals=0
        ),
    )(where, own, other, atoms, grads, mean, order)


def assemble(where, near, far, got):
    return pl.pallas_call(
        assemble_kernel,
        out_shape=jax.ShapeDtypeStruct((HELD, 512), BF16),
        in_specs=[in_smem()] + [in_vmem()] * 5,
        out_specs=in_vmem(),
        compiler_params=params(),
        cost_estimate=pl.CostEstimate(flops=0, bytes_accessed=1 << 20, transcendentals=0),
    )(where, near, far, *got)


def trail_rows(where, own, other, atoms, grads, mean, order):
    blocks = own.shape[0]
    step = 4
    half = pl.BlockSpec((step, 64, 1024), lambda i, w: (i, 0, 0))
    whole = lambda shape: pl.BlockSpec(shape, lambda i, w: (0, 0))
    return pl.pallas_call(
        trail_kernel,
        out_shape=jax.ShapeDtypeStruct((8, blocks, SENT, 128), BF16),
        grid_spec=pltpu.PrefetchScalarGridSpec(
            num_scalar_prefetch=1,
            grid=(blocks // step,),
            in_specs=[
                half,
                half,
                whole(atoms.shape),
                whole(grads.shape),
                whole(mean.shape),
                whole(order.shape),
            ],
            out_specs=pl.BlockSpec((8, step, SENT, 128), lambda i, w: (0, i, 0, 0)),
        ),
        compiler_params=params(),
        cost_estimate=pl.CostEstimate(
            flops=2 * 2048 * 1024 * 1088, bytes_accessed=9 << 20, transcendentals=0
        ),
    )(where, own, other, atoms, grads, mean, order)


def eliminate(a):
    lanes = lax.broadcasted_iota(jnp.int32, (8, 128), 1)
    subs = lax.broadcasted_iota(jnp.int32, (8, 128), 0)
    left = [a[8 * g : 8 * g + 8] for g in range(16)]
    right = [(lanes == subs + 8 * g).astype(F32) for g in range(16)]
    done = []
    for p in range(16):
        count = 16 - p
        cols = [
            [
                jnp.broadcast_to(left[g][:, 8 * p + q : 8 * p + q + 1], (8, 128))
                for g in range(count)
            ]
            for q in range(8)
        ]
        pivots = jnp.ones((8, 128), F32)
        for q in range(8):
            pivot = cols[q][0][q : q + 1]
            inverse = 1.0 / pivot
            pivots = jnp.where(subs == q, pivot, pivots)
            ratio = [c * inverse for c in cols[q]]
            ratio[0] = jnp.where(subs > q, ratio[0], 0.0)
            for t in range(q + 1, 8):
                here = cols[t][0][q : q + 1]
                for g in range(count):
                    cols[t][g] = cols[t][g] - ratio[g] * here
            row_left = left[0][q : q + 1]
            row_right = right[0][q : q + 1]
            for g in range(count):
                left[g] = left[g] - ratio[g] * row_left
                right[g] = right[g] - ratio[g] * row_right
        done.append(right[0] * lax.rsqrt(pivots))
        left, right = left[1:], right[1:]
    return jnp.concatenate(done, axis=0)


def factor_kernel(rows_total, gram_ref, factor_ref, inverse_ref, work):
    n = factor_ref.shape[0]
    r = lax.broadcasted_iota(jnp.int32, (n, n), 0)
    c = lax.broadcasted_iota(jnp.int32, (n, n), 1)
    same = r[:128, :128] == c[:128, :128]
    work[:, :n] = jnp.zeros((n, n), F32)
    for m, (i, j) in enumerate(UPPER):
        block = gram_ref[128 * m : 128 * m + 128] / rows_total
        if i == j:
            block = block + jnp.where(same, ridge_value, 0.0)
        work[128 * i : 128 * i + 128, 128 * j : 128 * j + 128] = block
    work[:, n:] = jnp.where(r == c, 1.0, 0.0)

    def step(b, carry):
        at = pl.multiple_of(b * 128, 128)
        low = eliminate(work[pl.ds(at, 128), pl.ds(at, 128)])
        row = dot(low, work[pl.ds(at, 128), :], NN, HIGHEST)
        lane = lax.broadcasted_iota(jnp.int32, (128, n), 1)
        later = jnp.where(lane >= at + 128, row[:, :n], 0.0)
        work[...] = work[...] - dot(later, row, TN, HIGHEST)
        work[pl.ds(at, 128), :] = row
        return carry

    lax.fori_loop(0, n // 128, step, 0)
    factor_ref[...] = jnp.where(c >= r, work[:, :n], 0.0)
    inverse_ref[...] = jnp.where(c <= r, work[:, n:], 0.0)


def factor_panel(gram, rows_total):
    n = 512
    return pl.pallas_call(
        functools.partial(factor_kernel, float(rows_total)),
        out_shape=(jax.ShapeDtypeStruct((n, n), F32), jax.ShapeDtypeStruct((n, n), F32)),
        scratch_shapes=[pltpu.VMEM((n, 2 * n), F32)],
        compiler_params=params(),
        cost_estimate=pl.CostEstimate(
            flops=20 * n * n * n, bytes_accessed=4 << 20, transcendentals=n
        ),
    )(gram)


def cross_kernel(panel_ref, trail_ref, out_ref):
    @pl.when(pl.program_id(0) == 0)
    def _():
        out_ref[...] = jnp.zeros_like(out_ref)

    n = panel_ref.shape[2]
    trail = jnp.concatenate(
        [trail_chunk(trail_ref, i) for i in range(panel_ref.shape[0])], axis=0
    )
    out_ref[...] += dot(trail, panel_ref[...].reshape(-1, n), TN)


def cross_part(segment, trail):
    n = segment.shape[2]
    return pl.pallas_call(
        cross_kernel,
        out_shape=jax.ShapeDtypeStruct((128, n), F32),
        grid=(segment.shape[0] // 4,),
        in_specs=[
            pl.BlockSpec((4, HELD, n), lambda i: (i, 0, 0)),
            pl.BlockSpec((8, 4, SENT, 128), lambda i: (0, i, 0, 0)),
        ],
        out_specs=pl.BlockSpec((128, n), lambda i: (0, 0)),
        compiler_params=params(),
        cost_estimate=pl.CostEstimate(
            flops=2 * 128 * n * 8192, bytes_accessed=11 << 20, transcendentals=0
        ),
    )(segment, trail)


def residual_kernel(
    rows_total, cross_ref, inverse_ref, panel_ref, trail_ref, coupling_ref, out_ref, weights, spread
):
    @pl.when(pl.program_id(0) == 0)
    def _():
        coupling = dot(cross_ref[...] / rows_total, inverse_ref[...], NT, HIGHEST)
        coupling_ref[...] = coupling
        solved = dot(coupling, inverse_ref[...], NN, HIGHEST)
        high = solved.astype(BF16)
        weights[:128] = high
        weights[128:] = (solved - high.astype(F32)).astype(BF16)
        held = lax.broadcasted_iota(jnp.int32, (HELD, 512), 0)
        column = lax.broadcasted_iota(jnp.int32, (HELD, 512), 1)
        struct, place = column >> 6, column & 63
        wanted = jnp.where(place <= 48, struct * 48 + place - 1, -1)
        wanted = jnp.where(place == 0, 384 + struct, wanted)
        spread[...] = (held == wanted).astype(F32).astype(BF16)

    r = lax.broadcasted_iota(jnp.int32, (128, 128), 0)
    c = lax.broadcasted_iota(jnp.int32, (128, 128), 1)
    same = (r == c).astype(BF16)
    for i in range(panel_ref.shape[0]):
        both = dot(weights[...], panel_ref[i], NT)
        own = dot(same, trail_chunk(trail_ref, i), NT)
        rest = own - both[:128] - both[128:]
        high = rest.astype(BF16)
        low = (rest - high.astype(F32)).astype(BF16)
        full = dot(jnp.concatenate([high, low], axis=0), spread[...], NN)
        out_ref[:, i * 512 : i * 512 + 512] = full[:128] + full[128:]


def residual(cross, inverse, segment, trail, rows_total):
    n = inverse.shape[0]
    chunks = segment.shape[0]
    whole = lambda shape: pl.BlockSpec(shape, lambda i: (0, 0))
    return pl.pallas_call(
        functools.partial(residual_kernel, float(rows_total)),
        out_shape=(
            jax.ShapeDtypeStruct((128, n), F32),
            jax.ShapeDtypeStruct((128, 512 * chunks), F32),
        ),
        grid=(chunks // 4,),
        in_specs=[
            whole((128, n)),
            whole((n, n)),
            pl.BlockSpec((4, HELD, n), lambda i: (i, 0, 0)),
            pl.BlockSpec((8, 4, SENT, 128), lambda i: (0, i, 0, 0)),
        ],
        out_specs=(whole((128, n)), pl.BlockSpec((128, 2048), lambda i: (0, i))),
        scratch_shapes=[pltpu.VMEM((256, n), BF16), pltpu.VMEM((HELD, 512), BF16)],
        compiler_params=params(),
        cost_estimate=pl.CostEstimate(
            flops=4 * 128 * n * 8192, bytes_accessed=16 << 20, transcendentals=0
        ),
    )(cross, inverse, segment, trail)


def sum_row(v, core):
    v = sum4(swap_add(v, core), "row", y_pair)
    return jnp.concatenate(swap_gather(v, core), axis=0)


def per_device(
    descriptors, gradients, sparse_panel, sparse_trail, atom_counts, owner_rows, neighbor_ids
):
    row = lax.axis_index("row")
    col = lax.axis_index("col")
    core, y = row % 2, row // 2
    x, z = col // 4, col % 4
    rows_total = 65536

    where = jnp.stack([x, z, y, core]).astype(jnp.int32)

    trail_own = lax.dynamic_slice_in_dim(sparse_trail, core * 64, 64, 0)
    trail_own = lax.all_gather(trail_own, "col", axis=0, tiled=False)
    piece = lax.dynamic_slice_in_dim(sparse_panel, core * 16, 16, 0)
    piece = jnp.stack(shifted(piece, "col", z_shift))
    own = jnp.stack(shifted(piece, "col", x_shift))
    other = lax.ppermute(own, "row", CORE_SWAP)

    atoms, grads, mean, order = prepare(
        where,
        atom_counts,
        owner_rows,
        neighbor_ids.reshape(128, 4).T,
        descriptors,
        gradients.reshape(12, 128, 1024),
    )

    near, far, gram = panel_rows(where, own, other, atoms, grads, mean, order)
    far = lax.ppermute(far, "row", CORE_SWAP)
    gram = swap_add(gram, core)
    far, gram = lax.optimization_barrier((far, gram))
    got = [
        lax.ppermute(jnp.stack([near[s], far[s]]), "row", y_shift(s)) for s in (1, 2, 3)
    ]
    gram = scatter4(gram, "row", y_shift, y)
    got, gram = lax.optimization_barrier((got, gram))
    panel = assemble(where, near, far, got)
    segment = lax.all_gather(panel, "col", axis=0, tiled=False)
    trail_other = lax.ppermute(trail_own, "row", CORE_SWAP)
    gram = sum4(gram, "col", z_pair)
    trail_other, gram = lax.optimization_barrier((trail_other, gram))
    gram = sum4(gram, "col", x_pair)
    trail = trail_rows(where, trail_own, trail_other, atoms, grads, mean, order)
    trail, gram = lax.optimization_barrier((trail, gram))
    gram = gather4(gram, "row", y_shift, y)
    trail, gram = lax.optimization_barrier((trail, gram))
    gram = jnp.concatenate(swap_gather(gram, core), axis=0)
    trail = lax.all_to_all(
        trail.reshape(128, SENT, 128), ("row", "col"), 0, 0, tiled=True
    ).reshape(8, 16, SENT, 128)
    factor, inverse = factor_panel(gram, rows_total)

    segment, inverse = lax.optimization_barrier((segment, inverse))
    cross = sum_row(cross_part(segment, trail), core)
    coupling, result = residual(cross, inverse, segment, trail, rows_total)
    return factor, coupling, result


def solution(mesh):
    return jax.shard_map(
        per_device,
        mesh=mesh,
        in_specs=(
            P(("row", "col"), None),
            P(None, None, ("row", "col"), None),
            P("col", None),
            P("col", None),
            P(("row", "col"), None),
            P(("row", "col"), None),
            P(("row", "col"), None, None),
        ),
        out_specs=(P(), P("col", None), P("col", "row")),
        check_vma=False,
    )
```

```python
import functools

import jax
import jax.numpy as jnp
from jax import lax
from jax.experimental import pallas as pl
from jax.experimental.pallas import tpu as pltpu
from jax.sharding import PartitionSpec as P

ridge_value = 0.1
HIGHEST = lax.Precision.HIGHEST
F32 = jnp.float32
BF16 = jnp.bfloat16
NT = (((1,), (1,)), ((), ()))
NN = (((1,), (0,)), ((), ()))
TN = (((0,), (0,)), ((), ()))

CORE_SWAP = [(i, i ^ 1) for i in range(8)]


def y_shift(s):
    return [(2 * y + c, 2 * ((y + s) % 4) + c) for y in range(4) for c in range(2)]


def z_shift(s):
    return [(x * 4 + z, x * 4 + (z + s) % 4) for x in range(4) for z in range(4)]


def x_shift(s):
    return [(x * 4 + z, ((x + s) % 4) * 4 + z) for x in range(4) for z in range(4)]


SENT = 56
HELD = 400
UPPER = [(i, j) for i in range(4) for j in range(i, 4)]


def y_pair(f):
    return [(2 * y + c, 2 * (y ^ f) + c) for y in range(4) for c in range(2)]


def z_pair(f):
    return [(x * 4 + z, x * 4 + (z ^ f)) for x in range(4) for z in range(4)]


def x_pair(f):
    return [(x * 4 + z, (x ^ f) * 4 + z) for x in range(4) for z in range(4)]


def dot(a, b, dims, precision=None):
    return lax.dot_general(a, b, dims, precision=precision, preferred_element_type=F32)


def in_order(pieces, index):
    return jnp.concatenate(
        [lax.select_n((index - j) % 4, *pieces) for j in range(4)], axis=0
    )


def shifted(v, axis, shift):
    return [v] + [lax.ppermute(v, axis, shift(s)) for s in (1, 2, 3)]


def gather4(v, axis, shift, index):
    pieces = [v] + [lax.ppermute(v, axis, shift(s)) for s in (1, 2, 3)]
    return in_order(pieces, index)


def scatter4(v, axis, shift, index):
    n = v.shape[0] // 4
    total = lax.dynamic_slice_in_dim(v, index * n, n, 0)
    got = [
        lax.ppermute(
            lax.dynamic_slice_in_dim(v, ((index + s) % 4) * n, n, 0), axis, shift(s)
        )
        for s in (1, 2, 3)
    ]
    return total + got[0] + got[1] + got[2]


def swap_add(v, core):
    n = v.shape[0] // 2
    mine = lax.dynamic_slice_in_dim(v, core * n, n, 0)
    other = lax.dynamic_slice_in_dim(v, (1 - core) * n, n, 0)
    return mine + lax.ppermute(other, "row", CORE_SWAP)


def swap_gather(v, core):
    other = lax.ppermute(v, "row", CORE_SWAP)
    first = core == 0
    return jnp.where(first, v, other), jnp.where(first, other, v)


def sum4(v, axis, pairs):
    for flip in (1, 3):
        v = v + lax.ppermute(v, axis, pairs(flip))
    return v


def prep_kernel(
    where, count_ref, owner_ref, neighbor_ref, desc_ref, grad_ref, atoms_ref, grads_ref, mean_ref, order_ref
):
    counts = [count_ref[0, s] for s in range(8)]
    owners = [owner_ref[0, s] for s in range(8)]
    offsets = [jnp.int32(0)]
    for s in range(7):
        offsets.append(offsets[s] + counts[s])

    lane = lax.broadcasted_iota(jnp.int32, (8, 128), 1)
    struct, atom = lane >> 4, lane & 15
    count_l, offset_l = jnp.ones((8, 128), jnp.int32), jnp.zeros((8, 128), jnp.int32)
    for s in range(8):
        count_l = jnp.where(struct == s, counts[s], count_l)
        offset_l = jnp.where(struct == s, offsets[s], offset_l)
    place = jnp.where(atom < count_l, offset_l + atom, -1)
    rows = lax.broadcasted_iota(jnp.int32, (64, 128), 0)
    lanes = lax.broadcasted_iota(jnp.int32, (64, 128), 1)
    live = place[:1] == rows
    live_f = live.astype(F32)

    value = neighbor_ref[...].astype(F32)
    size = count_l.astype(F32)[:4]
    rest = value - size * jnp.floor(value / size)
    rest = jnp.where(rest < 0.0, rest + size, rest)
    rest = jnp.where(rest >= size, rest - size, rest)
    partner = rest + (16 * struct).astype(F32)[:4]

    picks = [live_f.astype(BF16)]
    for j in range(4):
        slot = jnp.sum(live_f * partner[j : j + 1], axis=1, keepdims=True)
        picks.append((slot == lanes.astype(F32)).astype(F32).astype(BF16))
    desc = desc_ref[...]
    for j in range(5):
        atoms_ref[64 * j : 64 * j + 64] = dot(picks[j], desc, NN).astype(BF16)
    for i in range(12):
        grads_ref[64 * i : 64 * i + 64] = dot(picks[0], grad_ref[i], NN).astype(BF16)

    sub8 = lax.broadcasted_iota(jnp.int32, (8, 64), 0)
    atom8 = lax.broadcasted_iota(jnp.int32, (8, 64), 1)
    low, size8 = jnp.zeros((8, 64), jnp.int32), jnp.ones((8, 64), jnp.int32)
    for s in range(8):
        low = jnp.where(sub8 == s, offsets[s], low)
        size8 = jnp.where(sub8 == s, counts[s], size8)
    inside = (atom8 >= low) & (atom8 < low + size8)
    mean_ref[...] = jnp.where(inside, 1.0 / size8.astype(F32), 0.0)

    source = 2 * where[2] + where[3]
    r = lax.broadcasted_iota(jnp.int32, (SENT, 256), 0)
    wanted = lax.broadcasted_iota(jnp.int32, (SENT, 256), 1)
    third = (r * 43) >> 7
    part = r - 3 * third
    for g in range(8):
        struct_g, count_g, offset_g = jnp.int32(0), jnp.int32(0), jnp.int32(0)
        for s in range(8):
            mine = owners[s] == g
            struct_g = jnp.where(mine, s, struct_g)
            count_g = jnp.where(mine, counts[s], count_g)
            offset_g = jnp.where(mine, offsets[s], offset_g)
        column = jnp.where((third < count_g) & (r < 48), part * 64 + offset_g + third, -1)
        column = jnp.where(r == 48 + source, 192 + struct_g, column)
        order_ref[SENT * g : SENT * g + SENT] = (column == wanted).astype(F32)


def prepare(where, count, owner, neighbors, descriptors, gradients):
    smem = pl.BlockSpec(memory_space=pltpu.SMEM)
    vmem = pl.BlockSpec(memory_space=pltpu.VMEM)
    return pl.pallas_call(
        prep_kernel,
        out_shape=(
            jax.ShapeDtypeStruct((320, 1024), BF16),
            jax.ShapeDtypeStruct((768, 1024), BF16),
            jax.ShapeDtypeStruct((8, 64), F32),
            jax.ShapeDtypeStruct((8 * SENT, 256), F32),
        ),
        in_specs=[smem, smem, smem, vmem, vmem, vmem],
        out_specs=(vmem, vmem, vmem, vmem),
        compiler_params=params(),
        cost_estimate=pl.CostEstimate(
            flops=2 * 64 * 128 * 1024 * 17, bytes_accessed=6 << 20, transcendentals=0
        ),
    )(where, count, owner, neighbors, descriptors, gradients)


def compact_rows(env, atoms, grads, mean):
    near = dot(atoms, env, NT)
    slope = dot(grads, env, NT)
    inner = near[:64]
    parts = []
    for k in range(3):
        total = near[64:128] * slope[k * 256 : k * 256 + 64]
        for j in range(1, 4):
            total = total + near[64 + j * 64 : 128 + j * 64] * slope[
                k * 256 + j * 64 : k * 256 + j * 64 + 64
            ]
        parts.append((-2.0 * total).astype(BF16))
    energy = dot(mean, inner * inner, NN, HIGHEST)
    pad = jnp.zeros((56, env.shape[0]), F32)
    parts.append(jnp.concatenate([energy, pad], axis=0).astype(BF16))
    return jnp.concatenate(parts, axis=0)


def put_env(env, where, own, other, block, at):
    core = where[3]
    env[pl.ds(pl.multiple_of(at + core * 16, 16), 16)] = own[block]
    env[pl.ds(pl.multiple_of(at + (1 - core) * 16, 16), 16)] = other[block]


def panel_kernel(
    where, own, other, atoms_ref, grads_ref, mean_ref, order_ref, near_ref, far_ref, gram_ref, env
):
    x, z, y, core = where[0], where[1], where[2], where[3]
    for i in range(4):
        for j in range(4):
            place = ((x - i) & 3) * 4 + ((z - j) & 3)
            put_env(env, where, own, other, (i, j), place * 32)
    rows = compact_rows(env[...], atoms_ref[...], grads_ref[...], mean_ref[...])
    full = dot(order_ref[...].astype(BF16), rows, NN)
    first = core == 0
    for i in range(4):
        at = 2 * SENT * i
        low, high = full[at : at + SENT], full[at + SENT : at + 2 * SENT]
        s = (i - y) & 3
        near_ref[s] = jnp.where(first, low, high).astype(BF16)
        far_ref[s] = jnp.where(first, high, low).astype(BF16)
    gram = dot(rows, rows, TN)
    for n, (i, j) in enumerate(UPPER):
        gram_ref[128 * n : 128 * n + 128] = gram[
            128 * i : 128 * i + 128, 128 * j : 128 * j + 128
        ]


def trail_kernel(
    where, own, other, atoms_ref, grads_ref, mean_ref, order_ref, out_ref, env
):
    z, y = where[1], where[2]
    for j in range(4):
        place = ((z - j) & 3) * 128
        for s in range(4):
            put_env(env, where, own, other, (s, 0, j), place + ((y - s) & 3) * 32)
    rows = compact_rows(env[...], atoms_ref[...], grads_ref[...], mean_ref[...])
    full = dot(order_ref[...].astype(BF16), rows, NN)
    for c in range(out_ref.shape[1]):
        part = full[:, c * 128 : c * 128 + 128].reshape(8, SENT, 128)
        out_ref[:, c] = part.astype(BF16)


def assemble_kernel(where, near, far, got1, got2, got3, out):
    y, core = where[2], where[3]
    blocks = [(near, 0, 0, core), (far, 0, 0, 1 - core)]
    for s, got in ((1, got1), (2, got2), (3, got3)):
        blocks += [(got, 0, s, core), (got, 1, s, 1 - core)]
    energy = jnp.zeros((8, out.shape[1]), F32)
    for ref, i, s, c in blocks:
        at = (2 * ((y - s) & 3) + c) * 48
        out[pl.ds(pl.multiple_of(at, 16), 48)] = ref[i, :48]
        energy = energy + ref[i, 48:].astype(F32)
    out[384:] = jnp.concatenate([energy, jnp.zeros_like(energy)], axis=0).astype(BF16)


def trail_chunk(ref, i):
    rows = [ref[r, i, :48].astype(F32) for r in range(8)]
    energy = ref[0, i, 48:].astype(F32)
    for r in range(1, 8):
        energy = energy + ref[r, i, 48:].astype(F32)
    return jnp.concatenate(rows + [energy, jnp.zeros_like(energy)], axis=0).astype(BF16)


def params(mib=40):
    return pltpu.CompilerParams(vmem_limit_bytes=mib << 20)


def in_smem():
    return pl.BlockSpec(memory_space=pltpu.SMEM)


def in_vmem():
    return pl.BlockSpec(memory_space=pltpu.VMEM)


def panel_rows(where, own, other, atoms, grads, mean, order):
    return pl.pallas_call(
        panel_kernel,
        out_shape=(
            jax.ShapeDtypeStruct((4, SENT, 512), BF16),
            jax.ShapeDtypeStruct((4, SENT, 512), BF16),
            jax.ShapeDtypeStruct((1280, 128), F32),
        ),
        in_specs=[in_smem()] + [in_vmem()] * 6,
        out_specs=(in_vmem(),) * 3,
        scratch_shapes=[pltpu.VMEM((512, 1024), BF16)],
        compiler_params=params(),
        cost_estimate=pl.CostEstimate(
            flops=2 * 512 * 1024 * 1088, bytes_accessed=5 << 20, transcendentals=0
        ),
    )(where, own, other, atoms, grads, mean, order)


def assemble(where, near, far, got):
    return pl.pallas_call(
        assemble_kernel,
        out_shape=jax.ShapeDtypeStruct((HELD, 512), BF16),
        in_specs=[in_smem()] + [in_vmem()] * 5,
        out_specs=in_vmem(),
        compiler_params=params(),
        cost_estimate=pl.CostEstimate(flops=0, bytes_accessed=1 << 20, transcendentals=0),
    )(where, near, far, *got)


def trail_rows(where, own, other, atoms, grads, mean, order):
    piece = pl.BlockSpec((4, 1, 4, 16, 1024), lambda i, w: (0, i, 0, 0, 0))
    whole = lambda shape: pl.BlockSpec(shape, lambda i, w: (0, 0))
    return pl.pallas_call(
        trail_kernel,
        out_shape=jax.ShapeDtypeStruct((8, 16, SENT, 128), BF16),
        grid_spec=pltpu.PrefetchScalarGridSpec(
            num_scalar_prefetch=1,
            grid=(4,),
            in_specs=[piece] * 2
            + [
                whole(atoms.shape),
                whole(grads.shape),
                whole(mean.shape),
                whole(order.shape),
            ],
            out_specs=pl.BlockSpec((8, 4, SENT, 128), lambda i, w: (0, (w[0] - i) & 3, 0, 0)),
            scratch_shapes=[pltpu.VMEM((512, 1024), BF16)],
        ),
        compiler_params=params(),
        cost_estimate=pl.CostEstimate(
            flops=2 * 2048 * 1024 * 1088, bytes_accessed=9 << 20, transcendentals=0
        ),
    )(where, own, other, atoms, grads, mean, order)


def eliminate(a):
    lanes = lax.broadcasted_iota(jnp.int32, (8, 128), 1)
    subs = lax.broadcasted_iota(jnp.int32, (8, 128), 0)
    left = [a[8 * g : 8 * g + 8] for g in range(16)]
    right = [(lanes == subs + 8 * g).astype(F32) for g in range(16)]
    done = []
    for p in range(16):
        count = 16 - p
        cols = [
            [
                jnp.broadcast_to(left[g][:, 8 * p + q : 8 * p + q + 1], (8, 128))
                for g in range(count)
            ]
            for q in range(8)
        ]
        pivots = jnp.ones((8, 128), F32)
        for q in range(8):
            pivot = cols[q][0][q : q + 1]
            inverse = 1.0 / pivot
            pivots = jnp.where(subs == q, pivot, pivots)
            ratio = [c * inverse for c in cols[q]]
            ratio[0] = jnp.where(subs > q, ratio[0], 0.0)
            for t in range(q + 1, 8):
                here = cols[t][0][q : q + 1]
                for g in range(count):
                    cols[t][g] = cols[t][g] - ratio[g] * here
            row_left = left[0][q : q + 1]
            row_right = right[0][q : q + 1]
            for g in range(count):
                left[g] = left[g] - ratio[g] * row_left
                right[g] = right[g] - ratio[g] * row_right
        done.append(right[0] * lax.rsqrt(pivots))
        left, right = left[1:], right[1:]
    return jnp.concatenate(done, axis=0)


def factor_kernel(rows_total, gram_ref, factor_ref, inverse_ref, work):
    n = factor_ref.shape[0]
    r = lax.broadcasted_iota(jnp.int32, (n, n), 0)
    c = lax.broadcasted_iota(jnp.int32, (n, n), 1)
    same = r[:128, :128] == c[:128, :128]
    work[:, :n] = jnp.zeros((n, n), F32)
    for m, (i, j) in enumerate(UPPER):
        block = gram_ref[128 * m : 128 * m + 128] / rows_total
        if i == j:
            block = block + jnp.where(same, ridge_value, 0.0)
        work[128 * i : 128 * i + 128, 128 * j : 128 * j + 128] = block
    work[:, n:] = jnp.where(r == c, 1.0, 0.0)

    def step(b, carry):
        at = pl.multiple_of(b * 128, 128)
        low = eliminate(work[pl.ds(at, 128), pl.ds(at, 128)])
        row = dot(low, work[pl.ds(at, 128), :], NN, HIGHEST)
        lane = lax.broadcasted_iota(jnp.int32, (128, n), 1)
        later = jnp.where(lane >= at + 128, row[:, :n], 0.0)
        work[...] = work[...] - dot(later, row, TN, HIGHEST)
        work[pl.ds(at, 128), :] = row
        return carry

    lax.fori_loop(0, n // 128, step, 0)
    factor_ref[...] = jnp.where(c >= r, work[:, :n], 0.0)
    inverse_ref[...] = jnp.where(c <= r, work[:, n:], 0.0)


def factor_panel(gram, rows_total):
    n = 512
    return pl.pallas_call(
        functools.partial(factor_kernel, float(rows_total)),
        out_shape=(jax.ShapeDtypeStruct((n, n), F32), jax.ShapeDtypeStruct((n, n), F32)),
        scratch_shapes=[pltpu.VMEM((n, 2 * n), F32)],
        compiler_params=params(),
        cost_estimate=pl.CostEstimate(
            flops=20 * n * n * n, bytes_accessed=4 << 20, transcendentals=n
        ),
    )(gram)


def cross_kernel(panel_ref, trail_ref, out_ref):
    @pl.when(pl.program_id(0) == 0)
    def _():
        out_ref[...] = jnp.zeros_like(out_ref)

    n = panel_ref.shape[2]
    trail = jnp.concatenate(
        [trail_chunk(trail_ref, i) for i in range(panel_ref.shape[0])], axis=0
    )
    out_ref[...] += dot(trail, panel_ref[...].reshape(-1, n), TN)


def cross_part(segment, trail):
    n = segment.shape[2]
    return pl.pallas_call(
        cross_kernel,
        out_shape=jax.ShapeDtypeStruct((128, n), F32),
        grid=(segment.shape[0] // 4,),
        in_specs=[
            pl.BlockSpec((4, HELD, n), lambda i: (i, 0, 0)),
            pl.BlockSpec((8, 4, SENT, 128), lambda i: (0, i, 0, 0)),
        ],
        out_specs=pl.BlockSpec((128, n), lambda i: (0, 0)),
        compiler_params=params(),
        cost_estimate=pl.CostEstimate(
            flops=2 * 128 * n * 8192, bytes_accessed=11 << 20, transcendentals=0
        ),
    )(segment, trail)


def residual_kernel(
    rows_total, cross_ref, inverse_ref, panel_ref, trail_ref, coupling_ref, out_ref, weights, spread
):
    @pl.when(pl.program_id(0) == 0)
    def _():
        coupling = dot(cross_ref[...] / rows_total, inverse_ref[...], NT, HIGHEST)
        coupling_ref[...] = coupling
        solved = dot(coupling, inverse_ref[...], NN, HIGHEST)
        high = solved.astype(BF16)
        weights[:128] = high
        weights[128:] = (solved - high.astype(F32)).astype(BF16)
        held = lax.broadcasted_iota(jnp.int32, (HELD, 512), 0)
        column = lax.broadcasted_iota(jnp.int32, (HELD, 512), 1)
        struct, place = column >> 6, column & 63
        wanted = jnp.where(place <= 48, struct * 48 + place - 1, -1)
        wanted = jnp.where(place == 0, 384 + struct, wanted)
        spread[...] = (held == wanted).astype(F32).astype(BF16)

    r = lax.broadcasted_iota(jnp.int32, (128, 128), 0)
    c = lax.broadcasted_iota(jnp.int32, (128, 128), 1)
    same = (r == c).astype(BF16)
    for i in range(panel_ref.shape[0]):
        both = dot(weights[...], panel_ref[i], NT)
        own = dot(same, trail_chunk(trail_ref, i), NT)
        rest = own - both[:128] - both[128:]
        high = rest.astype(BF16)
        low = (rest - high.astype(F32)).astype(BF16)
        full = dot(jnp.concatenate([high, low], axis=0), spread[...], NN)
        out_ref[:, i * 512 : i * 512 + 512] = full[:128] + full[128:]


def residual(cross, inverse, segment, trail, rows_total):
    n = inverse.shape[0]
    chunks = segment.shape[0]
    whole = lambda shape: pl.BlockSpec(shape, lambda i: (0, 0))
    return pl.pallas_call(
        functools.partial(residual_kernel, float(rows_total)),
        out_shape=(
            jax.ShapeDtypeStruct((128, n), F32),
            jax.ShapeDtypeStruct((128, 512 * chunks), F32),
        ),
        grid=(chunks // 4,),
        in_specs=[
            whole((128, n)),
            whole((n, n)),
            pl.BlockSpec((4, HELD, n), lambda i: (i, 0, 0)),
            pl.BlockSpec((8, 4, SENT, 128), lambda i: (0, i, 0, 0)),
        ],
        out_specs=(whole((128, n)), pl.BlockSpec((128, 2048), lambda i: (0, i))),
        scratch_shapes=[pltpu.VMEM((256, n), BF16), pltpu.VMEM((HELD, 512), BF16)],
        compiler_params=params(),
        cost_estimate=pl.CostEstimate(
            flops=4 * 128 * n * 8192, bytes_accessed=16 << 20, transcendentals=0
        ),
    )(cross, inverse, segment, trail)


def sum_row(v, core):
    v = sum4(swap_add(v, core), "row", y_pair)
    return jnp.concatenate(swap_gather(v, core), axis=0)


def per_device(
    descriptors, gradients, sparse_panel, sparse_trail, atom_counts, owner_rows, neighbor_ids
):
    row = lax.axis_index("row")
    col = lax.axis_index("col")
    core, y = row % 2, row // 2
    x, z = col // 4, col % 4
    rows_total = 65536

    where = jnp.stack([x, z, y, core]).astype(jnp.int32)

    piece = jnp.concatenate(
        [
            lax.dynamic_slice_in_dim(sparse_panel, core * 16, 16, 0),
            lax.dynamic_slice_in_dim(sparse_trail, row * 16, 16, 0),
        ],
        axis=0,
    )
    pieces = shifted(piece, "col", z_shift)
    piece = jnp.stack([p[:16] for p in pieces])
    piece_trail = jnp.stack([p[16:] for p in pieces])
    own = jnp.stack(shifted(piece, "col", x_shift))
    own, piece_trail = lax.optimization_barrier((own, piece_trail))
    other = lax.ppermute(own, "row", CORE_SWAP)
    own_trail = jnp.stack(shifted(piece_trail, "col", x_shift))

    atoms, grads, mean, order = prepare(
        where,
        atom_counts,
        owner_rows,
        neighbor_ids.reshape(128, 4).T,
        descriptors,
        gradients.reshape(12, 128, 1024),
    )

    near, far, gram = panel_rows(where, own, other, atoms, grads, mean, order)
    far = lax.ppermute(far, "row", CORE_SWAP)
    gram = swap_add(gram, core)
    far, gram, own_trail = lax.optimization_barrier((far, gram, own_trail))
    got = [
        lax.ppermute(jnp.stack([near[s], far[s]]), "row", y_shift(s)) for s in (1, 2, 3)
    ]
    gram = scatter4(gram, "row", y_shift, y)
    got, gram, own_trail = lax.optimization_barrier((got, gram, own_trail))
    panel = assemble(where, near, far, got)
    segment = lax.all_gather(panel, "col", axis=0, tiled=False)
    trail_own = jnp.stack(shifted(own_trail, "row", y_shift))
    gram = sum4(gram, "col", z_pair)
    gram = sum4(gram, "col", x_pair)
    trail_own, gram = lax.optimization_barrier((trail_own, gram))
    trail_other = lax.ppermute(trail_own, "row", CORE_SWAP)
    trail = trail_rows(where, trail_own, trail_other, atoms, grads, mean, order)
    gram = gather4(gram, "row", y_shift, y)
    gram = jnp.concatenate(swap_gather(gram, core), axis=0)
    trail, gram = lax.optimization_barrier((trail, gram))
    trail = lax.all_to_all(
        trail.reshape(128, SENT, 128), ("row", "col"), 0, 0, tiled=True
    ).reshape(8, 16, SENT, 128)
    factor, inverse = factor_panel(gram, rows_total)

    segment, inverse = lax.optimization_barrier((segment, inverse))
    cross = sum_row(cross_part(segment, trail), core)
    coupling, result = residual(cross, inverse, segment, trail, rows_total)
    return factor, coupling, result


def solution(mesh):
    return jax.shard_map(
        per_device,
        mesh=mesh,
        in_specs=(
            P(("row", "col"), None),
            P(None, None, ("row", "col"), None),
            P("col", None),
            P("col", None),
            P(("row", "col"), None),
            P(("row", "col"), None),
            P(("row", "col"), None, None),
        ),
        out_specs=(P(), P("col", None), P("col", "row")),
        check_vma=False,
    )
```

```python
import functools

import jax
import jax.numpy as jnp
from jax import lax
from jax.experimental import pallas as pl
from jax.experimental.pallas import tpu as pltpu
from jax.sharding import PartitionSpec as P

ridge_value = 0.1
HIGHEST = lax.Precision.HIGHEST
F32 = jnp.float32
BF16 = jnp.bfloat16
NT = (((1,), (1,)), ((), ()))
NN = (((1,), (0,)), ((), ()))
TN = (((0,), (0,)), ((), ()))

CORE_SWAP = [(i, i ^ 1) for i in range(8)]


def y_shift(s):
    return [(2 * y + c, 2 * ((y + s) % 4) + c) for y in range(4) for c in range(2)]


def z_shift(s):
    return [(x * 4 + z, x * 4 + (z + s) % 4) for x in range(4) for z in range(4)]


def x_shift(s):
    return [(x * 4 + z, ((x + s) % 4) * 4 + z) for x in range(4) for z in range(4)]


SENT = 56
FIRST, SECOND = 208, 192
HELD = FIRST + SECOND
UPPER = [(i, j) for i in range(4) for j in range(i, 4)]


def y_pair(f):
    return [(2 * y + c, 2 * (y ^ f) + c) for y in range(4) for c in range(2)]


def z_pair(f):
    return [(x * 4 + z, x * 4 + (z ^ f)) for x in range(4) for z in range(4)]


def x_pair(f):
    return [(x * 4 + z, (x ^ f) * 4 + z) for x in range(4) for z in range(4)]


def dot(a, b, dims, precision=None):
    return lax.dot_general(a, b, dims, precision=precision, preferred_element_type=F32)


def in_order(pieces, index):
    return jnp.concatenate(
        [lax.select_n((index - j) % 4, *pieces) for j in range(4)], axis=0
    )


def shifted(v, axis, shift):
    return [v] + [lax.ppermute(v, axis, shift(s)) for s in (1, 2, 3)]


def gather4(v, axis, shift, index):
    pieces = [v] + [lax.ppermute(v, axis, shift(s)) for s in (1, 2, 3)]
    return in_order(pieces, index)


def scatter4(v, axis, shift, index):
    n = v.shape[0] // 4
    total = lax.dynamic_slice_in_dim(v, index * n, n, 0)
    got = [
        lax.ppermute(
            lax.dynamic_slice_in_dim(v, ((index + s) % 4) * n, n, 0), axis, shift(s)
        )
        for s in (1, 2, 3)
    ]
    return total + got[0] + got[1] + got[2]


def swap_add(v, core):
    n = v.shape[0] // 2
    mine = lax.dynamic_slice_in_dim(v, core * n, n, 0)
    other = lax.dynamic_slice_in_dim(v, (1 - core) * n, n, 0)
    return mine + lax.ppermute(other, "row", CORE_SWAP)


def swap_gather(v, core):
    other = lax.ppermute(v, "row", CORE_SWAP)
    first = core == 0
    return jnp.where(first, v, other), jnp.where(first, other, v)


def ring(v, axis, shift):
    cut = v.shape[0] // 2
    one = lax.ppermute(v, axis, shift(1))
    three = lax.ppermute(v, axis, shift(3))
    low = lax.ppermute(one[:cut], axis, shift(1))
    high = lax.ppermute(three[cut:], axis, shift(3))
    return one, low, high, three


def ring_stack(v, axis, shift):
    one, low, high, three = ring(v, axis, shift)
    return jnp.stack([v, one, jnp.concatenate([low, high], axis=0), three])


def sum4(v, axis, pairs):
    for flip in (1, 3):
        v = v + lax.ppermute(v, axis, pairs(flip))
    return v


def prep_kernel(
    where, count_ref, owner_ref, neighbor_ref, desc_ref, grad_ref, atoms_ref, grads_ref, mean_ref, order_ref
):
    counts = [count_ref[0, s] for s in range(8)]
    owners = [owner_ref[0, s] for s in range(8)]
    offsets = [jnp.int32(0)]
    for s in range(7):
        offsets.append(offsets[s] + counts[s])

    lane = lax.broadcasted_iota(jnp.int32, (8, 128), 1)
    struct, atom = lane >> 4, lane & 15
    count_l, offset_l = jnp.ones((8, 128), jnp.int32), jnp.zeros((8, 128), jnp.int32)
    for s in range(8):
        count_l = jnp.where(struct == s, counts[s], count_l)
        offset_l = jnp.where(struct == s, offsets[s], offset_l)
    place = jnp.where(atom < count_l, offset_l + atom, -1)
    rows = lax.broadcasted_iota(jnp.int32, (64, 128), 0)
    lanes = lax.broadcasted_iota(jnp.int32, (64, 128), 1)
    live = place[:1] == rows
    live_f = live.astype(F32)

    value = neighbor_ref[...].astype(F32)
    size = count_l.astype(F32)[:4]
    rest = value - size * jnp.floor(value / size)
    rest = jnp.where(rest < 0.0, rest + size, rest)
    rest = jnp.where(rest >= size, rest - size, rest)
    partner = rest + (16 * struct).astype(F32)[:4]

    picks = [live_f.astype(BF16)]
    for j in range(4):
        slot = jnp.sum(live_f * partner[j : j + 1], axis=1, keepdims=True)
        picks.append((slot == lanes.astype(F32)).astype(F32).astype(BF16))
    desc = desc_ref[...]
    for j in range(5):
        atoms_ref[64 * j : 64 * j + 64] = dot(picks[j], desc, NN).astype(BF16)
    for i in range(12):
        grads_ref[64 * i : 64 * i + 64] = dot(picks[0], grad_ref[i], NN).astype(BF16)

    sub8 = lax.broadcasted_iota(jnp.int32, (8, 64), 0)
    atom8 = lax.broadcasted_iota(jnp.int32, (8, 64), 1)
    low, size8 = jnp.zeros((8, 64), jnp.int32), jnp.ones((8, 64), jnp.int32)
    for s in range(8):
        low = jnp.where(sub8 == s, offsets[s], low)
        size8 = jnp.where(sub8 == s, counts[s], size8)
    inside = (atom8 >= low) & (atom8 < low + size8)
    mean_ref[...] = jnp.where(inside, 1.0 / size8.astype(F32), 0.0)

    source = 2 * where[2] + where[3]
    r = lax.broadcasted_iota(jnp.int32, (SENT, 256), 0)
    wanted = lax.broadcasted_iota(jnp.int32, (SENT, 256), 1)
    third = (r * 43) >> 7
    part = r - 3 * third
    for g in range(8):
        struct_g, count_g, offset_g = jnp.int32(0), jnp.int32(0), jnp.int32(0)
        for s in range(8):
            mine = owners[s] == g
            struct_g = jnp.where(mine, s, struct_g)
            count_g = jnp.where(mine, counts[s], count_g)
            offset_g = jnp.where(mine, offsets[s], offset_g)
        column = jnp.where((third < count_g) & (r < 48), part * 64 + offset_g + third, -1)
        column = jnp.where(r == 48 + source, 192 + struct_g, column)
        order_ref[SENT * g : SENT * g + SENT] = (column == wanted).astype(F32)


def prepare(where, count, owner, neighbors, descriptors, gradients):
    smem = pl.BlockSpec(memory_space=pltpu.SMEM)
    vmem = pl.BlockSpec(memory_space=pltpu.VMEM)
    return pl.pallas_call(
        prep_kernel,
        out_shape=(
            jax.ShapeDtypeStruct((320, 1024), BF16),
            jax.ShapeDtypeStruct((768, 1024), BF16),
            jax.ShapeDtypeStruct((8, 64), F32),
            jax.ShapeDtypeStruct((8 * SENT, 256), F32),
        ),
        in_specs=[smem, smem, smem, vmem, vmem, vmem],
        out_specs=(vmem, vmem, vmem, vmem),
        compiler_params=params(),
        cost_estimate=pl.CostEstimate(
            flops=2 * 64 * 128 * 1024 * 17, bytes_accessed=6 << 20, transcendentals=0
        ),
    )(where, count, owner, neighbors, descriptors, gradients)


def compact_rows(env, atoms, grads, mean):
    near = dot(atoms, env, NT)
    slope = dot(grads, env, NT)
    inner = near[:64]
    parts = []
    for k in range(3):
        total = near[64:128] * slope[k * 256 : k * 256 + 64]
        for j in range(1, 4):
            total = total + near[64 + j * 64 : 128 + j * 64] * slope[
                k * 256 + j * 64 : k * 256 + j * 64 + 64
            ]
        parts.append((-2.0 * total).astype(BF16))
    energy = dot(mean, inner * inner, NN, HIGHEST)
    pad = jnp.zeros((56, env.shape[0]), F32)
    parts.append(jnp.concatenate([energy, pad], axis=0).astype(BF16))
    return jnp.concatenate(parts, axis=0)


def put_env(env, where, own, other, block, at):
    core = where[3]
    env[pl.ds(pl.multiple_of(at + core * 16, 16), 16)] = own[block]
    env[pl.ds(pl.multiple_of(at + (1 - core) * 16, 16), 16)] = other[block]


def panel_kernel(
    where, own, other, atoms_ref, grads_ref, mean_ref, order_ref, near_ref, far_ref, gram_ref, env
):
    x, z, y, core = where[0], where[1], where[2], where[3]
    for i in range(4):
        for j in range(4):
            place = ((x - i) & 3) * 4 + ((z - j) & 3)
            put_env(env, where, own, other, (i, j), place * 32)
    rows = compact_rows(env[...], atoms_ref[...], grads_ref[...], mean_ref[...])
    full = dot(order_ref[...].astype(BF16), rows, NN)
    first = core == 0
    for i in range(4):
        at = 2 * SENT * i
        low, high = full[at : at + SENT], full[at + SENT : at + 2 * SENT]
        s = (i - y) & 3
        near_ref[s] = jnp.where(first, low, high).astype(BF16)
        far_ref[s] = jnp.where(first, high, low).astype(BF16)
    gram = dot(rows, rows, TN)
    for n, (i, j) in enumerate(UPPER):
        gram_ref[128 * n : 128 * n + 128] = gram[
            128 * i : 128 * i + 128, 128 * j : 128 * j + 128
        ]


def trail_kernel(
    where, own_ref, other_ref, atoms_ref, grads_ref, mean_ref, order_ref, out_ref
):
    first = where[3] == 0
    own, other = own_ref[...], other_ref[...]
    low, high = jnp.where(first, own, other), jnp.where(first, other, own)
    env = jnp.concatenate([low, high], axis=1).reshape(-1, 1024)
    rows = compact_rows(env, atoms_ref[...], grads_ref[...], mean_ref[...])
    full = dot(order_ref[...].astype(BF16), rows, NN)
    for c in range(out_ref.shape[1]):
        part = full[:, c * 128 : c * 128 + 128].reshape(8, SENT, 128)
        out_ref[:, c] = part.astype(BF16)


def assemble_kernel(where, near, far, got1, got2, got3, first, second):
    y, core = where[2], where[3]
    blocks = [(near, 0, 0, core), (far, 0, 0, 1 - core)]
    for s, got in ((1, got1), (2, got2), (3, got3)):
        blocks += [(got, 0, s, core), (got, 1, s, 1 - core)]
    energy = jnp.zeros((8, first.shape[1]), F32)
    for ref, i, s, c in blocks:
        source = 2 * ((y - s) & 3) + c
        at = pl.ds(pl.multiple_of((source & 3) * 48, 16), 48)

        @pl.when(source < 4)
        def _(ref=ref, i=i, at=at):
            first[at] = ref[i, :48]

        @pl.when(source >= 4)
        def _(ref=ref, i=i, at=at):
            second[at] = ref[i, :48]

        energy = energy + ref[i, 48:].astype(F32)
    first[192:] = jnp.concatenate([energy, jnp.zeros_like(energy)], axis=0).astype(BF16)


def trail_first(ref, c):
    rows = [ref[r, c, :48].astype(F32) for r in range(4)]
    energy = ref[0, c, 48:].astype(F32)
    for r in range(1, 8):
        energy = energy + ref[r, c, 48:].astype(F32)
    return jnp.concatenate(rows + [energy, jnp.zeros_like(energy)], axis=0).astype(BF16)


def trail_second(ref, c):
    return jnp.concatenate([ref[r, c, :48] for r in range(4, 8)], axis=0)


def params(mib=40):
    return pltpu.CompilerParams(vmem_limit_bytes=mib << 20)


def in_smem():
    return pl.BlockSpec(memory_space=pltpu.SMEM)


def in_vmem():
    return pl.BlockSpec(memory_space=pltpu.VMEM)


def panel_rows(where, own, other, atoms, grads, mean, order):
    return pl.pallas_call(
        panel_kernel,
        out_shape=(
            jax.ShapeDtypeStruct((4, SENT, 512), BF16),
            jax.ShapeDtypeStruct((4, SENT, 512), BF16),
            jax.ShapeDtypeStruct((1280, 128), F32),
        ),
        in_specs=[in_smem()] + [in_vmem()] * 6,
        out_specs=(in_vmem(),) * 3,
        scratch_shapes=[pltpu.VMEM((512, 1024), BF16)],
        compiler_params=params(),
        cost_estimate=pl.CostEstimate(
            flops=2 * 512 * 1024 * 1088, bytes_accessed=5 << 20, transcendentals=0
        ),
    )(where, own, other, atoms, grads, mean, order)


def assemble(where, near, far, got):
    return pl.pallas_call(
        assemble_kernel,
        out_shape=(
            jax.ShapeDtypeStruct((FIRST, 512), BF16),
            jax.ShapeDtypeStruct((SECOND, 512), BF16),
        ),
        in_specs=[in_smem()] + [in_vmem()] * 5,
        out_specs=(in_vmem(), in_vmem()),
        compiler_params=params(),
        cost_estimate=pl.CostEstimate(flops=0, bytes_accessed=1 << 20, transcendentals=0),
    )(where, near, far, *got)


def trail_rows(where, own, other, atoms, grads, mean, order):
    blocks = own.shape[0]
    step = 4
    half = pl.BlockSpec((step, 64, 1024), lambda i, w: (i, 0, 0))
    whole = lambda shape: pl.BlockSpec(shape, lambda i, w: (0, 0))
    return pl.pallas_call(
        trail_kernel,
        out_shape=jax.ShapeDtypeStruct((8, blocks, SENT, 128), BF16),
        grid_spec=pltpu.PrefetchScalarGridSpec(
            num_scalar_prefetch=1,
            grid=(blocks // step,),
            in_specs=[
                half,
                half,
                whole(atoms.shape),
                whole(grads.shape),
                whole(mean.shape),
                whole(order.shape),
            ],
            out_specs=pl.BlockSpec((8, step, SENT, 128), lambda i, w: (0, i, 0, 0)),
        ),
        compiler_params=params(),
        cost_estimate=pl.CostEstimate(
            flops=2 * 2048 * 1024 * 1088, bytes_accessed=9 << 20, transcendentals=0
        ),
    )(where, own, other, atoms, grads, mean, order)


def eliminate(a):
    lanes = lax.broadcasted_iota(jnp.int32, (8, 128), 1)
    subs = lax.broadcasted_iota(jnp.int32, (8, 128), 0)
    left = [a[8 * g : 8 * g + 8] for g in range(16)]
    right = [(lanes == subs + 8 * g).astype(F32) for g in range(16)]
    done = []
    for p in range(16):
        count = 16 - p
        cols = [
            [
                jnp.broadcast_to(left[g][:, 8 * p + q : 8 * p + q + 1], (8, 128))
                for g in range(count)
            ]
            for q in range(8)
        ]
        pivots = jnp.ones((8, 128), F32)
        for q in range(8):
            pivot = cols[q][0][q : q + 1]
            inverse = 1.0 / pivot
            pivots = jnp.where(subs == q, pivot, pivots)
            ratio = [c * inverse for c in cols[q]]
            ratio[0] = jnp.where(subs > q, ratio[0], 0.0)
            for t in range(q + 1, 8):
                here = cols[t][0][q : q + 1]
                for g in range(count):
                    cols[t][g] = cols[t][g] - ratio[g] * here
            row_left = left[0][q : q + 1]
            row_right = right[0][q : q + 1]
            for g in range(count):
                left[g] = left[g] - ratio[g] * row_left
                right[g] = right[g] - ratio[g] * row_right
        done.append(right[0] * lax.rsqrt(pivots))
        left, right = left[1:], right[1:]
    return jnp.concatenate(done, axis=0)


def factor_kernel(rows_total, gram_ref, factor_ref, inverse_ref, work):
    n = factor_ref.shape[0]
    r = lax.broadcasted_iota(jnp.int32, (n, n), 0)
    c = lax.broadcasted_iota(jnp.int32, (n, n), 1)
    same = r[:128, :128] == c[:128, :128]
    work[:, :n] = jnp.zeros((n, n), F32)
    for m, (i, j) in enumerate(UPPER):
        block = gram_ref[128 * m : 128 * m + 128] / rows_total
        if i == j:
            block = block + jnp.where(same, ridge_value, 0.0)
        work[128 * i : 128 * i + 128, 128 * j : 128 * j + 128] = block
    work[:, n:] = jnp.where(r == c, 1.0, 0.0)

    def step(b, carry):
        at = pl.multiple_of(b * 128, 128)
        low = eliminate(work[pl.ds(at, 128), pl.ds(at, 128)])
        for k in range(n // 128):

            @pl.when(b == k)
            def _(k=k):
                here, after = slice(128 * k, 128 * k + 128), slice(128 * k + 128, n)
                left, right = slice(128 * k, n), slice(n, n + 128 * k + 128)
                row = dot(low, work[here, left], NN, HIGHEST)
                solved = dot(low, work[here, right], NN, HIGHEST)
                work[here, left] = row
                work[here, right] = solved
                if k < n // 128 - 1:
                    later = row[:, 128:]
                    work[after, after] -= dot(later, later, TN, HIGHEST)
                    work[after, right] -= dot(later, solved, TN, HIGHEST)

        return carry

    lax.fori_loop(0, n // 128, step, 0)
    factor_ref[...] = jnp.where(c >= r, work[:, :n], 0.0)
    inverse_ref[...] = jnp.where(c <= r, work[:, n:], 0.0)


def factor_panel(gram, rows_total):
    n = 512
    return pl.pallas_call(
        functools.partial(factor_kernel, float(rows_total)),
        out_shape=(jax.ShapeDtypeStruct((n, n), F32), jax.ShapeDtypeStruct((n, n), F32)),
        scratch_shapes=[pltpu.VMEM((n, 2 * n), F32)],
        compiler_params=params(),
        cost_estimate=pl.CostEstimate(
            flops=20 * n * n * n, bytes_accessed=4 << 20, transcendentals=n
        ),
    )(gram)


def chunk_place(where, i, j):
    return ((where[0] - i) & 3) * 4 + ((where[1] - j) & 3)


def first_pieces(refs):
    own, one, low, high, three = refs
    rows = [[(own, j) for j in range(4)], [(one, j) for j in range(4)]]
    rows.append([(low, 0), (low, 1), (high, 0), (high, 1)])
    return rows + [[(three, j) for j in range(4)]]


def second_pieces(refs):
    turned = first_pieces(refs)
    return [[turned[j][i] for j in range(4)] for i in range(4)]


def cross_kernel(where, *refs):
    first, second = first_pieces(refs[:5]), second_pieces(refs[5:10])
    trail_ref, out_ref = refs[10], refs[11]
    total = jnp.zeros(out_ref.shape, F32)
    for i in range(4):
        for j in range(4):
            c = chunk_place(where, i, j)
            ref, at = first[i][j]
            total = total + dot(trail_first(trail_ref, c), ref[at], TN)
            ref, at = second[i][j]
            total = total + dot(trail_second(trail_ref, c), ref[at], TN)
    out_ref[...] = total


def cross_part(where, segment, trail):
    n = 512
    return pl.pallas_call(
        cross_kernel,
        out_shape=jax.ShapeDtypeStruct((128, n), F32),
        in_specs=[in_smem()] + [in_vmem()] * 11,
        out_specs=in_vmem(),
        compiler_params=params(),
        cost_estimate=pl.CostEstimate(
            flops=2 * 128 * n * 6400, bytes_accessed=9 << 20, transcendentals=0
        ),
    )(where, *segment, trail)


def residual_kernel(rows_total, where, cross_ref, inverse_ref, *refs):
    first, second = first_pieces(refs[:5]), second_pieces(refs[5:10])
    trail_ref, coupling_ref, out_ref, weights, spread = refs[10:]

    @pl.when(pl.program_id(0) == 0)
    def _():
        coupling = dot(cross_ref[...] / rows_total, inverse_ref[...], NT, HIGHEST)
        coupling_ref[...] = coupling
        solved = dot(coupling, inverse_ref[...], NN, HIGHEST)
        high = solved.astype(BF16)
        weights[:128] = high
        weights[128:] = (solved - high.astype(F32)).astype(BF16)
        held = lax.broadcasted_iota(jnp.int32, (HELD, 512), 0)
        column = lax.broadcasted_iota(jnp.int32, (HELD, 512), 1)
        struct, place = column >> 6, column & 63
        wanted = jnp.where(place <= 48, struct * 48 + place - 1, -1)
        wanted = jnp.where((place <= 48) & (struct >= 4), wanted + 16, wanted)
        wanted = jnp.where(place == 0, 192 + struct, wanted)
        spread[...] = (held == wanted).astype(F32).astype(BF16)

    r = lax.broadcasted_iota(jnp.int32, (128, 128), 0)
    c = lax.broadcasted_iota(jnp.int32, (128, 128), 1)
    same = (r == c).astype(BF16)

    def piece(panel, trail):
        both = dot(weights[...], panel, NT)
        rest = dot(same, trail, NT) - both[:128] - both[128:]
        high = rest.astype(BF16)
        low = (rest - high.astype(F32)).astype(BF16)
        return jnp.concatenate([high, low], axis=0)

    for i in range(4):

        @pl.when(pl.program_id(0) == i)
        def _(i=i):
            for j in range(4):
                c = chunk_place(where, i, j)
                ref, at = first[i][j]
                full = dot(piece(ref[at], trail_first(trail_ref, c)), spread[:FIRST], NN)
                ref, at = second[i][j]
                full = full + dot(
                    piece(ref[at], trail_second(trail_ref, c)), spread[FIRST:], NN
                )
                at = pl.multiple_of(((where[1] - j) & 3) * 512, 512)
                out_ref[:, pl.ds(at, 512)] = full[:128] + full[128:]


def residual(where, cross, inverse, segment, trail, rows_total):
    n = inverse.shape[0]
    whole = lambda v: pl.BlockSpec(v.shape, lambda i, w: (0,) * v.ndim)
    operands = [cross, inverse, *segment, trail]
    return pl.pallas_call(
        functools.partial(residual_kernel, float(rows_total)),
        out_shape=(
            jax.ShapeDtypeStruct((128, n), F32),
            jax.ShapeDtypeStruct((128, 8192), F32),
        ),
        grid_spec=pltpu.PrefetchScalarGridSpec(
            num_scalar_prefetch=1,
            grid=(4,),
            in_specs=[whole(v) for v in operands],
            out_specs=(
                pl.BlockSpec((128, n), lambda i, w: (0, 0)),
                pl.BlockSpec((128, 2048), lambda i, w: (0, (w[0] - i) & 3)),
            ),
            scratch_shapes=[pltpu.VMEM((256, n), BF16), pltpu.VMEM((HELD, 512), BF16)],
        ),
        compiler_params=params(),
        cost_estimate=pl.CostEstimate(
            flops=4 * 128 * n * 6400, bytes_accessed=14 << 20, transcendentals=0
        ),
    )(where, *operands)


def sum_row(v, core):
    v = sum4(swap_add(v, core), "row", y_pair)
    return jnp.concatenate(swap_gather(v, core), axis=0)


def per_device(
    descriptors, gradients, sparse_panel, sparse_trail, atom_counts, owner_rows, neighbor_ids
):
    row = lax.axis_index("row")
    col = lax.axis_index("col")
    core, y = row % 2, row // 2
    x, z = col // 4, col % 4
    rows_total = 65536

    where = jnp.stack([x, z, y, core]).astype(jnp.int32)

    trail_own = lax.dynamic_slice_in_dim(sparse_trail, core * 64, 64, 0)
    trail_own = lax.all_gather(trail_own, "col", axis=0, tiled=False)
    piece = lax.dynamic_slice_in_dim(sparse_panel, core * 16, 16, 0)
    piece = jnp.stack(shifted(piece, "col", z_shift))
    own = jnp.stack(shifted(piece, "col", x_shift))
    other = lax.ppermute(own, "row", CORE_SWAP)

    atoms, grads, mean, order = prepare(
        where,
        atom_counts,
        owner_rows,
        neighbor_ids.reshape(128, 4).T,
        descriptors,
        gradients.reshape(12, 128, 1024),
    )

    near, far, gram = panel_rows(where, own, other, atoms, grads, mean, order)
    far = lax.ppermute(far, "row", CORE_SWAP)
    gram = swap_add(gram, core)
    far, gram = lax.optimization_barrier((far, gram))
    got = [
        lax.ppermute(jnp.stack([near[s], far[s]]), "row", y_shift(s)) for s in (1, 2, 3)
    ]
    gram = scatter4(gram, "row", y_shift, y)
    got, gram = lax.optimization_barrier((got, gram))
    first, second = assemble(where, near, far, got)
    first = ring_stack(first, "col", z_shift)
    second = ring_stack(second, "col", x_shift)
    trail_other = lax.ppermute(trail_own, "row", CORE_SWAP)
    gram = sum4(gram, "col", z_pair)
    trail_other, gram = lax.optimization_barrier((trail_other, gram))
    gram = sum4(gram, "col", x_pair)
    trail = trail_rows(where, trail_own, trail_other, atoms, grads, mean, order)
    first, second, gram = lax.optimization_barrier((first, second, gram))
    segment = (
        first,
        *ring(first, "col", x_shift),
        second,
        *ring(second, "col", z_shift),
    )
    gram = gather4(gram, "row", y_shift, y)
    trail, segment, gram = lax.optimization_barrier((trail, segment, gram))
    gram = jnp.concatenate(swap_gather(gram, core), axis=0)
    trail = lax.all_to_all(
        trail.reshape(128, SENT, 128), ("row", "col"), 0, 0, tiled=True
    ).reshape(8, 16, SENT, 128)
    factor, inverse = factor_panel(gram, rows_total)

    segment, inverse = lax.optimization_barrier((segment, inverse))
    cross = sum_row(cross_part(where, segment, trail), core)
    coupling, result = residual(where, cross, inverse, segment, trail, rows_total)
    return factor, coupling, result


def solution(mesh):
    return jax.shard_map(
        per_device,
        mesh=mesh,
        in_specs=(
            P(("row", "col"), None),
            P(None, None, ("row", "col"), None),
            P("col", None),
            P("col", None),
            P(("row", "col"), None),
            P(("row", "col"), None),
            P(("row", "col"), None, None),
        ),
        out_specs=(P(), P("col", None), P("col", "row")),
        check_vma=False,
    )
```

```python
import functools

import jax
import jax.numpy as jnp
from jax import lax
from jax.experimental import pallas as pl
from jax.experimental.pallas import tpu as pltpu
from jax.sharding import PartitionSpec as P

ridge_value = 0.1
HIGHEST = lax.Precision.HIGHEST
F32 = jnp.float32
BF16 = jnp.bfloat16
NT = (((1,), (1,)), ((), ()))
NN = (((1,), (0,)), ((), ()))
TN = (((0,), (0,)), ((), ()))

CORE_SWAP = [(i, i ^ 1) for i in range(8)]


def y_shift(s):
    return [(2 * y + c, 2 * ((y + s) % 4) + c) for y in range(4) for c in range(2)]


def z_shift(s):
    return [(x * 4 + z, x * 4 + (z + s) % 4) for x in range(4) for z in range(4)]


def x_shift(s):
    return [(x * 4 + z, ((x + s) % 4) * 4 + z) for x in range(4) for z in range(4)]


SENT = 56
HELD = 400
UPPER = [(i, j) for i in range(4) for j in range(i, 4)]


def y_pair(f):
    return [(2 * y + c, 2 * (y ^ f) + c) for y in range(4) for c in range(2)]


def z_pair(f):
    return [(x * 4 + z, x * 4 + (z ^ f)) for x in range(4) for z in range(4)]


def x_pair(f):
    return [(x * 4 + z, (x ^ f) * 4 + z) for x in range(4) for z in range(4)]


def dot(a, b, dims, precision=None):
    return lax.dot_general(a, b, dims, precision=precision, preferred_element_type=F32)


def in_order(pieces, index):
    return jnp.concatenate(
        [lax.select_n((index - j) % 4, *pieces) for j in range(4)], axis=0
    )


def shifted(v, axis, shift):
    return [v] + [lax.ppermute(v, axis, shift(s)) for s in (1, 2, 3)]


def gather4(v, axis, shift, index):
    pieces = [v] + [lax.ppermute(v, axis, shift(s)) for s in (1, 2, 3)]
    return in_order(pieces, index)


def scatter4(v, axis, shift, index):
    n = v.shape[0] // 4
    total = lax.dynamic_slice_in_dim(v, index * n, n, 0)
    got = [
        lax.ppermute(
            lax.dynamic_slice_in_dim(v, ((index + s) % 4) * n, n, 0), axis, shift(s)
        )
        for s in (1, 2, 3)
    ]
    return total + got[0] + got[1] + got[2]


def swap_add(v, core):
    n = v.shape[0] // 2
    mine = lax.dynamic_slice_in_dim(v, core * n, n, 0)
    other = lax.dynamic_slice_in_dim(v, (1 - core) * n, n, 0)
    return mine + lax.ppermute(other, "row", CORE_SWAP)


def swap_gather(v, core):
    other = lax.ppermute(v, "row", CORE_SWAP)
    first = core == 0
    return jnp.where(first, v, other), jnp.where(first, other, v)


def sum4(v, axis, pairs):
    for flip in (1, 3):
        v = v + lax.ppermute(v, axis, pairs(flip))
    return v


def prep_kernel(
    where, count_ref, owner_ref, neighbor_ref, desc_ref, grad_ref, atoms_ref, grads_ref, mean_ref, order_ref
):
    counts = [count_ref[0, s] for s in range(8)]
    owners = [owner_ref[0, s] for s in range(8)]
    offsets = [jnp.int32(0)]
    for s in range(7):
        offsets.append(offsets[s] + counts[s])

    lane = lax.broadcasted_iota(jnp.int32, (8, 128), 1)
    struct, atom = lane >> 4, lane & 15
    count_l, offset_l = jnp.ones((8, 128), jnp.int32), jnp.zeros((8, 128), jnp.int32)
    for s in range(8):
        count_l = jnp.where(struct == s, counts[s], count_l)
        offset_l = jnp.where(struct == s, offsets[s], offset_l)
    place = jnp.where(atom < count_l, offset_l + atom, -1)
    rows = lax.broadcasted_iota(jnp.int32, (64, 128), 0)
    lanes = lax.broadcasted_iota(jnp.int32, (64, 128), 1)
    live = place[:1] == rows
    live_f = live.astype(F32)

    value = neighbor_ref[...].astype(F32)
    size = count_l.astype(F32)[:4]
    rest = value - size * jnp.floor(value / size)
    rest = jnp.where(rest < 0.0, rest + size, rest)
    rest = jnp.where(rest >= size, rest - size, rest)
    partner = rest + (16 * struct).astype(F32)[:4]

    picks = [live_f.astype(BF16)]
    for j in range(4):
        slot = jnp.sum(live_f * partner[j : j + 1], axis=1, keepdims=True)
        picks.append((slot == lanes.astype(F32)).astype(F32).astype(BF16))
    desc = desc_ref[...]
    for j in range(5):
        atoms_ref[64 * j : 64 * j + 64] = dot(picks[j], desc, NN).astype(BF16)
    for i in range(12):
        grads_ref[64 * i : 64 * i + 64] = dot(picks[0], grad_ref[i], NN).astype(BF16)

    sub8 = lax.broadcasted_iota(jnp.int32, (8, 64), 0)
    atom8 = lax.broadcasted_iota(jnp.int32, (8, 64), 1)
    low, size8 = jnp.zeros((8, 64), jnp.int32), jnp.ones((8, 64), jnp.int32)
    for s in range(8):
        low = jnp.where(sub8 == s, offsets[s], low)
        size8 = jnp.where(sub8 == s, counts[s], size8)
    inside = (atom8 >= low) & (atom8 < low + size8)
    mean_ref[...] = jnp.where(inside, 1.0 / size8.astype(F32), 0.0)

    source = 2 * where[2] + where[3]
    r = lax.broadcasted_iota(jnp.int32, (SENT, 256), 0)
    wanted = lax.broadcasted_iota(jnp.int32, (SENT, 256), 1)
    third = (r * 43) >> 7
    part = r - 3 * third
    for g in range(8):
        struct_g, count_g, offset_g = jnp.int32(0), jnp.int32(0), jnp.int32(0)
        for s in range(8):
            mine = owners[s] == g
            struct_g = jnp.where(mine, s, struct_g)
            count_g = jnp.where(mine, counts[s], count_g)
            offset_g = jnp.where(mine, offsets[s], offset_g)
        column = jnp.where((third < count_g) & (r < 48), part * 64 + offset_g + third, -1)
        column = jnp.where(r == 48 + source, 192 + struct_g, column)
        order_ref[SENT * g : SENT * g + SENT] = (column == wanted).astype(F32)


def prepare(where, count, owner, neighbors, descriptors, gradients):
    smem = pl.BlockSpec(memory_space=pltpu.SMEM)
    vmem = pl.BlockSpec(memory_space=pltpu.VMEM)
    return pl.pallas_call(
        prep_kernel,
        out_shape=(
            jax.ShapeDtypeStruct((320, 1024), BF16),
            jax.ShapeDtypeStruct((768, 1024), BF16),
            jax.ShapeDtypeStruct((8, 64), F32),
            jax.ShapeDtypeStruct((8 * SENT, 256), F32),
        ),
        in_specs=[smem, smem, smem, vmem, vmem, vmem],
        out_specs=(vmem, vmem, vmem, vmem),
        compiler_params=params(),
        cost_estimate=pl.CostEstimate(
            flops=2 * 64 * 128 * 1024 * 17, bytes_accessed=6 << 20, transcendentals=0
        ),
    )(where, count, owner, neighbors, descriptors, gradients)


def compact_rows(env, atoms, grads, mean):
    near = dot(atoms, env, NT)
    slope = dot(grads, env, NT)
    inner = near[:64]
    parts = []
    for k in range(3):
        total = near[64:128] * slope[k * 256 : k * 256 + 64]
        for j in range(1, 4):
            total = total + near[64 + j * 64 : 128 + j * 64] * slope[
                k * 256 + j * 64 : k * 256 + j * 64 + 64
            ]
        parts.append((-2.0 * total).astype(BF16))
    energy = dot(mean, inner * inner, NN, HIGHEST)
    pad = jnp.zeros((56, env.shape[0]), F32)
    parts.append(jnp.concatenate([energy, pad], axis=0).astype(BF16))
    return jnp.concatenate(parts, axis=0)


def put_env(env, where, own, other, block, at):
    core = where[3]
    env[pl.ds(pl.multiple_of(at + core * 16, 16), 16)] = own[block]
    env[pl.ds(pl.multiple_of(at + (1 - core) * 16, 16), 16)] = other[block]


def panel_kernel(
    where, own, other, atoms_ref, grads_ref, mean_ref, order_ref, near_ref, far_ref, gram_ref, env
):
    x, z, y, core = where[0], where[1], where[2], where[3]
    for i in range(4):
        for j in range(4):
            place = ((x - i) & 3) * 4 + ((z - j) & 3)
            put_env(env, where, own, other, (i, j), place * 32)
    rows = compact_rows(env[...], atoms_ref[...], grads_ref[...], mean_ref[...])
    full = dot(order_ref[...].astype(BF16), rows, NN)
    first = core == 0
    for i in range(4):
        at = 2 * SENT * i
        low, high = full[at : at + SENT], full[at + SENT : at + 2 * SENT]
        s = (i - y) & 3
        near_ref[s] = jnp.where(first, low, high).astype(BF16)
        far_ref[s] = jnp.where(first, high, low).astype(BF16)
    gram = dot(rows, rows, TN)
    for n, (i, j) in enumerate(UPPER):
        gram_ref[128 * n : 128 * n + 128] = gram[
            128 * i : 128 * i + 128, 128 * j : 128 * j + 128
        ]


def trail_kernel(
    where, own_ref, other_ref, atoms_ref, grads_ref, mean_ref, order_ref, out_ref
):
    first = where[3] == 0
    own, other = own_ref[...], other_ref[...]
    low, high = jnp.where(first, own, other), jnp.where(first, other, own)
    env = jnp.concatenate([low, high], axis=1).reshape(-1, 1024)
    rows = compact_rows(env, atoms_ref[...], grads_ref[...], mean_ref[...])
    full = dot(order_ref[...].astype(BF16), rows, NN)
    for c in range(out_ref.shape[1]):
        part = full[:, c * 128 : c * 128 + 128].reshape(8, SENT, 128)
        out_ref[:, c] = part.astype(BF16)


def assemble_kernel(where, near, far, got1, got2, got3, out):
    y, core = where[2], where[3]
    blocks = [(near, 0, 0, core), (far, 0, 0, 1 - core)]
    for s, got in ((1, got1), (2, got2), (3, got3)):
        blocks += [(got, 0, s, core), (got, 1, s, 1 - core)]
    energy = jnp.zeros((8, out.shape[1]), F32)
    for ref, i, s, c in blocks:
        at = (2 * ((y - s) & 3) + c) * 48
        out[pl.ds(pl.multiple_of(at, 16), 48)] = ref[i, :48]
        energy = energy + ref[i, 48:].astype(F32)
    out[384:] = jnp.concatenate([energy, jnp.zeros_like(energy)], axis=0).astype(BF16)


def trail_chunk(ref, i):
    rows = [ref[r, i, :48].astype(F32) for r in range(8)]
    energy = ref[0, i, 48:].astype(F32)
    for r in range(1, 8):
        energy = energy + ref[r, i, 48:].astype(F32)
    return jnp.concatenate(rows + [energy, jnp.zeros_like(energy)], axis=0).astype(BF16)


def params(mib=40):
    return pltpu.CompilerParams(vmem_limit_bytes=mib << 20)


def in_smem():
    return pl.BlockSpec(memory_space=pltpu.SMEM)


def in_vmem():
    return pl.BlockSpec(memory_space=pltpu.VMEM)


def panel_rows(where, own, other, atoms, grads, mean, order):
    return pl.pallas_call(
        panel_kernel,
        out_shape=(
            jax.ShapeDtypeStruct((4, SENT, 512), BF16),
            jax.ShapeDtypeStruct((4, SENT, 512), BF16),
            jax.ShapeDtypeStruct((1280, 128), F32),
        ),
        in_specs=[in_smem()] + [in_vmem()] * 6,
        out_specs=(in_vmem(),) * 3,
        scratch_shapes=[pltpu.VMEM((512, 1024), BF16)],
        compiler_params=params(),
        cost_estimate=pl.CostEstimate(
            flops=2 * 512 * 1024 * 1088, bytes_accessed=5 << 20, transcendentals=0
        ),
    )(where, own, other, atoms, grads, mean, order)


def assemble(where, near, far, got):
    return pl.pallas_call(
        assemble_kernel,
        out_shape=jax.ShapeDtypeStruct((HELD, 512), BF16),
        in_specs=[in_smem()] + [in_vmem()] * 5,
        out_specs=in_vmem(),
        compiler_params=params(),
        cost_estimate=pl.CostEstimate(flops=0, bytes_accessed=1 << 20, transcendentals=0),
    )(where, near, far, *got)


def trail_rows(where, own, other, atoms, grads, mean, order):
    blocks = own.shape[0]
    step = 4
    half = pl.BlockSpec((step, 64, 1024), lambda i, w: (i, 0, 0))
    whole = lambda shape: pl.BlockSpec(shape, lambda i, w: (0, 0))
    return pl.pallas_call(
        trail_kernel,
        out_shape=jax.ShapeDtypeStruct((8, blocks, SENT, 128), BF16),
        grid_spec=pltpu.PrefetchScalarGridSpec(
            num_scalar_prefetch=1,
            grid=(blocks // step,),
            in_specs=[
                half,
                half,
                whole(atoms.shape),
                whole(grads.shape),
                whole(mean.shape),
                whole(order.shape),
            ],
            out_specs=pl.BlockSpec((8, step, SENT, 128), lambda i, w: (0, i, 0, 0)),
        ),
        compiler_params=params(),
        cost_estimate=pl.CostEstimate(
            flops=2 * 2048 * 1024 * 1088, bytes_accessed=9 << 20, transcendentals=0
        ),
    )(where, own, other, atoms, grads, mean, order)


def eliminate(a):
    lanes = lax.broadcasted_iota(jnp.int32, (8, 128), 1)
    subs = lax.broadcasted_iota(jnp.int32, (8, 128), 0)
    left = [a[8 * g : 8 * g + 8] for g in range(16)]
    right = [(lanes == subs + 8 * g).astype(F32) for g in range(16)]
    done = []
    for p in range(16):
        count = 16 - p
        cols = [
            [
                jnp.broadcast_to(left[g][:, 8 * p + q : 8 * p + q + 1], (8, 128))
                for g in range(count)
            ]
            for q in range(8)
        ]
        pivots = jnp.ones((8, 128), F32)
        for q in range(8):
            pivot = cols[q][0][q : q + 1]
            inverse = 1.0 / pivot
            pivots = jnp.where(subs == q, pivot, pivots)
            ratio = [c * inverse for c in cols[q]]
            ratio[0] = jnp.where(subs > q, ratio[0], 0.0)
            for t in range(q + 1, 8):
                here = cols[t][0][q : q + 1]
                for g in range(count):
                    cols[t][g] = cols[t][g] - ratio[g] * here
            row_left = left[0][q : q + 1]
            row_right = right[0][q : q + 1]
            for g in range(count):
                left[g] = left[g] - ratio[g] * row_left
                right[g] = right[g] - ratio[g] * row_right
        done.append(right[0] * lax.rsqrt(pivots))
        left, right = left[1:], right[1:]
    return jnp.concatenate(done, axis=0)


def factor_kernel(rows_total, gram_ref, factor_ref, inverse_ref, work):
    n = factor_ref.shape[0]
    r = lax.broadcasted_iota(jnp.int32, (n, n), 0)
    c = lax.broadcasted_iota(jnp.int32, (n, n), 1)
    same = r[:128, :128] == c[:128, :128]
    work[:, :n] = jnp.zeros((n, n), F32)
    for m, (i, j) in enumerate(UPPER):
        block = gram_ref[128 * m : 128 * m + 128] / rows_total
        if i == j:
            block = block + jnp.where(same, ridge_value, 0.0)
        work[128 * i : 128 * i + 128, 128 * j : 128 * j + 128] = block
    work[:, n:] = jnp.where(r == c, 1.0, 0.0)

    def step(b, carry):
        at = pl.multiple_of(b * 128, 128)
        low = eliminate(work[pl.ds(at, 128), pl.ds(at, 128)])
        for k in range(n // 128):

            @pl.when(b == k)
            def _(k=k):
                here, after = slice(128 * k, 128 * k + 128), slice(128 * k + 128, n)
                left, right = slice(128 * k, n), slice(n, n + 128 * k + 128)
                row = dot(low, work[here, left], NN, HIGHEST)
                solved = dot(low, work[here, right], NN, HIGHEST)
                work[here, left] = row
                work[here, right] = solved
                if k < n // 128 - 1:
                    later = row[:, 128:]
                    work[after, after] -= dot(later, later, TN, HIGHEST)
                    work[after, right] -= dot(later, solved, TN, HIGHEST)

        return carry

    lax.fori_loop(0, n // 128, step, 0)
    factor_ref[...] = jnp.where(c >= r, work[:, :n], 0.0)
    inverse_ref[...] = jnp.where(c <= r, work[:, n:], 0.0)


def factor_panel(gram, rows_total):
    n = 512
    return pl.pallas_call(
        functools.partial(factor_kernel, float(rows_total)),
        out_shape=(jax.ShapeDtypeStruct((n, n), F32), jax.ShapeDtypeStruct((n, n), F32)),
        scratch_shapes=[pltpu.VMEM((n, 2 * n), F32)],
        compiler_params=params(),
        cost_estimate=pl.CostEstimate(
            flops=20 * n * n * n, bytes_accessed=4 << 20, transcendentals=n
        ),
    )(gram)


def cross_kernel(panel_ref, trail_ref, out_ref):
    @pl.when(pl.program_id(0) == 0)
    def _():
        out_ref[...] = jnp.zeros_like(out_ref)

    n = panel_ref.shape[2]
    trail = jnp.concatenate(
        [trail_chunk(trail_ref, i) for i in range(panel_ref.shape[0])], axis=0
    )
    out_ref[...] += dot(trail, panel_ref[...].reshape(-1, n), TN)


def cross_part(segment, trail):
    n = segment.shape[2]
    return pl.pallas_call(
        cross_kernel,
        out_shape=jax.ShapeDtypeStruct((128, n), F32),
        grid=(segment.shape[0] // 4,),
        in_specs=[
            pl.BlockSpec((4, HELD, n), lambda i: (i, 0, 0)),
            pl.BlockSpec((8, 4, SENT, 128), lambda i: (0, i, 0, 0)),
        ],
        out_specs=pl.BlockSpec((128, n), lambda i: (0, 0)),
        compiler_params=params(),
        cost_estimate=pl.CostEstimate(
            flops=2 * 128 * n * 8192, bytes_accessed=11 << 20, transcendentals=0
        ),
    )(segment, trail)


def spread_pair(rest, k, lane):
    full = jnp.zeros((128, 128), F32)
    for m in (0, 1):
        struct, at = 2 * k + m, 64 * m
        start = 48 * struct
        turn = (at + 1 - start) % 128
        part = start // 128
        split = at + 1 + min(48, 128 * (part + 1) - start)
        force = pltpu.roll(rest[:, 128 * part : 128 * part + 128], turn, 1)
        full = jnp.where((lane > at) & (lane < split), force, full)
        if split < at + 49:
            force = pltpu.roll(rest[:, 128 * part + 128 : 128 * part + 256], turn, 1)
            full = jnp.where((lane >= split) & (lane < at + 49), force, full)
        energy = jnp.broadcast_to(rest[:, 384 + struct : 385 + struct], (128, 128))
        full = jnp.where(lane == at, energy, full)
    return full


def residual_kernel(
    rows_total, cross_ref, inverse_ref, panel_ref, trail_ref, coupling_ref, out_ref, weights
):
    @pl.when(pl.program_id(0) == 0)
    def _():
        coupling = dot(cross_ref[...] / rows_total, inverse_ref[...], NT, HIGHEST)
        coupling_ref[...] = coupling
        solved = dot(coupling, inverse_ref[...], NN, HIGHEST)
        high = solved.astype(BF16)
        weights[:128] = high
        weights[128:] = (solved - high.astype(F32)).astype(BF16)

    r = lax.broadcasted_iota(jnp.int32, (128, 128), 0)
    c = lax.broadcasted_iota(jnp.int32, (128, 128), 1)
    same = (r == c).astype(BF16)
    for i in range(panel_ref.shape[0]):
        both = dot(weights[...], panel_ref[i], NT)
        own = dot(same, trail_chunk(trail_ref, i), NT)
        rest = own - both[:128] - both[128:]
        for k in range(4):
            at = i * 512 + k * 128
            out_ref[:, at : at + 128] = spread_pair(rest, k, c)


def residual(cross, inverse, segment, trail, rows_total):
    n = inverse.shape[0]
    chunks = segment.shape[0]
    whole = lambda shape: pl.BlockSpec(shape, lambda i: (0, 0))
    return pl.pallas_call(
        functools.partial(residual_kernel, float(rows_total)),
        out_shape=(
            jax.ShapeDtypeStruct((128, n), F32),
            jax.ShapeDtypeStruct((128, 512 * chunks), F32),
        ),
        grid=(chunks // 4,),
        in_specs=[
            whole((128, n)),
            whole((n, n)),
            pl.BlockSpec((4, HELD, n), lambda i: (i, 0, 0)),
            pl.BlockSpec((8, 4, SENT, 128), lambda i: (0, i, 0, 0)),
        ],
        out_specs=(whole((128, n)), pl.BlockSpec((128, 2048), lambda i: (0, i))),
        scratch_shapes=[pltpu.VMEM((256, n), BF16)],
        compiler_params=params(),
        cost_estimate=pl.CostEstimate(
            flops=4 * 128 * n * 8192, bytes_accessed=16 << 20, transcendentals=0
        ),
    )(cross, inverse, segment, trail)


def sum_row(v, core):
    v = sum4(swap_add(v, core), "row", y_pair)
    return jnp.concatenate(swap_gather(v, core), axis=0)


def per_device(
    descriptors, gradients, sparse_panel, sparse_trail, atom_counts, owner_rows, neighbor_ids
):
    row = lax.axis_index("row")
    col = lax.axis_index("col")
    core, y = row % 2, row // 2
    x, z = col // 4, col % 4
    rows_total = 65536

    where = jnp.stack([x, z, y, core]).astype(jnp.int32)

    trail_own = lax.dynamic_slice_in_dim(sparse_trail, core * 64, 64, 0)
    trail_own = lax.all_gather(trail_own, "col", axis=0, tiled=False)
    piece = lax.dynamic_slice_in_dim(sparse_panel, core * 16, 16, 0)
    piece = jnp.stack(shifted(piece, "col", z_shift))
    own = jnp.stack(shifted(piece, "col", x_shift))
    other = lax.ppermute(own, "row", CORE_SWAP)

    atoms, grads, mean, order = prepare(
        where,
        atom_counts,
        owner_rows,
        neighbor_ids.reshape(128, 4).T,
        descriptors,
        gradients.reshape(12, 128, 1024),
    )

    near, far, gram = panel_rows(where, own, other, atoms, grads, mean, order)
    far = lax.ppermute(far, "row", CORE_SWAP)
    gram = swap_add(gram, core)
    far, gram = lax.optimization_barrier((far, gram))
    got = [
        lax.ppermute(jnp.stack([near[s], far[s]]), "row", y_shift(s)) for s in (1, 2, 3)
    ]
    gram = scatter4(gram, "row", y_shift, y)
    got, gram = lax.optimization_barrier((got, gram))
    panel = assemble(where, near, far, got)
    segment = lax.all_gather(panel, "col", axis=0, tiled=False)
    trail_other = lax.ppermute(trail_own, "row", CORE_SWAP)
    gram = sum4(gram, "col", z_pair)
    gram = sum4(gram, "col", x_pair)
    trail_other, gram = lax.optimization_barrier((trail_other, gram))
    trail = trail_rows(where, trail_own, trail_other, atoms, grads, mean, order)
    gram = gather4(gram, "row", y_shift, y)
    trail, gram = lax.optimization_barrier((trail, gram))
    gram = jnp.concatenate(swap_gather(gram, core), axis=0)
    trail = lax.all_to_all(
        trail.reshape(128, SENT, 128), ("row", "col"), 0, 0, tiled=True
    ).reshape(8, 16, SENT, 128)
    factor, inverse = factor_panel(gram, rows_total)

    segment, inverse = lax.optimization_barrier((segment, inverse))
    cross = sum_row(cross_part(segment, trail), core)
    coupling, result = residual(cross, inverse, segment, trail, rows_total)
    return factor, coupling, result


def solution(mesh):
    return jax.shard_map(
        per_device,
        mesh=mesh,
        in_specs=(
            P(("row", "col"), None),
            P(None, None, ("row", "col"), None),
            P("col", None),
            P("col", None),
            P(("row", "col"), None),
            P(("row", "col"), None),
            P(("row", "col"), None, None),
        ),
        out_specs=(P(), P("col", None), P("col", "row")),
        check_vma=False,
    )
```

```python
import functools

import jax
import jax.numpy as jnp
from jax import lax
from jax.experimental import pallas as pl
from jax.experimental.pallas import tpu as pltpu
from jax.sharding import PartitionSpec as P

ridge_value = 0.1
HIGHEST = lax.Precision.HIGHEST
F32 = jnp.float32
BF16 = jnp.bfloat16
NT = (((1,), (1,)), ((), ()))
NN = (((1,), (0,)), ((), ()))
TN = (((0,), (0,)), ((), ()))

CORE_SWAP = [(i, i ^ 1) for i in range(8)]


def y_shift(s):
    return [(2 * y + c, 2 * ((y + s) % 4) + c) for y in range(4) for c in range(2)]


def z_shift(s):
    return [(x * 4 + z, x * 4 + (z + s) % 4) for x in range(4) for z in range(4)]


def x_shift(s):
    return [(x * 4 + z, ((x + s) % 4) * 4 + z) for x in range(4) for z in range(4)]


SENT = 56
HELD = 400
UPPER = [(i, j) for i in range(4) for j in range(i, 4)]


def y_pair(f):
    return [(2 * y + c, 2 * (y ^ f) + c) for y in range(4) for c in range(2)]


def z_pair(f):
    return [(x * 4 + z, x * 4 + (z ^ f)) for x in range(4) for z in range(4)]


def x_pair(f):
    return [(x * 4 + z, (x ^ f) * 4 + z) for x in range(4) for z in range(4)]


def dot(a, b, dims, precision=None):
    return lax.dot_general(a, b, dims, precision=precision, preferred_element_type=F32)


def in_order(pieces, index):
    return jnp.concatenate(
        [lax.select_n((index - j) % 4, *pieces) for j in range(4)], axis=0
    )


def shifted(v, axis, shift):
    return [v] + [lax.ppermute(v, axis, shift(s)) for s in (1, 2, 3)]


def gather4(v, axis, shift, index):
    pieces = [v] + [lax.ppermute(v, axis, shift(s)) for s in (1, 2, 3)]
    return in_order(pieces, index)


def scatter4(v, axis, shift, index):
    n = v.shape[0] // 4
    total = lax.dynamic_slice_in_dim(v, index * n, n, 0)
    got = [
        lax.ppermute(
            lax.dynamic_slice_in_dim(v, ((index + s) % 4) * n, n, 0), axis, shift(s)
        )
        for s in (1, 2, 3)
    ]
    return total + got[0] + got[1] + got[2]


def swap_add(v, core):
    n = v.shape[0] // 2
    mine = lax.dynamic_slice_in_dim(v, core * n, n, 0)
    other = lax.dynamic_slice_in_dim(v, (1 - core) * n, n, 0)
    return mine + lax.ppermute(other, "row", CORE_SWAP)


def swap_gather(v, core):
    other = lax.ppermute(v, "row", CORE_SWAP)
    first = core == 0
    return jnp.where(first, v, other), jnp.where(first, other, v)


def sum4(v, axis, pairs):
    for flip in (1, 3):
        v = v + lax.ppermute(v, axis, pairs(flip))
    return v


def prep_kernel(
    where, count_ref, owner_ref, neighbor_ref, desc_ref, grad_ref, atoms_ref, grads_ref, mean_ref, order_ref
):
    counts = [count_ref[0, s] for s in range(8)]
    owners = [owner_ref[0, s] for s in range(8)]
    offsets = [jnp.int32(0)]
    for s in range(7):
        offsets.append(offsets[s] + counts[s])

    lane = lax.broadcasted_iota(jnp.int32, (8, 128), 1)
    struct, atom = lane >> 4, lane & 15
    count_l, offset_l = jnp.ones((8, 128), jnp.int32), jnp.zeros((8, 128), jnp.int32)
    for s in range(8):
        count_l = jnp.where(struct == s, counts[s], count_l)
        offset_l = jnp.where(struct == s, offsets[s], offset_l)
    place = jnp.where(atom < count_l, offset_l + atom, -1)
    rows = lax.broadcasted_iota(jnp.int32, (64, 128), 0)
    lanes = lax.broadcasted_iota(jnp.int32, (64, 128), 1)
    live = place[:1] == rows
    live_f = live.astype(F32)

    value = neighbor_ref[...].astype(F32)
    size = count_l.astype(F32)[:4]
    rest = value - size * jnp.floor(value / size)
    rest = jnp.where(rest < 0.0, rest + size, rest)
    rest = jnp.where(rest >= size, rest - size, rest)
    partner = rest + (16 * struct).astype(F32)[:4]

    picks = [live_f.astype(BF16)]
    for j in range(4):
        slot = jnp.sum(live_f * partner[j : j + 1], axis=1, keepdims=True)
        picks.append((slot == lanes.astype(F32)).astype(F32).astype(BF16))
    desc = desc_ref[...]
    for j in range(5):
        atoms_ref[64 * j : 64 * j + 64] = dot(picks[j], desc, NN).astype(BF16)
    for i in range(12):
        grads_ref[64 * i : 64 * i + 64] = dot(picks[0], grad_ref[i], NN).astype(BF16)

    sub8 = lax.broadcasted_iota(jnp.int32, (8, 64), 0)
    atom8 = lax.broadcasted_iota(jnp.int32, (8, 64), 1)
    low, size8 = jnp.zeros((8, 64), jnp.int32), jnp.ones((8, 64), jnp.int32)
    for s in range(8):
        low = jnp.where(sub8 == s, offsets[s], low)
        size8 = jnp.where(sub8 == s, counts[s], size8)
    inside = (atom8 >= low) & (atom8 < low + size8)
    mean_ref[...] = jnp.where(inside, 1.0 / size8.astype(F32), 0.0)

    source = 2 * where[2] + where[3]
    r = lax.broadcasted_iota(jnp.int32, (SENT, 256), 0)
    wanted = lax.broadcasted_iota(jnp.int32, (SENT, 256), 1)
    third = (r * 43) >> 7
    part = r - 3 * third
    for g in range(8):
        struct_g, count_g, offset_g = jnp.int32(0), jnp.int32(0), jnp.int32(0)
        for s in range(8):
            mine = owners[s] == g
            struct_g = jnp.where(mine, s, struct_g)
            count_g = jnp.where(mine, counts[s], count_g)
            offset_g = jnp.where(mine, offsets[s], offset_g)
        column = jnp.where((third < count_g) & (r < 48), part * 64 + offset_g + third, -1)
        column = jnp.where(r == 48 + source, 192 + struct_g, column)
        order_ref[SENT * g : SENT * g + SENT] = (column == wanted).astype(F32)


def prepare(where, count, owner, neighbors, descriptors, gradients):
    smem = pl.BlockSpec(memory_space=pltpu.SMEM)
    vmem = pl.BlockSpec(memory_space=pltpu.VMEM)
    return pl.pallas_call(
        prep_kernel,
        out_shape=(
            jax.ShapeDtypeStruct((320, 1024), BF16),
            jax.ShapeDtypeStruct((768, 1024), BF16),
            jax.ShapeDtypeStruct((8, 64), F32),
            jax.ShapeDtypeStruct((8 * SENT, 256), F32),
        ),
        in_specs=[smem, smem, smem, vmem, vmem, vmem],
        out_specs=(vmem, vmem, vmem, vmem),
        compiler_params=params(),
        cost_estimate=pl.CostEstimate(
            flops=2 * 64 * 128 * 1024 * 17, bytes_accessed=6 << 20, transcendentals=0
        ),
    )(where, count, owner, neighbors, descriptors, gradients)


def compact_rows(env, atoms, grads, mean):
    near = dot(atoms, env, NT)
    slope = dot(grads, env, NT)
    inner = near[:64]
    parts = []
    for k in range(3):
        total = near[64:128] * slope[k * 256 : k * 256 + 64]
        for j in range(1, 4):
            total = total + near[64 + j * 64 : 128 + j * 64] * slope[
                k * 256 + j * 64 : k * 256 + j * 64 + 64
            ]
        parts.append((-2.0 * total).astype(BF16))
    energy = dot(mean, inner * inner, NN, HIGHEST)
    pad = jnp.zeros((56, env.shape[0]), F32)
    parts.append(jnp.concatenate([energy, pad], axis=0).astype(BF16))
    return jnp.concatenate(parts, axis=0)


def put_env(env, where, own, other, block, at):
    core = where[3]
    env[pl.ds(pl.multiple_of(at + core * 16, 16), 16)] = own[block]
    env[pl.ds(pl.multiple_of(at + (1 - core) * 16, 16), 16)] = other[block]


def panel_kernel(
    where, own, other, atoms_ref, grads_ref, mean_ref, order_ref, near_ref, far_ref, gram_ref, env
):
    x, z, y, core = where[0], where[1], where[2], where[3]
    for i in range(4):
        for j in range(4):
            place = ((x - i) & 3) * 4 + ((z - j) & 3)
            put_env(env, where, own, other, (i, j), place * 32)
    rows = compact_rows(env[...], atoms_ref[...], grads_ref[...], mean_ref[...])
    full = dot(order_ref[...].astype(BF16), rows, NN)
    first = core == 0
    for i in range(4):
        at = 2 * SENT * i
        low, high = full[at : at + SENT], full[at + SENT : at + 2 * SENT]
        s = (i - y) & 3
        near_ref[s] = jnp.where(first, low, high).astype(BF16)
        far_ref[s] = jnp.where(first, high, low).astype(BF16)
    gram = dot(rows, rows, TN)
    for n, (i, j) in enumerate(UPPER):
        gram_ref[128 * n : 128 * n + 128] = gram[
            128 * i : 128 * i + 128, 128 * j : 128 * j + 128
        ]


def trail_kernel(
    where, own, other, atoms_ref, grads_ref, mean_ref, order_ref, out_ref, env
):
    z, y = where[1], where[2]
    for j in range(4):
        place = ((z - j) & 3) * 128
        for s in range(4):
            put_env(env, where, own, other, (s, 0, j), place + ((y - s) & 3) * 32)
    rows = compact_rows(env[...], atoms_ref[...], grads_ref[...], mean_ref[...])
    full = dot(order_ref[...].astype(BF16), rows, NN)
    for c in range(out_ref.shape[1]):
        part = full[:, c * 128 : c * 128 + 128].reshape(8, SENT, 128)
        out_ref[:, c] = part.astype(BF16)


def assemble_kernel(where, near, far, got1, got2, got3, out):
    y, core = where[2], where[3]
    blocks = [(near, 0, 0, core), (far, 0, 0, 1 - core)]
    for s, got in ((1, got1), (2, got2), (3, got3)):
        blocks += [(got, 0, s, core), (got, 1, s, 1 - core)]
    energy = jnp.zeros((8, out.shape[1]), F32)
    for ref, i, s, c in blocks:
        at = (2 * ((y - s) & 3) + c) * 48
        out[pl.ds(pl.multiple_of(at, 16), 48)] = ref[i, :48]
        energy = energy + ref[i, 48:].astype(F32)
    out[384:] = jnp.concatenate([energy, jnp.zeros_like(energy)], axis=0).astype(BF16)


def trail_chunk(ref, i):
    rows = [ref[r, i, :48].astype(F32) for r in range(8)]
    energy = ref[0, i, 48:].astype(F32)
    for r in range(1, 8):
        energy = energy + ref[r, i, 48:].astype(F32)
    return jnp.concatenate(rows + [energy, jnp.zeros_like(energy)], axis=0).astype(BF16)


def params(mib=40):
    return pltpu.CompilerParams(vmem_limit_bytes=mib << 20)


def in_smem():
    return pl.BlockSpec(memory_space=pltpu.SMEM)


def in_vmem():
    return pl.BlockSpec(memory_space=pltpu.VMEM)


def panel_rows(where, own, other, atoms, grads, mean, order):
    return pl.pallas_call(
        panel_kernel,
        out_shape=(
            jax.ShapeDtypeStruct((4, SENT, 512), BF16),
            jax.ShapeDtypeStruct((4, SENT, 512), BF16),
            jax.ShapeDtypeStruct((1280, 128), F32),
        ),
        in_specs=[in_smem()] + [in_vmem()] * 6,
        out_specs=(in_vmem(),) * 3,
        scratch_shapes=[pltpu.VMEM((512, 1024), BF16)],
        compiler_params=params(),
        cost_estimate=pl.CostEstimate(
            flops=2 * 512 * 1024 * 1088, bytes_accessed=5 << 20, transcendentals=0
        ),
    )(where, own, other, atoms, grads, mean, order)


def assemble(where, near, far, got):
    return pl.pallas_call(
        assemble_kernel,
        out_shape=jax.ShapeDtypeStruct((HELD, 512), BF16),
        in_specs=[in_smem()] + [in_vmem()] * 5,
        out_specs=in_vmem(),
        compiler_params=params(),
        cost_estimate=pl.CostEstimate(flops=0, bytes_accessed=1 << 20, transcendentals=0),
    )(where, near, far, *got)


def trail_rows(where, own, other, atoms, grads, mean, order):
    piece = pl.BlockSpec((4, 1, 4, 16, 1024), lambda i, w: (0, i, 0, 0, 0))
    whole = lambda shape: pl.BlockSpec(shape, lambda i, w: (0, 0))
    return pl.pallas_call(
        trail_kernel,
        out_shape=jax.ShapeDtypeStruct((8, 16, SENT, 128), BF16),
        grid_spec=pltpu.PrefetchScalarGridSpec(
            num_scalar_prefetch=1,
            grid=(4,),
            in_specs=[piece] * 2
            + [
                whole(atoms.shape),
                whole(grads.shape),
                whole(mean.shape),
                whole(order.shape),
            ],
            out_specs=pl.BlockSpec((8, 4, SENT, 128), lambda i, w: (0, (w[0] - i) & 3, 0, 0)),
            scratch_shapes=[pltpu.VMEM((512, 1024), BF16)],
        ),
        compiler_params=params(),
        cost_estimate=pl.CostEstimate(
            flops=2 * 2048 * 1024 * 1088, bytes_accessed=9 << 20, transcendentals=0
        ),
    )(where, own, other, atoms, grads, mean, order)


def eliminate(a):
    lanes = lax.broadcasted_iota(jnp.int32, (8, 128), 1)
    subs = lax.broadcasted_iota(jnp.int32, (8, 128), 0)
    left = [a[8 * g : 8 * g + 8] for g in range(16)]
    right = [(lanes == subs + 8 * g).astype(F32) for g in range(16)]
    done = []
    for p in range(16):
        count = 16 - p
        cols = [
            [
                jnp.broadcast_to(left[g][:, 8 * p + q : 8 * p + q + 1], (8, 128))
                for g in range(count)
            ]
            for q in range(8)
        ]
        pivots = jnp.ones((8, 128), F32)
        for q in range(8):
            pivot = cols[q][0][q : q + 1]
            inverse = 1.0 / pivot
            pivots = jnp.where(subs == q, pivot, pivots)
            ratio = [c * inverse for c in cols[q]]
            ratio[0] = jnp.where(subs > q, ratio[0], 0.0)
            for t in range(q + 1, 8):
                here = cols[t][0][q : q + 1]
                for g in range(count):
                    cols[t][g] = cols[t][g] - ratio[g] * here
            row_left = left[0][q : q + 1]
            row_right = right[0][q : q + 1]
            for g in range(count):
                left[g] = left[g] - ratio[g] * row_left
                right[g] = right[g] - ratio[g] * row_right
        done.append(right[0] * lax.rsqrt(pivots))
        left, right = left[1:], right[1:]
    return jnp.concatenate(done, axis=0)


def factor_kernel(rows_total, gram_ref, factor_ref, inverse_ref, work):
    n = factor_ref.shape[0]
    r = lax.broadcasted_iota(jnp.int32, (n, n), 0)
    c = lax.broadcasted_iota(jnp.int32, (n, n), 1)
    same = r[:128, :128] == c[:128, :128]
    work[:, :n] = jnp.zeros((n, n), F32)
    for m, (i, j) in enumerate(UPPER):
        block = gram_ref[128 * m : 128 * m + 128] / rows_total
        if i == j:
            block = block + jnp.where(same, ridge_value, 0.0)
        work[128 * i : 128 * i + 128, 128 * j : 128 * j + 128] = block
    work[:, n:] = jnp.where(r == c, 1.0, 0.0)

    def step(b, carry):
        at = pl.multiple_of(b * 128, 128)
        low = eliminate(work[pl.ds(at, 128), pl.ds(at, 128)])
        for k in range(n // 128):

            @pl.when(b == k)
            def _(k=k):
                here, after = slice(128 * k, 128 * k + 128), slice(128 * k + 128, n)
                left, right = slice(128 * k, n), slice(n, n + 128 * k + 128)
                row = dot(low, work[here, left], NN, HIGHEST)
                solved = dot(low, work[here, right], NN, HIGHEST)
                work[here, left] = row
                work[here, right] = solved
                if k < n // 128 - 1:
                    later = row[:, 128:]
                    work[after, after] -= dot(later, later, TN, HIGHEST)
                    work[after, right] -= dot(later, solved, TN, HIGHEST)

        return carry

    lax.fori_loop(0, n // 128, step, 0)
    factor_ref[...] = jnp.where(c >= r, work[:, :n], 0.0)
    inverse_ref[...] = jnp.where(c <= r, work[:, n:], 0.0)


def factor_panel(gram, rows_total):
    n = 512
    return pl.pallas_call(
        functools.partial(factor_kernel, float(rows_total)),
        out_shape=(jax.ShapeDtypeStruct((n, n), F32), jax.ShapeDtypeStruct((n, n), F32)),
        scratch_shapes=[pltpu.VMEM((n, 2 * n), F32)],
        compiler_params=params(),
        cost_estimate=pl.CostEstimate(
            flops=20 * n * n * n, bytes_accessed=4 << 20, transcendentals=n
        ),
    )(gram)


def cross_kernel(panel_ref, trail_ref, out_ref):
    @pl.when(pl.program_id(0) == 0)
    def _():
        out_ref[...] = jnp.zeros_like(out_ref)

    n = panel_ref.shape[2]
    trail = jnp.concatenate(
        [trail_chunk(trail_ref, i) for i in range(panel_ref.shape[0])], axis=0
    )
    out_ref[...] += dot(trail, panel_ref[...].reshape(-1, n), TN)


def cross_part(segment, trail):
    n = segment.shape[2]
    return pl.pallas_call(
        cross_kernel,
        out_shape=jax.ShapeDtypeStruct((128, n), F32),
        grid=(segment.shape[0] // 4,),
        in_specs=[
            pl.BlockSpec((4, HELD, n), lambda i: (i, 0, 0)),
            pl.BlockSpec((8, 4, SENT, 128), lambda i: (0, i, 0, 0)),
        ],
        out_specs=pl.BlockSpec((128, n), lambda i: (0, 0)),
        compiler_params=params(),
        cost_estimate=pl.CostEstimate(
            flops=2 * 128 * n * 8192, bytes_accessed=11 << 20, transcendentals=0
        ),
    )(segment, trail)


def spread_pair(rest, k, lane):
    full = jnp.zeros((128, 128), F32)
    for m in (0, 1):
        struct, at = 2 * k + m, 64 * m
        start = 48 * struct
        turn = (at + 1 - start) % 128
        part = start // 128
        split = at + 1 + min(48, 128 * (part + 1) - start)
        force = pltpu.roll(rest[:, 128 * part : 128 * part + 128], turn, 1)
        full = jnp.where((lane > at) & (lane < split), force, full)
        if split < at + 49:
            force = pltpu.roll(rest[:, 128 * part + 128 : 128 * part + 256], turn, 1)
            full = jnp.where((lane >= split) & (lane < at + 49), force, full)
        energy = jnp.broadcast_to(rest[:, 384 + struct : 385 + struct], (128, 128))
        full = jnp.where(lane == at, energy, full)
    return full


def residual_kernel(
    rows_total, cross_ref, inverse_ref, panel_ref, trail_ref, coupling_ref, out_ref, weights
):
    @pl.when(pl.program_id(0) == 0)
    def _():
        coupling = dot(cross_ref[...] / rows_total, inverse_ref[...], NT, HIGHEST)
        coupling_ref[...] = coupling
        solved = dot(coupling, inverse_ref[...], NN, HIGHEST)
        high = solved.astype(BF16)
        weights[:128] = high
        weights[128:] = (solved - high.astype(F32)).astype(BF16)

    r = lax.broadcasted_iota(jnp.int32, (128, 128), 0)
    c = lax.broadcasted_iota(jnp.int32, (128, 128), 1)
    same = (r == c).astype(BF16)
    for i in range(panel_ref.shape[0]):
        both = dot(weights[...], panel_ref[i], NT)
        own = dot(same, trail_chunk(trail_ref, i), NT)
        rest = own - both[:128] - both[128:]
        for k in range(4):
            at = i * 512 + k * 128
            out_ref[:, at : at + 128] = spread_pair(rest, k, c)


def residual(cross, inverse, segment, trail, rows_total):
    n = inverse.shape[0]
    chunks = segment.shape[0]
    whole = lambda shape: pl.BlockSpec(shape, lambda i: (0, 0))
    return pl.pallas_call(
        functools.partial(residual_kernel, float(rows_total)),
        out_shape=(
            jax.ShapeDtypeStruct((128, n), F32),
            jax.ShapeDtypeStruct((128, 512 * chunks), F32),
        ),
        grid=(chunks // 4,),
        in_specs=[
            whole((128, n)),
            whole((n, n)),
            pl.BlockSpec((4, HELD, n), lambda i: (i, 0, 0)),
            pl.BlockSpec((8, 4, SENT, 128), lambda i: (0, i, 0, 0)),
        ],
        out_specs=(whole((128, n)), pl.BlockSpec((128, 2048), lambda i: (0, i))),
        scratch_shapes=[pltpu.VMEM((256, n), BF16)],
        compiler_params=params(58),
        cost_estimate=pl.CostEstimate(
            flops=4 * 128 * n * 8192, bytes_accessed=16 << 20, transcendentals=0
        ),
    )(cross, inverse, segment, trail)


def sum_row(v, core):
    v = sum4(swap_add(v, core), "row", y_pair)
    return jnp.concatenate(swap_gather(v, core), axis=0)


def per_device(
    descriptors, gradients, sparse_panel, sparse_trail, atom_counts, owner_rows, neighbor_ids
):
    row = lax.axis_index("row")
    col = lax.axis_index("col")
    core, y = row % 2, row // 2
    x, z = col // 4, col % 4
    rows_total = 65536

    where = jnp.stack([x, z, y, core]).astype(jnp.int32)

    piece = jnp.concatenate(
        [
            lax.dynamic_slice_in_dim(sparse_panel, core * 16, 16, 0),
            lax.dynamic_slice_in_dim(sparse_trail, row * 16, 16, 0),
        ],
        axis=0,
    )
    pieces = shifted(piece, "col", z_shift)
    piece = jnp.stack([p[:16] for p in pieces])
    piece_trail = jnp.stack([p[16:] for p in pieces])
    own = jnp.stack(shifted(piece, "col", x_shift))
    own, piece_trail = lax.optimization_barrier((own, piece_trail))
    other = lax.ppermute(own, "row", CORE_SWAP)
    own_trail = jnp.stack(shifted(piece_trail, "col", x_shift))

    atoms, grads, mean, order = prepare(
        where,
        atom_counts,
        owner_rows,
        neighbor_ids.reshape(128, 4).T,
        descriptors,
        gradients.reshape(12, 128, 1024),
    )

    near, far, gram = panel_rows(where, own, other, atoms, grads, mean, order)
    far = lax.ppermute(far, "row", CORE_SWAP)
    gram = swap_add(gram, core)
    far, gram, own_trail = lax.optimization_barrier((far, gram, own_trail))
    got = [
        lax.ppermute(jnp.stack([near[s], far[s]]), "row", y_shift(s)) for s in (1, 2, 3)
    ]
    gram = scatter4(gram, "row", y_shift, y)
    got, gram, own_trail = lax.optimization_barrier((got, gram, own_trail))
    panel = assemble(where, near, far, got)
    segment = lax.all_gather(panel, "col", axis=0, tiled=False)
    one = lax.ppermute(own_trail, "row", y_shift(1))
    three = lax.ppermute(own_trail, "row", y_shift(3))
    gram = sum4(gram, "col", z_pair)
    one, three, gram = lax.optimization_barrier((one, three, gram))
    low = lax.ppermute(one[:2], "row", y_shift(1))
    high = lax.ppermute(three[2:], "row", y_shift(3))
    trail_own = jnp.stack([own_trail, one, jnp.concatenate([low, high], axis=0), three])
    gram = sum4(gram, "col", x_pair)
    trail_own, gram = lax.optimization_barrier((trail_own, gram))
    trail_other = lax.ppermute(trail_own, "row", CORE_SWAP)
    trail = trail_rows(where, trail_own, trail_other, atoms, grads, mean, order)
    gram = gather4(gram, "row", y_shift, y)
    gram = jnp.concatenate(swap_gather(gram, core), axis=0)
    trail, gram = lax.optimization_barrier((trail, gram))
    trail = lax.all_to_all(
        trail.reshape(128, SENT, 128), ("row", "col"), 0, 0, tiled=True
    ).reshape(8, 16, SENT, 128)
    factor, inverse = factor_panel(gram, rows_total)

    segment, inverse = lax.optimization_barrier((segment, inverse))
    cross = sum_row(cross_part(segment, trail), core)
    coupling, result = residual(cross, inverse, segment, trail, rows_total)
    return factor, coupling, result


def solution(mesh):
    return jax.shard_map(
        per_device,
        mesh=mesh,
        in_specs=(
            P(("row", "col"), None),
            P(None, None, ("row", "col"), None),
            P("col", None),
            P("col", None),
            P(("row", "col"), None),
            P(("row", "col"), None),
            P(("row", "col"), None, None),
        ),
        out_specs=(P(), P("col", None), P("col", "row")),
        check_vma=False,
    )
```

```python
import functools

import jax
import jax.numpy as jnp
from jax import lax
from jax.experimental import pallas as pl
from jax.experimental.pallas import tpu as pltpu
from jax.sharding import PartitionSpec as P

ridge_value = 0.1
HIGHEST = lax.Precision.HIGHEST
F32 = jnp.float32
BF16 = jnp.bfloat16
NT = (((1,), (1,)), ((), ()))
NN = (((1,), (0,)), ((), ()))
TN = (((0,), (0,)), ((), ()))

CORE_SWAP = [(i, i ^ 1) for i in range(8)]


def y_shift(s):
    return [(2 * y + c, 2 * ((y + s) % 4) + c) for y in range(4) for c in range(2)]


def z_shift(s):
    return [(x * 4 + z, x * 4 + (z + s) % 4) for x in range(4) for z in range(4)]


def x_shift(s):
    return [(x * 4 + z, ((x + s) % 4) * 4 + z) for x in range(4) for z in range(4)]


SENT = 56
HELD = 400
UPPER = [(i, j) for i in range(4) for j in range(i, 4)]


def y_pair(f):
    return [(2 * y + c, 2 * (y ^ f) + c) for y in range(4) for c in range(2)]


def z_pair(f):
    return [(x * 4 + z, x * 4 + (z ^ f)) for x in range(4) for z in range(4)]


def x_pair(f):
    return [(x * 4 + z, (x ^ f) * 4 + z) for x in range(4) for z in range(4)]


def dot(a, b, dims, precision=None):
    return lax.dot_general(a, b, dims, precision=precision, preferred_element_type=F32)


def in_order(pieces, index):
    return jnp.concatenate(
        [lax.select_n((index - j) % 4, *pieces) for j in range(4)], axis=0
    )


def shifted(v, axis, shift):
    return [v] + [lax.ppermute(v, axis, shift(s)) for s in (1, 2, 3)]


def gather4(v, axis, shift, index):
    pieces = [v] + [lax.ppermute(v, axis, shift(s)) for s in (1, 2, 3)]
    return in_order(pieces, index)


def scatter4(v, axis, shift, index):
    n = v.shape[0] // 4
    total = lax.dynamic_slice_in_dim(v, index * n, n, 0)
    got = [
        lax.ppermute(
            lax.dynamic_slice_in_dim(v, ((index + s) % 4) * n, n, 0), axis, shift(s)
        )
        for s in (1, 2, 3)
    ]
    return total + got[0] + got[1] + got[2]


def swap_add(v, core):
    n = v.shape[0] // 2
    mine = lax.dynamic_slice_in_dim(v, core * n, n, 0)
    other = lax.dynamic_slice_in_dim(v, (1 - core) * n, n, 0)
    return mine + lax.ppermute(other, "row", CORE_SWAP)


def swap_gather(v, core):
    other = lax.ppermute(v, "row", CORE_SWAP)
    first = core == 0
    return jnp.where(first, v, other), jnp.where(first, other, v)


def sum4(v, axis, pairs):
    for flip in (1, 3):
        v = v + lax.ppermute(v, axis, pairs(flip))
    return v


def prep_kernel(
    where, count_ref, owner_ref, neighbor_ref, desc_ref, grad_ref, atoms_ref, grads_ref, mean_ref, order_ref
):
    counts = [count_ref[0, s] for s in range(8)]
    owners = [owner_ref[0, s] for s in range(8)]
    offsets = [jnp.int32(0)]
    for s in range(7):
        offsets.append(offsets[s] + counts[s])

    lane = lax.broadcasted_iota(jnp.int32, (8, 128), 1)
    struct, atom = lane >> 4, lane & 15
    count_l, offset_l = jnp.ones((8, 128), jnp.int32), jnp.zeros((8, 128), jnp.int32)
    for s in range(8):
        count_l = jnp.where(struct == s, counts[s], count_l)
        offset_l = jnp.where(struct == s, offsets[s], offset_l)
    place = jnp.where(atom < count_l, offset_l + atom, -1)
    rows = lax.broadcasted_iota(jnp.int32, (64, 128), 0)
    lanes = lax.broadcasted_iota(jnp.int32, (64, 128), 1)
    live = place[:1] == rows
    live_f = live.astype(F32)

    value = neighbor_ref[...].astype(F32)
    size = count_l.astype(F32)[:4]
    rest = value - size * jnp.floor(value / size)
    rest = jnp.where(rest < 0.0, rest + size, rest)
    rest = jnp.where(rest >= size, rest - size, rest)
    partner = rest + (16 * struct).astype(F32)[:4]

    picks = [live_f.astype(BF16)]
    for j in range(4):
        slot = jnp.sum(live_f * partner[j : j + 1], axis=1, keepdims=True)
        picks.append((slot == lanes.astype(F32)).astype(F32).astype(BF16))
    desc = desc_ref[...]
    for j in range(5):
        atoms_ref[64 * j : 64 * j + 64] = dot(picks[j], desc, NN).astype(BF16)
    for i in range(12):
        grads_ref[64 * i : 64 * i + 64] = dot(picks[0], grad_ref[i], NN).astype(BF16)

    sub8 = lax.broadcasted_iota(jnp.int32, (8, 64), 0)
    atom8 = lax.broadcasted_iota(jnp.int32, (8, 64), 1)
    low, size8 = jnp.zeros((8, 64), jnp.int32), jnp.ones((8, 64), jnp.int32)
    for s in range(8):
        low = jnp.where(sub8 == s, offsets[s], low)
        size8 = jnp.where(sub8 == s, counts[s], size8)
    inside = (atom8 >= low) & (atom8 < low + size8)
    mean_ref[...] = jnp.where(inside, 1.0 / size8.astype(F32), 0.0)

    source = 2 * where[2] + where[3]
    r = lax.broadcasted_iota(jnp.int32, (SENT, 256), 0)
    wanted = lax.broadcasted_iota(jnp.int32, (SENT, 256), 1)
    third = (r * 43) >> 7
    part = r - 3 * third
    for g in range(8):
        struct_g, count_g, offset_g = jnp.int32(0), jnp.int32(0), jnp.int32(0)
        for s in range(8):
            mine = owners[s] == g
            struct_g = jnp.where(mine, s, struct_g)
            count_g = jnp.where(mine, counts[s], count_g)
            offset_g = jnp.where(mine, offsets[s], offset_g)
        column = jnp.where((third < count_g) & (r < 48), part * 64 + offset_g + third, -1)
        column = jnp.where(r == 48 + source, 192 + struct_g, column)
        order_ref[SENT * g : SENT * g + SENT] = (column == wanted).astype(F32)


def prepare(where, count, owner, neighbors, descriptors, gradients):
    smem = pl.BlockSpec(memory_space=pltpu.SMEM)
    vmem = pl.BlockSpec(memory_space=pltpu.VMEM)
    return pl.pallas_call(
        prep_kernel,
        out_shape=(
            jax.ShapeDtypeStruct((320, 1024), BF16),
            jax.ShapeDtypeStruct((768, 1024), BF16),
            jax.ShapeDtypeStruct((8, 64), F32),
            jax.ShapeDtypeStruct((8 * SENT, 256), F32),
        ),
        in_specs=[smem, smem, smem, vmem, vmem, vmem],
        out_specs=(vmem, vmem, vmem, vmem),
        compiler_params=params(),
        cost_estimate=pl.CostEstimate(
            flops=2 * 64 * 128 * 1024 * 17, bytes_accessed=6 << 20, transcendentals=0
        ),
    )(where, count, owner, neighbors, descriptors, gradients)


def compact_rows(env, atoms, grads, mean):
    near = dot(atoms, env, NT)
    slope = dot(grads, env, NT)
    inner = near[:64]
    parts = []
    for k in range(3):
        total = near[64:128] * slope[k * 256 : k * 256 + 64]
        for j in range(1, 4):
            total = total + near[64 + j * 64 : 128 + j * 64] * slope[
                k * 256 + j * 64 : k * 256 + j * 64 + 64
            ]
        parts.append((-2.0 * total).astype(BF16))
    energy = dot(mean, inner * inner, NN, HIGHEST)
    pad = jnp.zeros((56, env.shape[0]), F32)
    parts.append(jnp.concatenate([energy, pad], axis=0).astype(BF16))
    return jnp.concatenate(parts, axis=0)


def put_env(env, where, own, other, block, at):
    core = where[3]
    env[pl.ds(pl.multiple_of(at + core * 16, 16), 16)] = own[block]
    env[pl.ds(pl.multiple_of(at + (1 - core) * 16, 16), 16)] = other[block]


def panel_kernel(
    where, own, other, atoms_ref, grads_ref, mean_ref, order_ref, near_ref, far_ref, gram_ref, env
):
    x, z, y, core = where[0], where[1], where[2], where[3]
    for i in range(4):
        for j in range(4):
            place = ((x - i) & 3) * 4 + ((z - j) & 3)
            put_env(env, where, own, other, (i, j), place * 32)
    rows = compact_rows(env[...], atoms_ref[...], grads_ref[...], mean_ref[...])
    full = dot(order_ref[...].astype(BF16), rows, NN)
    first = core == 0
    for i in range(4):
        at = 2 * SENT * i
        low, high = full[at : at + SENT], full[at + SENT : at + 2 * SENT]
        s = (i - y) & 3
        near_ref[s] = jnp.where(first, low, high).astype(BF16)
        far_ref[s] = jnp.where(first, high, low).astype(BF16)
    gram = dot(rows, rows, TN)
    for n, (i, j) in enumerate(UPPER):
        gram_ref[128 * n : 128 * n + 128] = gram[
            128 * i : 128 * i + 128, 128 * j : 128 * j + 128
        ]


def trail_kernel(
    where, own, other, own2, other2, atoms_ref, grads_ref, mean_ref, order_ref, out_ref, env
):
    z, y = where[1], where[2]
    for j in range(4):
        place = ((z - j) & 3) * 128
        for k, s in enumerate((0, 1, 3)):
            put_env(env, where, own, other, (k, 0, j), place + ((y - s) & 3) * 32)
        put_env(env, where, own2, other2, (0, j), place + ((y - 2) & 3) * 32)
    rows = compact_rows(env[...], atoms_ref[...], grads_ref[...], mean_ref[...])
    full = dot(order_ref[...].astype(BF16), rows, NN)
    for c in range(out_ref.shape[1]):
        part = full[:, c * 128 : c * 128 + 128].reshape(8, SENT, 128)
        out_ref[:, c] = part.astype(BF16)


def assemble_kernel(where, near, far, got1, got2, got3, out):
    y, core = where[2], where[3]
    blocks = [(near, 0, 0, core), (far, 0, 0, 1 - core)]
    for s, got in ((1, got1), (2, got2), (3, got3)):
        blocks += [(got, 0, s, core), (got, 1, s, 1 - core)]
    energy = jnp.zeros((8, out.shape[1]), F32)
    for ref, i, s, c in blocks:
        at = (2 * ((y - s) & 3) + c) * 48
        out[pl.ds(pl.multiple_of(at, 16), 48)] = ref[i, :48]
        energy = energy + ref[i, 48:].astype(F32)
    out[384:] = jnp.concatenate([energy, jnp.zeros_like(energy)], axis=0).astype(BF16)


def trail_chunk(ref, i):
    rows = [ref[r, i, :48].astype(F32) for r in range(8)]
    energy = ref[0, i, 48:].astype(F32)
    for r in range(1, 8):
        energy = energy + ref[r, i, 48:].astype(F32)
    return jnp.concatenate(rows + [energy, jnp.zeros_like(energy)], axis=0).astype(BF16)


def params(mib=40):
    return pltpu.CompilerParams(vmem_limit_bytes=mib << 20)


def in_smem():
    return pl.BlockSpec(memory_space=pltpu.SMEM)


def in_vmem():
    return pl.BlockSpec(memory_space=pltpu.VMEM)


def panel_rows(where, own, other, atoms, grads, mean, order):
    return pl.pallas_call(
        panel_kernel,
        out_shape=(
            jax.ShapeDtypeStruct((4, SENT, 512), BF16),
            jax.ShapeDtypeStruct((4, SENT, 512), BF16),
            jax.ShapeDtypeStruct((1280, 128), F32),
        ),
        in_specs=[in_smem()] + [in_vmem()] * 6,
        out_specs=(in_vmem(),) * 3,
        scratch_shapes=[pltpu.VMEM((512, 1024), BF16)],
        compiler_params=params(),
        cost_estimate=pl.CostEstimate(
            flops=2 * 512 * 1024 * 1088, bytes_accessed=5 << 20, transcendentals=0
        ),
    )(where, own, other, atoms, grads, mean, order)


def assemble(where, near, far, got):
    return pl.pallas_call(
        assemble_kernel,
        out_shape=jax.ShapeDtypeStruct((HELD, 512), BF16),
        in_specs=[in_smem()] + [in_vmem()] * 5,
        out_specs=in_vmem(),
        compiler_params=params(),
        cost_estimate=pl.CostEstimate(flops=0, bytes_accessed=1 << 20, transcendentals=0),
    )(where, near, far, *got)


def trail_rows(where, own, other, own2, other2, atoms, grads, mean, order):
    piece = pl.BlockSpec((3, 1, 4, 16, 1024), lambda i, w: (0, i, 0, 0, 0))
    last = pl.BlockSpec((1, 4, 16, 1024), lambda i, w: (i, 0, 0, 0))
    whole = lambda shape: pl.BlockSpec(shape, lambda i, w: (0, 0))
    return pl.pallas_call(
        trail_kernel,
        out_shape=jax.ShapeDtypeStruct((8, 16, SENT, 128), BF16),
        grid_spec=pltpu.PrefetchScalarGridSpec(
            num_scalar_prefetch=1,
            grid=(4,),
            in_specs=[piece, piece, last, last]
            + [
                whole(atoms.shape),
                whole(grads.shape),
                whole(mean.shape),
                whole(order.shape),
            ],
            out_specs=pl.BlockSpec((8, 4, SENT, 128), lambda i, w: (0, (w[0] - i) & 3, 0, 0)),
            scratch_shapes=[pltpu.VMEM((512, 1024), BF16)],
        ),
        compiler_params=params(),
        cost_estimate=pl.CostEstimate(
            flops=2 * 2048 * 1024 * 1088, bytes_accessed=9 << 20, transcendentals=0
        ),
    )(where, own, other, own2, other2, atoms, grads, mean, order)


def eliminate(a):
    lanes = lax.broadcasted_iota(jnp.int32, (8, 128), 1)
    subs = lax.broadcasted_iota(jnp.int32, (8, 128), 0)
    left = [a[8 * g : 8 * g + 8] for g in range(16)]
    right = [(lanes == subs + 8 * g).astype(F32) for g in range(16)]
    done = []
    for p in range(16):
        count = 16 - p
        cols = [
            [
                jnp.broadcast_to(left[g][:, 8 * p + q : 8 * p + q + 1], (8, 128))
                for g in range(count)
            ]
            for q in range(8)
        ]
        pivots = jnp.ones((8, 128), F32)
        for q in range(8):
            pivot = cols[q][0][q : q + 1]
            inverse = 1.0 / pivot
            pivots = jnp.where(subs == q, pivot, pivots)
            ratio = [c * inverse for c in cols[q]]
            ratio[0] = jnp.where(subs > q, ratio[0], 0.0)
            for t in range(q + 1, 8):
                here = cols[t][0][q : q + 1]
                for g in range(count):
                    cols[t][g] = cols[t][g] - ratio[g] * here
            row_left = left[0][q : q + 1]
            row_right = right[0][q : q + 1]
            for g in range(count):
                left[g] = left[g] - ratio[g] * row_left
                right[g] = right[g] - ratio[g] * row_right
        done.append(right[0] * lax.rsqrt(pivots))
        left, right = left[1:], right[1:]
    return jnp.concatenate(done, axis=0)


def factor_kernel(rows_total, gram_ref, factor_ref, inverse_ref, work):
    n = factor_ref.shape[0]
    r = lax.broadcasted_iota(jnp.int32, (n, n), 0)
    c = lax.broadcasted_iota(jnp.int32, (n, n), 1)
    same = r[:128, :128] == c[:128, :128]
    work[:, :n] = jnp.zeros((n, n), F32)
    for m, (i, j) in enumerate(UPPER):
        block = gram_ref[128 * m : 128 * m + 128] / rows_total
        if i == j:
            block = block + jnp.where(same, ridge_value, 0.0)
        work[128 * i : 128 * i + 128, 128 * j : 128 * j + 128] = block
    work[:, n:] = jnp.where(r == c, 1.0, 0.0)

    def step(b, carry):
        at = pl.multiple_of(b * 128, 128)
        low = eliminate(work[pl.ds(at, 128), pl.ds(at, 128)])
        for k in range(n // 128):

            @pl.when(b == k)
            def _(k=k):
                here, after = slice(128 * k, 128 * k + 128), slice(128 * k + 128, n)
                left, right = slice(128 * k, n), slice(n, n + 128 * k + 128)
                row = dot(low, work[here, left], NN, HIGHEST)
                solved = dot(low, work[here, right], NN, HIGHEST)
                work[here, left] = row
                work[here, right] = solved
                if k < n // 128 - 1:
                    later = row[:, 128:]
                    work[after, after] -= dot(later, later, TN, HIGHEST)
                    work[after, right] -= dot(later, solved, TN, HIGHEST)

        return carry

    lax.fori_loop(0, n // 128, step, 0)
    factor_ref[...] = jnp.where(c >= r, work[:, :n], 0.0)
    inverse_ref[...] = jnp.where(c <= r, work[:, n:], 0.0)


def factor_panel(gram, rows_total):
    n = 512
    return pl.pallas_call(
        functools.partial(factor_kernel, float(rows_total)),
        out_shape=(jax.ShapeDtypeStruct((n, n), F32), jax.ShapeDtypeStruct((n, n), F32)),
        scratch_shapes=[pltpu.VMEM((n, 2 * n), F32)],
        compiler_params=params(),
        cost_estimate=pl.CostEstimate(
            flops=20 * n * n * n, bytes_accessed=4 << 20, transcendentals=n
        ),
    )(gram)


def cross_kernel(panel_ref, trail_ref, out_ref):
    @pl.when(pl.program_id(0) == 0)
    def _():
        out_ref[...] = jnp.zeros_like(out_ref)

    n = panel_ref.shape[2]
    trail = jnp.concatenate(
        [trail_chunk(trail_ref, i) for i in range(panel_ref.shape[0])], axis=0
    )
    out_ref[...] += dot(trail, panel_ref[...].reshape(-1, n), TN)


def cross_part(segment, trail):
    n = segment.shape[2]
    return pl.pallas_call(
        cross_kernel,
        out_shape=jax.ShapeDtypeStruct((128, n), F32),
        grid=(segment.shape[0] // 4,),
        in_specs=[
            pl.BlockSpec((4, HELD, n), lambda i: (i, 0, 0)),
            pl.BlockSpec((8, 4, SENT, 128), lambda i: (0, i, 0, 0)),
        ],
        out_specs=pl.BlockSpec((128, n), lambda i: (0, 0)),
        compiler_params=params(),
        cost_estimate=pl.CostEstimate(
            flops=2 * 128 * n * 8192, bytes_accessed=11 << 20, transcendentals=0
        ),
    )(segment, trail)


def spread_pair(rest, k, lane):
    full = jnp.zeros((128, 128), F32)
    for m in (0, 1):
        struct, at = 2 * k + m, 64 * m
        start = 48 * struct
        turn = (at + 1 - start) % 128
        part = start // 128
        split = at + 1 + min(48, 128 * (part + 1) - start)
        force = pltpu.roll(rest[:, 128 * part : 128 * part + 128], turn, 1)
        full = jnp.where((lane > at) & (lane < split), force, full)
        if split < at + 49:
            force = pltpu.roll(rest[:, 128 * part + 128 : 128 * part + 256], turn, 1)
            full = jnp.where((lane >= split) & (lane < at + 49), force, full)
        energy = jnp.broadcast_to(rest[:, 384 + struct : 385 + struct], (128, 128))
        full = jnp.where(lane == at, energy, full)
    return full


def residual_kernel(
    rows_total, cross_ref, inverse_ref, panel_ref, trail_ref, coupling_ref, out_ref, weights
):
    @pl.when(pl.program_id(0) == 0)
    def _():
        coupling = dot(cross_ref[...] / rows_total, inverse_ref[...], NT, HIGHEST)
        coupling_ref[...] = coupling
        solved = dot(coupling, inverse_ref[...], NN, HIGHEST)
        high = solved.astype(BF16)
        weights[:128] = high
        weights[128:] = (solved - high.astype(F32)).astype(BF16)

    r = lax.broadcasted_iota(jnp.int32, (128, 128), 0)
    c = lax.broadcasted_iota(jnp.int32, (128, 128), 1)
    same = (r == c).astype(BF16)
    for i in range(panel_ref.shape[0]):
        both = dot(weights[...], panel_ref[i], NT)
        own = dot(same, trail_chunk(trail_ref, i), NT)
        rest = own - both[:128] - both[128:]
        for k in range(4):
            at = i * 512 + k * 128
            out_ref[:, at : at + 128] = spread_pair(rest, k, c)


def residual(cross, inverse, segment, trail, rows_total):
    n = inverse.shape[0]
    chunks = segment.shape[0]
    whole = lambda shape: pl.BlockSpec(shape, lambda i: (0, 0))
    return pl.pallas_call(
        functools.partial(residual_kernel, float(rows_total)),
        out_shape=(
            jax.ShapeDtypeStruct((128, n), F32),
            jax.ShapeDtypeStruct((128, 512 * chunks), F32),
        ),
        grid=(chunks // 4,),
        in_specs=[
            whole((128, n)),
            whole((n, n)),
            pl.BlockSpec((4, HELD, n), lambda i: (i, 0, 0)),
            pl.BlockSpec((8, 4, SENT, 128), lambda i: (0, i, 0, 0)),
        ],
        out_specs=(whole((128, n)), pl.BlockSpec((128, 2048), lambda i: (0, i))),
        scratch_shapes=[pltpu.VMEM((256, n), BF16)],
        compiler_params=params(58),
        cost_estimate=pl.CostEstimate(
            flops=4 * 128 * n * 8192, bytes_accessed=16 << 20, transcendentals=0
        ),
    )(cross, inverse, segment, trail)


def sum_row(v, core):
    v = sum4(swap_add(v, core), "row", y_pair)
    return jnp.concatenate(swap_gather(v, core), axis=0)


def per_device(
    descriptors, gradients, sparse_panel, sparse_trail, atom_counts, owner_rows, neighbor_ids
):
    row = lax.axis_index("row")
    col = lax.axis_index("col")
    core, y = row % 2, row // 2
    x, z = col // 4, col % 4
    rows_total = 65536

    where = jnp.stack([x, z, y, core]).astype(jnp.int32)

    piece = jnp.concatenate(
        [
            lax.dynamic_slice_in_dim(sparse_panel, core * 16, 16, 0),
            lax.dynamic_slice_in_dim(sparse_trail, row * 16, 16, 0),
        ],
        axis=0,
    )
    pieces = shifted(piece, "col", z_shift)
    piece = jnp.stack([p[:16] for p in pieces])
    piece_trail = jnp.stack([p[16:] for p in pieces])
    own = jnp.stack(shifted(piece, "col", x_shift))
    own, piece_trail = lax.optimization_barrier((own, piece_trail))
    other = lax.ppermute(own, "row", CORE_SWAP)
    own_trail = jnp.stack(shifted(piece_trail, "col", x_shift))

    atoms, grads, mean, order = prepare(
        where,
        atom_counts,
        owner_rows,
        neighbor_ids.reshape(128, 4).T,
        descriptors,
        gradients.reshape(12, 128, 1024),
    )

    near, far, gram = panel_rows(where, own, other, atoms, grads, mean, order)
    far = lax.ppermute(far, "row", CORE_SWAP)
    gram = swap_add(gram, core)
    far, gram, own_trail = lax.optimization_barrier((far, gram, own_trail))
    got = [
        lax.ppermute(jnp.stack([near[s], far[s]]), "row", y_shift(s)) for s in (1, 2, 3)
    ]
    gram = scatter4(gram, "row", y_shift, y)
    got, gram, own_trail = lax.optimization_barrier((got, gram, own_trail))
    panel = assemble(where, near, far, got)
    segment = lax.all_gather(panel, "col", axis=0, tiled=False)
    one = lax.ppermute(own_trail, "row", y_shift(1))
    three = lax.ppermute(own_trail, "row", y_shift(3))
    gram = sum4(gram, "col", z_pair)
    one, three, gram = lax.optimization_barrier((one, three, gram))
    low = lax.ppermute(one[:2], "row", y_shift(1))
    high = lax.ppermute(three[2:], "row", y_shift(3))
    trail_own = jnp.stack([own_trail, one, three])
    trail_other = lax.ppermute(trail_own, "row", CORE_SWAP)
    last = jnp.concatenate([low, high], axis=0)
    gram = sum4(gram, "col", x_pair)
    last, gram = lax.optimization_barrier((last, gram))
    last_other = lax.ppermute(last, "row", CORE_SWAP)
    trail_other, last_other, gram = lax.optimization_barrier((trail_other, last_other, gram))
    trail = trail_rows(
        where, trail_own, trail_other, last, last_other, atoms, grads, mean, order
    )
    gram = gather4(gram, "row", y_shift, y)
    gram = jnp.concatenate(swap_gather(gram, core), axis=0)
    trail, gram = lax.optimization_barrier((trail, gram))
    trail = lax.all_to_all(
        trail.reshape(128, SENT, 128), ("row", "col"), 0, 0, tiled=True
    ).reshape(8, 16, SENT, 128)
    factor, inverse = factor_panel(gram, rows_total)

    segment, inverse = lax.optimization_barrier((segment, inverse))
    cross = sum_row(cross_part(segment, trail), core)
    coupling, result = residual(cross, inverse, segment, trail, rows_total)
    return factor, coupling, result


def solution(mesh):
    return jax.shard_map(
        per_device,
        mesh=mesh,
        in_specs=(
            P(("row", "col"), None),
            P(None, None, ("row", "col"), None),
            P("col", None),
            P("col", None),
            P(("row", "col"), None),
            P(("row", "col"), None),
            P(("row", "col"), None, None),
        ),
        out_specs=(P(), P("col", None), P("col", "row")),
        check_vma=False,
    )
```

```python
import functools

import jax
import jax.numpy as jnp
from jax import lax
from jax.experimental import pallas as pl
from jax.experimental.pallas import tpu as pltpu
from jax.sharding import PartitionSpec as P

ridge_value = 0.1
HIGHEST = lax.Precision.HIGHEST
F32 = jnp.float32
BF16 = jnp.bfloat16
NT = (((1,), (1,)), ((), ()))
NN = (((1,), (0,)), ((), ()))
TN = (((0,), (0,)), ((), ()))

CORE_SWAP = [(i, i ^ 1) for i in range(8)]


def y_shift(s):
    return [(2 * y + c, 2 * ((y + s) % 4) + c) for y in range(4) for c in range(2)]


def z_shift(s):
    return [(x * 4 + z, x * 4 + (z + s) % 4) for x in range(4) for z in range(4)]


def x_shift(s):
    return [(x * 4 + z, ((x + s) % 4) * 4 + z) for x in range(4) for z in range(4)]


SENT = 56
HELD = 400
UPPER = [(i, j) for i in range(4) for j in range(i, 4)]


def y_pair(f):
    return [(2 * y + c, 2 * (y ^ f) + c) for y in range(4) for c in range(2)]


def z_pair(f):
    return [(x * 4 + z, x * 4 + (z ^ f)) for x in range(4) for z in range(4)]


def x_pair(f):
    return [(x * 4 + z, (x ^ f) * 4 + z) for x in range(4) for z in range(4)]


def dot(a, b, dims, precision=None):
    return lax.dot_general(a, b, dims, precision=precision, preferred_element_type=F32)


def in_order(pieces, index):
    return jnp.concatenate(
        [lax.select_n((index - j) % 4, *pieces) for j in range(4)], axis=0
    )


def shifted(v, axis, shift):
    return [v] + [lax.ppermute(v, axis, shift(s)) for s in (1, 2, 3)]


def gather4(v, axis, shift, index):
    pieces = [v] + [lax.ppermute(v, axis, shift(s)) for s in (1, 2, 3)]
    return in_order(pieces, index)


def scatter4(v, axis, shift, index):
    n = v.shape[0] // 4
    total = lax.dynamic_slice_in_dim(v, index * n, n, 0)
    got = [
        lax.ppermute(
            lax.dynamic_slice_in_dim(v, ((index + s) % 4) * n, n, 0), axis, shift(s)
        )
        for s in (1, 2, 3)
    ]
    return total + got[0] + got[1] + got[2]


def swap_add(v, core):
    n = v.shape[0] // 2
    mine = lax.dynamic_slice_in_dim(v, core * n, n, 0)
    other = lax.dynamic_slice_in_dim(v, (1 - core) * n, n, 0)
    return mine + lax.ppermute(other, "row", CORE_SWAP)


def swap_gather(v, core):
    other = lax.ppermute(v, "row", CORE_SWAP)
    first = core == 0
    return jnp.where(first, v, other), jnp.where(first, other, v)


def sum4(v, axis, pairs):
    for flip in (1, 3):
        v = v + lax.ppermute(v, axis, pairs(flip))
    return v


def prep_kernel(
    where, count_ref, owner_ref, neighbor_ref, desc_ref, grad_ref, atoms_ref, grads_ref, mean_ref, order_ref
):
    counts = [count_ref[0, s] for s in range(8)]
    owners = [owner_ref[0, s] for s in range(8)]
    offsets = [jnp.int32(0)]
    for s in range(7):
        offsets.append(offsets[s] + counts[s])

    lane = lax.broadcasted_iota(jnp.int32, (8, 128), 1)
    struct, atom = lane >> 4, lane & 15
    count_l, offset_l = jnp.ones((8, 128), jnp.int32), jnp.zeros((8, 128), jnp.int32)
    for s in range(8):
        count_l = jnp.where(struct == s, counts[s], count_l)
        offset_l = jnp.where(struct == s, offsets[s], offset_l)
    place = jnp.where(atom < count_l, offset_l + atom, -1)
    rows = lax.broadcasted_iota(jnp.int32, (64, 128), 0)
    lanes = lax.broadcasted_iota(jnp.int32, (64, 128), 1)
    live = place[:1] == rows
    live_f = live.astype(F32)

    value = neighbor_ref[...].astype(F32)
    size = count_l.astype(F32)[:4]
    rest = value - size * jnp.floor(value / size)
    rest = jnp.where(rest < 0.0, rest + size, rest)
    rest = jnp.where(rest >= size, rest - size, rest)
    partner = rest + (16 * struct).astype(F32)[:4]

    picks = [live_f.astype(BF16)]
    for j in range(4):
        slot = jnp.sum(live_f * partner[j : j + 1], axis=1, keepdims=True)
        picks.append((slot == lanes.astype(F32)).astype(F32).astype(BF16))
    desc = desc_ref[...]
    for j in range(5):
        atoms_ref[64 * j : 64 * j + 64] = dot(picks[j], desc, NN).astype(BF16)
    for i in range(12):
        grads_ref[64 * i : 64 * i + 64] = dot(picks[0], grad_ref[i], NN).astype(BF16)

    sub8 = lax.broadcasted_iota(jnp.int32, (8, 64), 0)
    atom8 = lax.broadcasted_iota(jnp.int32, (8, 64), 1)
    low, size8 = jnp.zeros((8, 64), jnp.int32), jnp.ones((8, 64), jnp.int32)
    for s in range(8):
        low = jnp.where(sub8 == s, offsets[s], low)
        size8 = jnp.where(sub8 == s, counts[s], size8)
    inside = (atom8 >= low) & (atom8 < low + size8)
    mean_ref[...] = jnp.where(inside, 1.0 / size8.astype(F32), 0.0)

    source = 2 * where[2] + where[3]
    r = lax.broadcasted_iota(jnp.int32, (SENT, 256), 0)
    wanted = lax.broadcasted_iota(jnp.int32, (SENT, 256), 1)
    third = (r * 43) >> 7
    part = r - 3 * third
    for g in range(8):
        struct_g, count_g, offset_g = jnp.int32(0), jnp.int32(0), jnp.int32(0)
        for s in range(8):
            mine = owners[s] == g
            struct_g = jnp.where(mine, s, struct_g)
            count_g = jnp.where(mine, counts[s], count_g)
            offset_g = jnp.where(mine, offsets[s], offset_g)
        column = jnp.where((third < count_g) & (r < 48), part * 64 + offset_g + third, -1)
        column = jnp.where(r == 48 + source, 192 + struct_g, column)
        order_ref[SENT * g : SENT * g + SENT] = (column == wanted).astype(F32)


def prepare(where, count, owner, neighbors, descriptors, gradients):
    smem = pl.BlockSpec(memory_space=pltpu.SMEM)
    vmem = pl.BlockSpec(memory_space=pltpu.VMEM)
    return pl.pallas_call(
        prep_kernel,
        out_shape=(
            jax.ShapeDtypeStruct((320, 1024), BF16),
            jax.ShapeDtypeStruct((768, 1024), BF16),
            jax.ShapeDtypeStruct((8, 64), F32),
            jax.ShapeDtypeStruct((8 * SENT, 256), F32),
        ),
        in_specs=[smem, smem, smem, vmem, vmem, vmem],
        out_specs=(vmem, vmem, vmem, vmem),
        compiler_params=params(),
        cost_estimate=pl.CostEstimate(
            flops=2 * 64 * 128 * 1024 * 17, bytes_accessed=6 << 20, transcendentals=0
        ),
    )(where, count, owner, neighbors, descriptors, gradients)


def compact_rows(env, atoms, grads, mean):
    near = dot(atoms, env, NT)
    slope = dot(grads, env, NT)
    inner = near[:64]
    parts = []
    for k in range(3):
        total = near[64:128] * slope[k * 256 : k * 256 + 64]
        for j in range(1, 4):
            total = total + near[64 + j * 64 : 128 + j * 64] * slope[
                k * 256 + j * 64 : k * 256 + j * 64 + 64
            ]
        parts.append((-2.0 * total).astype(BF16))
    energy = dot(mean, inner * inner, NN, HIGHEST)
    pad = jnp.zeros((56, env.shape[0]), F32)
    parts.append(jnp.concatenate([energy, pad], axis=0).astype(BF16))
    return jnp.concatenate(parts, axis=0)


def put_env(env, where, own, other, block, at):
    core = where[3]
    env[pl.ds(pl.multiple_of(at + core * 16, 16), 16)] = own[block]
    env[pl.ds(pl.multiple_of(at + (1 - core) * 16, 16), 16)] = other[block]


def panel_kernel(
    where, own, other, atoms_ref, grads_ref, mean_ref, order_ref, near_ref, far_ref, gram_ref, env
):
    x, z, y, core = where[0], where[1], where[2], where[3]
    for i in range(4):
        for j in range(4):
            place = ((x - i) & 3) * 4 + ((z - j) & 3)
            put_env(env, where, own, other, (i, j), place * 32)
    rows = compact_rows(env[...], atoms_ref[...], grads_ref[...], mean_ref[...])
    full = dot(order_ref[...].astype(BF16), rows, NN)
    first = core == 0
    for i in range(4):
        at = 2 * SENT * i
        low, high = full[at : at + SENT], full[at + SENT : at + 2 * SENT]
        s = (i - y) & 3
        near_ref[s] = jnp.where(first, low, high).astype(BF16)
        far_ref[s] = jnp.where(first, high, low).astype(BF16)
    gram = dot(rows, rows, TN)
    for n, (i, j) in enumerate(UPPER):
        gram_ref[128 * n : 128 * n + 128] = gram[
            128 * i : 128 * i + 128, 128 * j : 128 * j + 128
        ]


def trail_kernel(
    where, own_ref, other_ref, atoms_ref, grads_ref, mean_ref, order_ref, out_ref
):
    first = where[3] == 0
    own, other = own_ref[...], other_ref[...]
    low, high = jnp.where(first, own, other), jnp.where(first, other, own)
    env = jnp.concatenate([low, high], axis=1).reshape(-1, 1024)
    rows = compact_rows(env, atoms_ref[...], grads_ref[...], mean_ref[...])
    full = dot(order_ref[...].astype(BF16), rows, NN)
    for c in range(out_ref.shape[1]):
        part = full[:, c * 128 : c * 128 + 128].reshape(8, SENT, 128)
        out_ref[:, c] = part.astype(BF16)


def assemble_kernel(where, near, far, got1, got2, got3, out):
    y, core = where[2], where[3]
    blocks = [(near, 0, 0, core), (far, 0, 0, 1 - core)]
    for s, got in ((1, got1), (2, got2), (3, got3)):
        blocks += [(got, 0, s, core), (got, 1, s, 1 - core)]
    energy = jnp.zeros((8, out.shape[1]), F32)
    for ref, i, s, c in blocks:
        at = (2 * ((y - s) & 3) + c) * 48
        out[pl.ds(pl.multiple_of(at, 16), 48)] = ref[i, :48]
        energy = energy + ref[i, 48:].astype(F32)
    out[384:] = jnp.concatenate([energy, jnp.zeros_like(energy)], axis=0).astype(BF16)


def trail_chunk(ref, i):
    rows = [ref[r, i, :48] for r in range(8)]
    energy = ref[0, i, 48:].astype(F32)
    for r in range(1, 8):
        energy = energy + ref[r, i, 48:].astype(F32)
    last = jnp.concatenate([energy, jnp.zeros_like(energy)], axis=0).astype(BF16)
    return jnp.concatenate(rows + [last], axis=0)


def params(mib=40):
    return pltpu.CompilerParams(vmem_limit_bytes=mib << 20)


def in_smem():
    return pl.BlockSpec(memory_space=pltpu.SMEM)


def in_vmem():
    return pl.BlockSpec(memory_space=pltpu.VMEM)


def panel_rows(where, own, other, atoms, grads, mean, order):
    return pl.pallas_call(
        panel_kernel,
        out_shape=(
            jax.ShapeDtypeStruct((4, SENT, 512), BF16),
            jax.ShapeDtypeStruct((4, SENT, 512), BF16),
            jax.ShapeDtypeStruct((1280, 128), F32),
        ),
        in_specs=[in_smem()] + [in_vmem()] * 6,
        out_specs=(in_vmem(),) * 3,
        scratch_shapes=[pltpu.VMEM((512, 1024), BF16)],
        compiler_params=params(),
        cost_estimate=pl.CostEstimate(
            flops=2 * 512 * 1024 * 1088, bytes_accessed=5 << 20, transcendentals=0
        ),
    )(where, own, other, atoms, grads, mean, order)


def assemble(where, near, far, got):
    return pl.pallas_call(
        assemble_kernel,
        out_shape=jax.ShapeDtypeStruct((HELD, 512), BF16),
        in_specs=[in_smem()] + [in_vmem()] * 5,
        out_specs=in_vmem(),
        compiler_params=params(),
        cost_estimate=pl.CostEstimate(flops=0, bytes_accessed=1 << 20, transcendentals=0),
    )(where, near, far, *got)


def trail_rows(where, own, other, atoms, grads, mean, order):
    blocks = own.shape[0]
    step = 4
    half = pl.BlockSpec((step, 64, 1024), lambda i, w: (i, 0, 0))
    whole = lambda shape: pl.BlockSpec(shape, lambda i, w: (0, 0))
    return pl.pallas_call(
        trail_kernel,
        out_shape=jax.ShapeDtypeStruct((8, blocks, SENT, 128), BF16),
        grid_spec=pltpu.PrefetchScalarGridSpec(
            num_scalar_prefetch=1,
            grid=(blocks // step,),
            in_specs=[
                half,
                half,
                whole(atoms.shape),
                whole(grads.shape),
                whole(mean.shape),
                whole(order.shape),
            ],
            out_specs=pl.BlockSpec((8, step, SENT, 128), lambda i, w: (0, i, 0, 0)),
        ),
        compiler_params=params(),
        cost_estimate=pl.CostEstimate(
            flops=2 * 2048 * 1024 * 1088, bytes_accessed=9 << 20, transcendentals=0
        ),
    )(where, own, other, atoms, grads, mean, order)


def eliminate(a):
    lanes = lax.broadcasted_iota(jnp.int32, (8, 128), 1)
    subs = lax.broadcasted_iota(jnp.int32, (8, 128), 0)
    left = [a[8 * g : 8 * g + 8] for g in range(16)]
    right = [(lanes == subs + 8 * g).astype(F32) for g in range(16)]
    done = []
    for p in range(16):
        count = 16 - p
        cols = [
            [
                jnp.broadcast_to(left[g][:, 8 * p + q : 8 * p + q + 1], (8, 128))
                for g in range(count)
            ]
            for q in range(8)
        ]
        pivots = jnp.ones((8, 128), F32)
        for q in range(8):
            pivot = cols[q][0][q : q + 1]
            inverse = 1.0 / pivot
            pivots = jnp.where(subs == q, pivot, pivots)
            ratio = [c * inverse for c in cols[q]]
            ratio[0] = jnp.where(subs > q, ratio[0], 0.0)
            for t in range(q + 1, 8):
                here = cols[t][0][q : q + 1]
                for g in range(count):
                    cols[t][g] = cols[t][g] - ratio[g] * here
            row_left = left[0][q : q + 1]
            row_right = right[0][q : q + 1]
            for g in range(count):
                left[g] = left[g] - ratio[g] * row_left
                right[g] = right[g] - ratio[g] * row_right
        done.append(right[0] * lax.rsqrt(pivots))
        left, right = left[1:], right[1:]
    return jnp.concatenate(done, axis=0)


def factor_kernel(rows_total, gram_ref, factor_ref, inverse_ref, work):
    n = factor_ref.shape[0]
    r = lax.broadcasted_iota(jnp.int32, (n, n), 0)
    c = lax.broadcasted_iota(jnp.int32, (n, n), 1)
    same = r[:128, :128] == c[:128, :128]
    work[:, :n] = jnp.zeros((n, n), F32)
    for m, (i, j) in enumerate(UPPER):
        block = gram_ref[128 * m : 128 * m + 128] / rows_total
        if i == j:
            block = block + jnp.where(same, ridge_value, 0.0)
        work[128 * i : 128 * i + 128, 128 * j : 128 * j + 128] = block
    work[:, n:] = jnp.where(r == c, 1.0, 0.0)

    def step(b, carry):
        at = pl.multiple_of(b * 128, 128)
        low = eliminate(work[pl.ds(at, 128), pl.ds(at, 128)])
        for k in range(n // 128):

            @pl.when(b == k)
            def _(k=k):
                here, after = slice(128 * k, 128 * k + 128), slice(128 * k + 128, n)
                left, right = slice(128 * k, n), slice(n, n + 128 * k + 128)
                row = dot(low, work[here, left], NN, HIGHEST)
                solved = dot(low, work[here, right], NN, HIGHEST)
                work[here, left] = row
                work[here, right] = solved
                if k < n // 128 - 1:
                    later = row[:, 128:]
                    work[after, after] -= dot(later, later, TN, HIGHEST)
                    work[after, right] -= dot(later, solved, TN, HIGHEST)

        return carry

    lax.fori_loop(0, n // 128, step, 0)
    factor_ref[...] = jnp.where(c >= r, work[:, :n], 0.0)
    inverse_ref[...] = jnp.where(c <= r, work[:, n:], 0.0)


def factor_panel(gram, rows_total):
    n = 512
    return pl.pallas_call(
        functools.partial(factor_kernel, float(rows_total)),
        out_shape=(jax.ShapeDtypeStruct((n, n), F32), jax.ShapeDtypeStruct((n, n), F32)),
        scratch_shapes=[pltpu.VMEM((n, 2 * n), F32)],
        compiler_params=params(),
        cost_estimate=pl.CostEstimate(
            flops=20 * n * n * n, bytes_accessed=4 << 20, transcendentals=n
        ),
    )(gram)


def cross_kernel(panel_ref, trail_ref, out_ref):
    @pl.when(pl.program_id(0) == 0)
    def _():
        out_ref[...] = jnp.zeros_like(out_ref)

    n = panel_ref.shape[2]
    trail = jnp.concatenate(
        [trail_chunk(trail_ref, i) for i in range(panel_ref.shape[0])], axis=0
    )
    out_ref[...] += dot(trail, panel_ref[...].reshape(-1, n), TN)


def cross_part(segment, trail):
    n = segment.shape[2]
    return pl.pallas_call(
        cross_kernel,
        out_shape=jax.ShapeDtypeStruct((128, n), F32),
        grid=(segment.shape[0] // 4,),
        in_specs=[
            pl.BlockSpec((4, HELD, n), lambda i: (i, 0, 0)),
            pl.BlockSpec((8, 4, SENT, 128), lambda i: (0, i, 0, 0)),
        ],
        out_specs=pl.BlockSpec((128, n), lambda i: (0, 0)),
        compiler_params=params(),
        cost_estimate=pl.CostEstimate(
            flops=2 * 128 * n * 8192, bytes_accessed=11 << 20, transcendentals=0
        ),
    )(segment, trail)


def spread_pair(rest, k, lane):
    full = jnp.zeros((128, 128), F32)
    for m in (0, 1):
        struct, at = 2 * k + m, 64 * m
        start = 48 * struct
        turn = (at + 1 - start) % 128
        part = start // 128
        split = at + 1 + min(48, 128 * (part + 1) - start)
        force = pltpu.roll(rest[:, 128 * part : 128 * part + 128], turn, 1)
        full = jnp.where((lane > at) & (lane < split), force, full)
        if split < at + 49:
            force = pltpu.roll(rest[:, 128 * part + 128 : 128 * part + 256], turn, 1)
            full = jnp.where((lane >= split) & (lane < at + 49), force, full)
        energy = jnp.broadcast_to(rest[:, 384 + struct : 385 + struct], (128, 128))
        full = jnp.where(lane == at, energy, full)
    return full


def residual_kernel(
    rows_total, cross_ref, inverse_ref, panel_ref, trail_ref, coupling_ref, out_ref, weights
):
    @pl.when(pl.program_id(0) == 0)
    def _():
        coupling = dot(cross_ref[...] / rows_total, inverse_ref[...], NT, HIGHEST)
        coupling_ref[...] = coupling
        solved = dot(coupling, inverse_ref[...], NN, HIGHEST)
        high = solved.astype(BF16)
        weights[:128] = high
        weights[128:] = (solved - high.astype(F32)).astype(BF16)

    r = lax.broadcasted_iota(jnp.int32, (128, 128), 0)
    c = lax.broadcasted_iota(jnp.int32, (128, 128), 1)
    same = (r == c).astype(BF16)
    for i in range(panel_ref.shape[0]):
        both = dot(weights[...], panel_ref[i], NT)
        own = dot(same, trail_chunk(trail_ref, i), NT)
        rest = own - both[:128] - both[128:]
        for k in range(4):
            at = i * 512 + k * 128
            out_ref[:, at : at + 128] = spread_pair(rest, k, c)


def residual(cross, inverse, segment, trail, rows_total):
    n = inverse.shape[0]
    chunks = segment.shape[0]
    whole = lambda shape: pl.BlockSpec(shape, lambda i: (0, 0))
    return pl.pallas_call(
        functools.partial(residual_kernel, float(rows_total)),
        out_shape=(
            jax.ShapeDtypeStruct((128, n), F32),
            jax.ShapeDtypeStruct((128, 512 * chunks), F32),
        ),
        grid=(chunks // 4,),
        in_specs=[
            whole((128, n)),
            whole((n, n)),
            pl.BlockSpec((4, HELD, n), lambda i: (i, 0, 0)),
            pl.BlockSpec((8, 4, SENT, 128), lambda i: (0, i, 0, 0)),
        ],
        out_specs=(whole((128, n)), pl.BlockSpec((128, 2048), lambda i: (0, i))),
        scratch_shapes=[pltpu.VMEM((256, n), BF16)],
        compiler_params=params(),
        cost_estimate=pl.CostEstimate(
            flops=4 * 128 * n * 8192, bytes_accessed=16 << 20, transcendentals=0
        ),
    )(cross, inverse, segment, trail)


def sum_row(v, core):
    v = sum4(swap_add(v, core), "row", y_pair)
    return jnp.concatenate(swap_gather(v, core), axis=0)


def per_device(
    descriptors, gradients, sparse_panel, sparse_trail, atom_counts, owner_rows, neighbor_ids
):
    row = lax.axis_index("row")
    col = lax.axis_index("col")
    core, y = row % 2, row // 2
    x, z = col // 4, col % 4
    rows_total = 65536

    where = jnp.stack([x, z, y, core]).astype(jnp.int32)

    trail_own = lax.dynamic_slice_in_dim(sparse_trail, core * 64, 64, 0)
    trail_own = lax.all_gather(trail_own, "col", axis=0, tiled=False)
    piece = lax.dynamic_slice_in_dim(sparse_panel, core * 16, 16, 0)
    piece = jnp.stack(shifted(piece, "col", z_shift))
    own = jnp.stack(shifted(piece, "col", x_shift))
    other = lax.ppermute(own, "row", CORE_SWAP)

    atoms, grads, mean, order = prepare(
        where,
        atom_counts,
        owner_rows,
        neighbor_ids.reshape(128, 4).T,
        descriptors,
        gradients.reshape(12, 128, 1024),
    )

    near, far, gram = panel_rows(where, own, other, atoms, grads, mean, order)
    far = lax.ppermute(far, "row", CORE_SWAP)
    gram = swap_add(gram, core)
    far, gram = lax.optimization_barrier((far, gram))
    got = [
        lax.ppermute(jnp.stack([near[s], far[s]]), "row", y_shift(s)) for s in (1, 2, 3)
    ]
    gram = scatter4(gram, "row", y_shift, y)
    got, gram = lax.optimization_barrier((got, gram))
    panel = assemble(where, near, far, got)
    segment = lax.all_gather(panel, "col", axis=0, tiled=False)
    trail_other = lax.ppermute(trail_own, "row", CORE_SWAP)
    gram = sum4(gram, "col", z_pair)
    trail_other, gram = lax.optimization_barrier((trail_other, gram))
    gram = sum4(gram, "col", x_pair)
    trail = trail_rows(where, trail_own, trail_other, atoms, grads, mean, order)
    trail, gram = lax.optimization_barrier((trail, gram))
    gram = gather4(gram, "row", y_shift, y)
    trail, gram = lax.optimization_barrier((trail, gram))
    gram = jnp.concatenate(swap_gather(gram, core), axis=0)
    trail = lax.all_to_all(
        trail.reshape(128, SENT, 128), ("row", "col"), 0, 0, tiled=True
    ).reshape(8, 16, SENT, 128)
    factor, inverse = factor_panel(gram, rows_total)

    segment, inverse = lax.optimization_barrier((segment, inverse))
    cross = sum_row(cross_part(segment, trail), core)
    coupling, result = residual(cross, inverse, segment, trail, rows_total)
    return factor, coupling, result


def solution(mesh):
    return jax.shard_map(
        per_device,
        mesh=mesh,
        in_specs=(
            P(("row", "col"), None),
            P(None, None, ("row", "col"), None),
            P("col", None),
            P("col", None),
            P(("row", "col"), None),
            P(("row", "col"), None),
            P(("row", "col"), None, None),
        ),
        out_specs=(P(), P("col", None), P("col", "row")),
        check_vma=False,
    )
```
